32 devices in a mesh: dp: 4 (over y, core), tensor: 8 (over z, x).
Axes of the slice: x: 2, y: 2, z: 4, core: 2. Of those that a mesh axis runs over, the one named last changes fastest.
Arguments:
- hidden_in: bfloat16 [3072, 2048], P(('dp', 'tensor')), may hold values from -6 to 6
- norm1_gain: bfloat16 [2048], replicated, may hold values from 0.099609375 to 1.8984375
- norm2_gain: bfloat16 [2048], replicated, may hold values from 0.099609375 to 1.8984375
- w_query: bfloat16 [2048, 2048], P(None, 'tensor'), may hold values from -0.125 to 0.125
- w_keyval: bfloat16 [2048, 256], replicated, may hold values from -0.125 to 0.125
- w_out: bfloat16 [2048, 2048], P('tensor'), may hold values from -0.5 to 0.5
- w_fc: bfloat16 [2048, 8192], P(None, 'tensor'), may hold values from -0.125 to 0.125
- w_proj: bfloat16 [8192, 2048], P('tensor'), may hold values from -0.0625 to 0.0625
- prefix_kv: bfloat16 [4, 4096, 256], P('dp', 'tensor'), may hold values from -320 to 320
- owner_ids: int32 [4], replicated, may hold values from 0 to 3, each once
- segment_ids: int32 [4, 768], P('dp'), may hold values from 0 to 11, never falling along the last dimension, each value on 1 to 192 neighbouring positions
Outputs:
- layer_out: bfloat16 [3072, 2048], P(('dp', 'tensor'))
- attended: bfloat16 [3072, 2048], P(('dp', 'tensor'))
The draws below stay inside these ranges and needn't reach their ends.
Inputs may be any that keep to these rules, and one draw needn't show every extreme that they name: `owner_ids`: each stored prefix is extended by exactly one group. `segment_ids`: within a group the request ids never fall; every one of the 12 requests has 1 to 192 tokens, and at least one has exactly 192.
All inputs are finite; a program needn't handle non-finite values.
Results may differ from the reference program's by a relative error of at most 0.015.
Values may be sent and summed in bfloat16 or wider, within the bound.
A program may use at most 128 MiB of HBM per device.

```python
import math
import jax
import jax.numpy as jnp
import numpy as np
from jax import lax

D = 2048
H = 16
DH = 128
FF = 8192
PREFIX = 4096
REQUESTS = 12
S_ROW = 768
GROUPS = 4
TOKENS = 3072
N_TENSOR = 8


def draw_prefix_kv(key, part):
    first_key = jax.random.fold_in(key, 0)
    shape = (GROUPS, PREFIX, 2 * DH)
    result = jnp.clip(jax.random.normal(first_key, shape, jnp.float32), -4.0, 4.0)
    return result.astype(jnp.bfloat16)


def shard_levels(stream_key, extent, cuts, smallest, largest):
    level, own = 1.0, jax.random.fold_in(stream_key, 6)
    for position, parts in cuts:
        heights = jnp.exp(jax.random.uniform(jax.random.fold_in(own, position), (parts,), jnp.float32, smallest / len(cuts), largest / len(cuts)))
        level = level * jnp.repeat(heights, extent[position] // parts).reshape([-1 if axis == position else 1 for axis in range(len(extent))])
    return level


def length_profile(count, total, most, slope):
    loads = [(1 << 20) // math.isqrt(rank ** slope) + 1 for rank in range(2, count + 1)]
    spare, holding = total - most - (count - 1), [1] * (count - 1)
    while spare > 0:
        movable = [i for i in range(count - 1) if holding[i] < most]
        whole, budget = sum([loads[i] for i in movable]), spare
        for i in movable:
            extra = min(most - holding[i], max(1, budget * loads[i] // whole), spare)
            holding[i] = holding[i] + extra
            spare = spare - extra
    return np.array([most] + holding)


def ragged(own_key, number_of, total, bound, slope):
    if number_of == 2:
        one = jax.random.randint(own_key, (), max(1, total - bound), min(bound, total - 1) + 1)
        return jnp.stack([one, total - one])
    sizes = jnp.asarray(length_profile(number_of, total, bound, slope), jnp.int32)
    pairs = (number_of - 1) // 2
    donor, sink = sizes[1:1 + 2 * pairs:2], sizes[2:2 + 2 * pairs:2]
    margin = jnp.minimum(donor - 1, bound - sink)
    moved = jax.random.randint(jax.random.fold_in(own_key, 1), (pairs,), 0, 1 << 20) % (margin + 1)
    sizes = sizes.at[1:1 + 2 * pairs:2].set(donor - moved).at[2:2 + 2 * pairs:2].set(sink + moved)
    return sizes[jax.random.permutation(jax.random.fold_in(own_key, 2), number_of)]


def noise(rng, shape, scale, limit, shards=(), kind=jnp.bfloat16):
    loudness = shard_levels(rng, shape, shards, -0.22, 0.18) if shards else 1.0
    drawn = jax.random.normal(rng, shape, jnp.float32) * scale * loudness
    return jnp.minimum(jnp.maximum(drawn, -limit), limit).astype(kind)


def setup_inputs(seed: int = 0) -> dict:
    key_of = jax.random.split(jax.random.key(seed), 12)
    hidden_in = noise(key_of[0], (TOKENS, D), 1.0, 6.0, ((0, 32),))
    norm1_gain = jnp.clip(1.0 + 0.18 * jax.random.normal(key_of[1], (D,), jnp.float32), 0.099609375, 1.8984375).astype(jnp.bfloat16)
    norm2_gain = jnp.clip(1.0 + 0.18 * jax.random.normal(key_of[2], (D,), jnp.float32), 0.099609375, 1.8984375).astype(jnp.bfloat16)
    w_query = noise(key_of[3], (D, H * DH), D ** -0.5, 0.125, ((1, 8),))
    w_keyval = noise(key_of[4], (D, 2 * DH), D ** -0.5, 0.125)
    w_out = noise(key_of[5], (H * DH, D), DH ** -0.5, 0.5, ((0, 8),))
    w_fc = noise(key_of[6], (D, FF), D ** -0.5, 0.125, ((1, 8),))
    w_proj = noise(key_of[7], (FF, D), FF ** -0.5, 0.0625, ((0, 8),))
    prefix_kv = draw_prefix_kv(jax.random.fold_in(key_of[11], 71), 0)
    owner_ids = jax.random.permutation(key_of[9], GROUPS).astype(jnp.int32)
    segment_ids = jax.vmap(lambda own: jnp.searchsorted(jnp.cumsum(ragged(own, REQUESTS, S_ROW, S_ROW // 4, 2)), jnp.arange(S_ROW), side="right"))(jax.random.split(key_of[10], GROUPS)).reshape((GROUPS, S_ROW)).astype(jnp.int32)
    return dict(hidden_in=hidden_in, norm1_gain=norm1_gain, norm2_gain=norm2_gain, w_query=w_query, w_keyval=w_keyval, w_out=w_out, w_fc=w_fc, w_proj=w_proj, prefix_kv=prefix_kv, owner_ids=owner_ids, segment_ids=segment_ids)


HIGHEST = lax.Precision.HIGHEST

def layer_norm(values, scales):
    widened = values.astype(jnp.float32)
    centre = lax.optimization_barrier(jnp.mean(widened, axis=-1, keepdims=True))
    centred = widened - centre
    variance = lax.optimization_barrier(jnp.mean(centred * centred, axis=-1, keepdims=True))
    return (centred * lax.rsqrt(variance + 1e-05) * scales.astype(jnp.float32)).astype(jnp.bfloat16)

def reference(hidden_in, norm1_gain, norm2_gain, w_query, w_keyval, w_out, w_fc, w_proj, prefix_kv, owner_ids, segment_ids):
    groups = owner_ids.shape[0]
    row_len = hidden_in.shape[0] // groups
    heads_dev = H // N_TENSOR
    q_scale = 1.0 / math.sqrt(DH)
    inputs = hidden_in.reshape(groups, row_len, D)
    cached_all = jnp.take(prefix_kv, owner_ids.astype(jnp.int32), axis=0)
    positions = jnp.arange(row_len, dtype=jnp.int32)

    def one_row(packed):
        row_rows, cache_rows, request_ids = packed
        normed = layer_norm(row_rows, norm1_gain)
        queries = (jnp.dot(normed, w_query, preferred_element_type=jnp.float32) * q_scale).astype(jnp.bfloat16)
        suffix_kv = jnp.dot(normed, w_keyval, preferred_element_type=jnp.float32).astype(jnp.bfloat16)
        key_rows = jnp.concatenate([cache_rows[:, :DH], suffix_kv[:, :DH]], axis=0).astype(jnp.float32)
        value_rows = jnp.concatenate([cache_rows[:, DH:], suffix_kv[:, DH:]], axis=0)
        suffix_ok = (positions[None, :] <= positions[:, None]) & (request_ids[None, :] == request_ids[:, None])
        allowed = jnp.concatenate([jnp.ones((row_len, PREFIX), dtype=bool), suffix_ok], axis=1)
        head_queries = queries.astype(jnp.float32).reshape(row_len, H, DH).transpose(1, 0, 2)

        def one_head(head_q):
            scores = jnp.dot(head_q, key_rows.T, precision=HIGHEST)
            scores = jnp.where(allowed, scores, -jnp.inf)
            row_top = lax.optimization_barrier(jnp.max(scores, axis=-1, keepdims=True))
            probs = jnp.exp(scores - row_top)
            totals = lax.optimization_barrier(jnp.sum(probs, axis=-1, keepdims=True))
            probs_b = probs.astype(jnp.bfloat16)
            return (jnp.dot(probs_b, value_rows, preferred_element_type=jnp.float32) / totals).astype(jnp.bfloat16)
        attn_heads = lax.map(one_head, head_queries)
        grouped = attn_heads.reshape(N_TENSOR, heads_dev, row_len, DH).transpose(0, 2, 1, 3).reshape(N_TENSOR, row_len, heads_dev * DH)
        out_grouped = w_out.reshape(N_TENSOR, heads_dev * DH, D)
        partials = jnp.einsum('gtc,gcd->gtd', grouped.astype(jnp.float32), out_grouped.astype(jnp.float32), precision=HIGHEST).astype(jnp.bfloat16)
        attended = lax.optimization_barrier(jnp.sum(partials.astype(jnp.float32), axis=0)).astype(jnp.bfloat16)
        middle = (row_rows.astype(jnp.float32) + attended.astype(jnp.float32)).astype(jnp.bfloat16)
        normed2 = layer_norm(middle, norm2_gain)
        hidden_act = jax.nn.gelu(jnp.dot(normed2, w_fc, preferred_element_type=jnp.float32), approximate=True).astype(jnp.bfloat16)
        act_grouped = hidden_act.reshape(row_len, N_TENSOR, FF // N_TENSOR).transpose(1, 0, 2)
        proj_grouped = w_proj.reshape(N_TENSOR, FF // N_TENSOR, D)
        mlp_parts = jnp.einsum('gtf,gfd->gtd', act_grouped.astype(jnp.float32), proj_grouped.astype(jnp.float32), precision=HIGHEST).astype(jnp.bfloat16)
        mlp_sum = lax.optimization_barrier(jnp.sum(mlp_parts.astype(jnp.float32), axis=0))
        layer_out = (middle.astype(jnp.float32) + mlp_sum).astype(jnp.bfloat16)
        return (layer_out, attended)
    outs_rows, attended_rows = lax.map(one_row, (inputs, cached_all, segment_ids))
    return (outs_rows.reshape(groups * row_len, D), attended_rows.reshape(groups * row_len, D))
```

```python
import functools
import math

import jax
import jax.numpy as jnp
from jax import lax
from jax.experimental import pallas as pl
from jax.experimental.pallas import tpu as pltpu
from jax.sharding import PartitionSpec as P

MESH = pl.DeviceIdType.MESH
ROWS = 16
PIECES = 4
HALVES = 2
TEAM = 4


def plane(n):
    lines = 4 if n % 4 == 0 else n
    return lines, n // lines


def norm_rows(widened, gains):
    centre = jnp.mean(widened, axis=-1, keepdims=True)
    centred = widened - centre
    variance = jnp.mean(centred * centred, axis=-1, keepdims=True)
    return (centred * lax.rsqrt(variance + 1e-05) * gains).astype(jnp.bfloat16)


def row_loop(start, rows, body):
    def step(i, carry):
        body(pl.ds(pl.multiple_of(start + i * ROWS, ROWS), ROWS))
        return carry

    lax.fori_loop(0, rows // ROWS, step, 0)


def span_of(i, size):
    return pl.ds(pl.multiple_of(i * size, size), size)


class Place:
    def __init__(self, n, ndp):
        self.n, self.ndp = n, ndp
        self.A, self.B = plane(n)
        self.me = lax.axis_index("tensor")
        self.a = self.me // self.B
        self.b = self.me % self.B
        self.dp = lax.axis_index("dp")
        self.pairs = ndp // 2
        self.q = self.dp % TEAM
        base = self.dp - self.q
        self.q_core = self.q + 1 - 2 * (self.q % 2)
        self.q_far = (self.q + 2) % TEAM
        self.q_diag = (self.q_core + 2) % TEAM
        self.core = {"dp": base + self.q_core}
        self.across_dp = {"dp": base + self.q_far}

    def across(self, o):
        return (self.b + o) % self.B

    def peer(self, a, b):
        return {"tensor": a * self.B + b}

    def side(self, o):
        return self.peer(self.a, self.across(o))

    def up(self):
        return self.peer(jnp.minimum(self.a + 1, self.A - 1), self.b)

    def down(self):
        return self.peer(jnp.maximum(self.a - 1, 0), self.b)

    def same_core(self, o):
        return ((self.dp // 2 + o) % self.pairs) * 2 + self.dp % 2

    def choose(self, k, key):
        found = 0
        for a in range(self.A):
            order = sorted(range(self.A), key=lambda d: key(a, d))
            for i, d in enumerate(order):
                found = found + jnp.where((self.a == a) & (k == i), d, 0)
        return found

    def near(self, k):
        return self.choose(k, lambda a, d: (abs(d - a), d))

    def far(self, k):
        return self.choose(k, lambda a, d: (-abs(d - a), d))


def greet_signal(pc):
    barrier = pltpu.get_barrier_semaphore()

    def signal(device):
        pl.semaphore_signal(barrier, inc=1, device_id=device, device_id_type=MESH)

    @pl.when(pc.a > 0)
    def _():
        signal(pc.peer(pc.a - 1, pc.b))

    @pl.when(pc.a < pc.A - 1)
    def _():
        signal(pc.peer(pc.a + 1, pc.b))

    for o in range(1, pc.B):
        signal(pc.side(o))
    for o in range(1, pc.pairs):
        signal({"dp": pc.same_core(o)})
    signal(pc.core)


def greet_wait(pc):
    ends = jnp.where((pc.a == 0) | (pc.a == pc.A - 1), 1, 2)
    pl.semaphore_wait(pltpu.get_barrier_semaphore(), pc.B - 1 + pc.pairs + ends)


def remote(src, dst, send, recv, device):
    return pltpu.make_async_remote_copy(
        src_ref=src, dst_ref=dst, send_sem=send, recv_sem=recv, device_id=device, device_id_type=MESH
    )


class Gather:
    def __init__(self, place, buf, recv, up, down, side):
        self.pc, self.buf, self.recv, self.up, self.down, self.side = place, buf, recv, up, down, side

    def copy_up(self, a0):
        blk = a0 * self.pc.B + self.pc.b
        return remote(self.buf.at[blk], self.buf.at[blk], self.up.at[a0], self.recv.at[blk], self.pc.up())

    def copy_down(self, a0):
        blk = a0 * self.pc.B + self.pc.b
        return remote(self.buf.at[blk], self.buf.at[blk], self.down.at[a0], self.recv.at[blk], self.pc.down())

    def copy_side(self, a0, o):
        blk = a0 * self.pc.B + self.pc.b
        return remote(self.buf.at[blk], self.buf.at[blk], self.side.at[a0, o - 1], self.recv.at[blk],
                      self.pc.side(o))

    def arrived(self, blk):
        remote(self.buf.at[blk], self.buf.at[blk], self.up.at[0], self.recv.at[blk],
               self.pc.side(1)).wait_recv()

    def start(self):
        pc = self.pc

        @pl.when(pc.a < pc.A - 1)
        def _():
            self.copy_up(pc.a).start()

        @pl.when(pc.a > 0)
        def _():
            self.copy_down(pc.a).start()

        for o in range(1, pc.B):
            self.copy_side(pc.a, o).start()

    def round(self, r):
        pc = self.pc

        @pl.when(pc.a - r >= 0)
        def _():
            a0 = pc.a - r
            self.arrived(a0 * pc.B + pc.b)

            @pl.when(pc.a < pc.A - 1)
            def _():
                self.copy_up(a0).start()

            for o in range(1, pc.B):
                self.copy_side(a0, o).start()

        @pl.when(pc.a + r < pc.A)
        def _():
            a0 = pc.a + r
            self.arrived(a0 * pc.B + pc.b)

            @pl.when(pc.a > 0)
            def _():
                self.copy_down(a0).start()

            for o in range(1, pc.B):
                self.copy_side(a0, o).start()

    def pair_arrived(self, a0):
        for o in range(1, self.pc.B):
            self.arrived(a0 * self.pc.B + self.pc.across(o))

    def finish(self):
        pc = self.pc
        for a0 in range(pc.A):
            for o in range(1, pc.B):
                self.copy_side(a0, o).wait_send()

            @pl.when((pc.a >= a0) & (pc.a < pc.A - 1))
            def _():
                self.copy_up(a0).wait_send()

            @pl.when((pc.a <= a0) & (pc.a > 0))
            def _():
                self.copy_down(a0).wait_send()


DMA = pltpu.SemaphoreType.DMA


def gather_sems(n):
    A, B = plane(n)
    return [DMA((n,)), DMA((A,)), DMA((A,)), DMA((A, max(B - 1, 1)))]


class Team:
    def __init__(self, place, part, recv, far_send, core_send):
        self.pc, self.part, self.recv, self.far_send, self.core_send = place, part, recv, far_send, core_send

    def far_copy(self, s):
        pc = self.pc
        ref = self.part(s, pc.q)
        return remote(ref, ref, self.far_send.at[s], self.recv.at[s, pc.q], pc.across_dp)

    def core_copy(self, s, which):
        pc = self.pc
        q = pc.q_far if which else pc.q
        ref = self.part(s, q)
        return remote(ref, ref, self.core_send.at[s, which], self.recv.at[s, q], pc.core)

    def wait(self, s, q):
        ref = self.part(s, q)
        remote(ref, ref, self.far_send.at[s], self.recv.at[s, q], self.pc.core).wait_recv()

    def landed(self, s):
        self.wait(s, self.pc.q)
        self.far_copy(s).start()
        self.core_copy(s, 0).start()

    def spread(self, s):
        self.wait(s, self.pc.q_far)
        self.core_copy(s, 1).start()

    def here(self, s):
        self.wait(s, self.pc.q_core)
        self.wait(s, self.pc.q_diag)

    def finish(self, s):
        self.far_copy(s).wait_send()
        self.core_copy(s, 0).wait_send()
        self.core_copy(s, 1).wait_send()


def team_sems(slots):
    return [DMA((slots, TEAM)), DMA((slots,)), DMA((slots, 2))]


class LineWeights:
    def __init__(self, place, hbm, buf, recv, far_send, core_send, up, down):
        self.pc, self.hbm, self.up, self.down, self.recv = place, hbm, up, down, recv
        quarter = buf.shape[1] // TEAM
        self.part = lambda s, q: buf.at[s, span_of(q, quarter), :]
        self.own = lambda: hbm.at[span_of(place.q, quarter), :]
        self.team = Team(place, self.part, recv, far_send, core_send)

    def copy_up(self, a0, src=None):
        pc = self.pc
        ref = self.part(a0, pc.q)
        return remote(ref if src is None else src, ref, self.up.at[a0], self.recv.at[a0, pc.q], pc.up())

    def copy_down(self, a0, src=None):
        pc = self.pc
        ref = self.part(a0, pc.q)
        return remote(ref if src is None else src, ref, self.down.at[a0], self.recv.at[a0, pc.q], pc.down())

    def start(self):
        pc = self.pc

        @pl.when(pc.a < pc.A - 1)
        def _():
            self.copy_up(pc.a, self.own()).start()

        @pl.when(pc.a > 0)
        def _():
            self.copy_down(pc.a, self.own()).start()

    def hop(self, r):
        pc = self.pc

        @pl.when(pc.a - r >= 0)
        def _():
            self.team.landed(pc.a - r)

            @pl.when(pc.a < pc.A - 1)
            def _():
                self.copy_up(pc.a - r).start()

        @pl.when(pc.a + r < pc.A)
        def _():
            self.team.landed(pc.a + r)

            @pl.when(pc.a > 0)
            def _():
                self.copy_down(pc.a + r).start()

    def spread(self, r):
        pc = self.pc

        @pl.when(pc.a - r >= 0)
        def _():
            self.team.spread(pc.a - r)

        @pl.when(pc.a + r < pc.A)
        def _():
            self.team.spread(pc.a + r)

    def here(self, a0):
        self.team.here(a0)

    def finish(self):
        pc = self.pc
        for a0 in range(pc.A):

            @pl.when((pc.a >= a0) & (pc.a < pc.A - 1))
            def _():
                self.copy_up(a0).wait_send()

            @pl.when((pc.a <= a0) & (pc.a > 0))
            def _():
                self.copy_down(a0).wait_send()

            @pl.when(pc.a != a0)
            def _():
                self.team.finish(a0)


def line_weight_sems(n):
    A, _ = plane(n)
    return team_sems(A) + [DMA((A,)), DMA((A,))]


class SideWeights:
    def __init__(self, place, part, own, recv, far_send, core_send, side_send):
        self.pc, self.part3, self.own, self.recv, self.side_send = place, part, own, recv, side_send
        self.team = Team(place, lambda s, q: part(s // PIECES, s % PIECES, q), recv, far_send, core_send)

    def slots(self, i):
        return [self.pc.across(o) * PIECES + i for o in range(1, self.pc.B)]

    def copy(self, i, o):
        pc = self.pc
        return remote(self.own(i, pc.q), self.part3(pc.b, i, pc.q), self.side_send.at[o - 1, i],
                      self.recv.at[pc.b * PIECES + i, pc.q], pc.side(o))

    def start(self, i):
        for o in range(1, self.pc.B):
            self.copy(i, o).start()

    def hop(self, i):
        for s in self.slots(i):
            self.team.landed(s)

    def spread(self, i):
        for s in self.slots(i):
            self.team.spread(s)

    def here(self, i):
        for s in self.slots(i):
            self.team.here(s)

    def finish(self):
        for i in range(PIECES):
            for o in range(1, self.pc.B):
                self.copy(i, o).wait_send()
            for s in self.slots(i):
                self.team.finish(s)


def side_weight_sems(n):
    _, B = plane(n)
    return team_sems(B * PIECES) + [DMA((max(B - 1, 1), PIECES))]


class LineGather:
    def __init__(self, place, buf, recv, up, down):
        self.pc, self.buf, self.recv, self.up, self.down = place, buf, recv, up, down
        self.half = buf.shape[1] // HALVES

    def ref(self, a0, s):
        return self.buf.at[a0, pl.ds(s * self.half, self.half), :]

    def copy_up(self, a0, s):
        return remote(self.ref(a0, s), self.ref(a0, s), self.up.at[a0, s], self.recv.at[a0, s], self.pc.up())

    def copy_down(self, a0, s):
        return remote(self.ref(a0, s), self.ref(a0, s), self.down.at[a0, s], self.recv.at[a0, s], self.pc.down())

    def start(self, s):
        pc = self.pc

        @pl.when(pc.a < pc.A - 1)
        def _():
            self.copy_up(pc.a, s).start()

        @pl.when(pc.a > 0)
        def _():
            self.copy_down(pc.a, s).start()

    def hop(self, r):
        pc = self.pc
        for s in range(HALVES):

            @pl.when(pc.a - r >= 0)
            def _():
                self.copy_up(pc.a - r, s).wait_recv()

                @pl.when(pc.a < pc.A - 1)
                def _():
                    self.copy_up(pc.a - r, s).start()

            @pl.when(pc.a + r < pc.A)
            def _():
                self.copy_down(pc.a + r, s).wait_recv()

                @pl.when(pc.a > 0)
                def _():
                    self.copy_down(pc.a + r, s).start()

    def finish(self):
        pc = self.pc
        for a0 in range(pc.A):
            for s in range(HALVES):

                @pl.when((pc.a >= a0) & (pc.a < pc.A - 1))
                def _():
                    self.copy_up(a0, s).wait_send()

                @pl.when((pc.a <= a0) & (pc.a > 0))
                def _():
                    self.copy_down(a0, s).wait_send()


class LineReduce:
    def __init__(self, place, term, up_in, down_in, up_send, up_recv, down_send, down_recv):
        self.pc, self.term, self.up_in, self.down_in = place, term, up_in, down_in
        self.up_send, self.up_recv, self.down_send, self.down_recv = up_send, up_recv, down_send, down_recv
        self.rows = term.shape[1]
        self.wide = term.shape[2] // PIECES

    def copy_up(self, d, i):
        cols = span_of(i, self.wide)
        return remote(self.term.at[d, :, cols], self.up_in.at[d, :, cols], self.up_send.at[d, i],
                      self.up_recv.at[d, i], self.pc.up())

    def copy_down(self, d, i):
        cols = span_of(i, self.wide)
        return remote(self.term.at[d, :, cols], self.down_in.at[d, :, cols], self.down_send.at[d, i],
                      self.down_recv.at[d, i], self.pc.down())

    def add(self, d, i, arrived):
        cols = span_of(i, self.wide)

        def body(rows):
            total = self.term[d, rows, cols].astype(jnp.float32) + arrived[d, rows, cols].astype(jnp.float32)
            self.term[d, rows, cols] = total.astype(jnp.bfloat16)

        row_loop(0, self.rows, body)

    def pass_on(self, d, i):
        pc = self.pc

        @pl.when(d > pc.a)
        def _():
            @pl.when(pc.a > 0)
            def _():
                self.copy_up(d, i).wait_recv()
                self.add(d, i, self.up_in)

            self.copy_up(d, i).start()

        @pl.when(d < pc.a)
        def _():
            @pl.when(pc.a < pc.A - 1)
            def _():
                self.copy_down(d, i).wait_recv()
                self.add(d, i, self.down_in)

            self.copy_down(d, i).start()

    def result(self, i, use):
        pc = self.pc
        cols = span_of(i, self.wide)

        def go(terms):
            def body(rows):
                total = self.term[pc.a, rows, cols].astype(jnp.float32)
                for arrived in terms:
                    total = total + arrived[pc.a, rows, cols].astype(jnp.float32)
                use(rows, cols, total)

            row_loop(0, self.rows, body)

        @pl.when(pc.a == 0)
        def _():
            self.copy_down(pc.a, i).wait_recv()
            go([self.down_in])

        @pl.when(pc.a == pc.A - 1)
        def _():
            self.copy_up(pc.a, i).wait_recv()
            go([self.up_in])

        @pl.when((pc.a > 0) & (pc.a < pc.A - 1))
        def _():
            self.copy_up(pc.a, i).wait_recv()
            self.copy_down(pc.a, i).wait_recv()
            go([self.up_in, self.down_in])

    def finish(self):
        pc = self.pc
        for d in range(pc.A):
            for i in range(PIECES):

                @pl.when(pc.a < d)
                def _():
                    self.copy_up(d, i).wait_send()

                @pl.when(pc.a > d)
                def _():
                    self.copy_down(d, i).wait_send()


def layer_kernel(n, ndp, heads, q_scale, hidden, gain1, gain2, prefix, owners, seg, w_keyval_hbm, w_query_hbm,
                 w_out_hbm, w_fc_hbm, w_proj_hbm, attended, layer_out, *scratch):
    pc = Place(n, ndp)
    A, B = pc.A, pc.B
    greet_signal(pc)
    scratch = list(scratch)

    def take(count):
        got = scratch[:count]
        del scratch[:count]
        return got

    wkv, wq, wout, wfc, wproj = take(5)
    normed, normed2, act, term, up_in, down_in = take(6)
    cached, from_dp, queries, top_ref, total_ref, weighted_ref, attn, out_sum, out_send, out_in, middle = take(11)
    (load,) = take(1)
    tok_recv, tok_send, out_sem, out_recv = take(4)
    dp_recv, dp_send, dp_core = take(3)
    rows, width = hidden.shape
    slab = B * rows
    span = prefix.shape[1]
    row_len = n * rows
    head = wkv.shape[1] // 2
    units = w_fc_hbm.shape[1]
    half = rows // HALVES
    dp = pc.dp

    keys = Gather(pc, cached, *take(4))
    wq_line = LineWeights(pc, w_query_hbm, wq, *take(5))
    wout_line = LineWeights(pc, w_out_hbm, wout, *take(5))
    fc_rows, fc_cols = width // TEAM, units // PIECES
    pr_rows, pr_cols = units // TEAM, width // PIECES
    fc_side = SideWeights(
        pc,
        lambda s, i, q: wfc.at[s, span_of(q, fc_rows), span_of(i, fc_cols)],
        lambda i, q: w_fc_hbm.at[span_of(q, fc_rows), span_of(i, fc_cols)],
        *take(4))
    pr_side = SideWeights(
        pc,
        lambda s, i, q: wproj.at[pl.ds(pl.multiple_of(s * units + q * pr_rows, pr_rows), pr_rows), span_of(i, pr_cols)],
        lambda i, q: w_proj_hbm.at[span_of(q, pr_rows), span_of(i, pr_cols)],
        *take(4))
    gather = LineGather(pc, normed2, *take(3))
    reduce = LineReduce(pc, term, up_in, down_in, *take(4))

    def mlp(kind, j):
        if 0 <= j < 2 * PIECES:
            getattr(fc_side if j < PIECES else pr_side, kind)(j % PIECES)

    def tick(j):
        mlp("hop", j)
        mlp("start", j + 2)
        mlp("spread", j - 1)

    loads = [
        pltpu.make_async_copy(w_keyval_hbm, wkv, load.at[0]),
        pltpu.make_async_copy(w_query_hbm, wq.at[pc.a], load.at[1]),
        pltpu.make_async_copy(w_out_hbm, wout.at[pc.a], load.at[2]),
        pltpu.make_async_copy(w_fc_hbm, wfc.at[pc.b], load.at[3]),
        pltpu.make_async_copy(w_proj_hbm, wproj.at[span_of(pc.b, units), :], load.at[4]),
    ]
    for copy in loads:
        copy.start()

    gains = gain1[...].astype(jnp.float32).reshape(1, width)

    def first(part):
        normed[pc.b, part, :] = norm_rows(hidden[part, :].astype(jnp.float32), gains)

    row_loop(0, rows, first)
    greet_wait(pc)

    def dp_copy(o):
        return remote(prefix.at[0], from_dp.at[dp], dp_send.at[o - 1], dp_recv.at[dp], {"dp": pc.same_core(o)})

    def dp_to_core(o):
        src = pc.same_core(o)
        ref = prefix.at[0] if o == 0 else from_dp.at[src]
        return remote(ref, from_dp.at[src], dp_core.at[o], dp_recv.at[src], pc.core)

    def dp_arrived(src):
        remote(prefix.at[0], from_dp.at[src], dp_send.at[0], dp_recv.at[src], pc.core).wait_recv()

    for o in range(1, pc.pairs):
        dp_copy(o).start()
    dp_to_core(0).start()
    wq_line.start()

    def tok_copy(o):
        return remote(normed.at[pc.b], normed.at[pc.b], tok_send.at[o - 1], tok_recv.at[pc.b], pc.side(o))

    for o in range(1, B):
        tok_copy(o).start()
    from_dp[dp] = prefix[0]
    loads[0].wait()
    cached[pc.me, span:, :] = jnp.dot(
        normed[pc.b], wkv[...], preferred_element_type=jnp.float32
    ).astype(jnp.bfloat16)
    for o in range(1, pc.pairs):
        dp_arrived(pc.same_core(o))
        dp_to_core(o).start()
    for o in range(pc.pairs):
        src = pc.same_core(o)
        dp_arrived(src + 1 - 2 * (src % 2))
    cached[pc.me, :span, :] = from_dp[owners[dp]]
    keys.start()
    for o in range(1, B):
        s = pc.across(o)
        remote(normed.at[s], normed.at[s], tok_send.at[0], tok_recv.at[s], pc.side(1)).wait_recv()
    mlp("start", 0)
    mlp("start", 1)

    def project(a0):
        left = normed[...].reshape(slab, width)
        out = (jnp.dot(left, wq[a0], preferred_element_type=jnp.float32) * q_scale).astype(jnp.bfloat16)
        for h in range(heads):
            queries[a0, h * slab : (h + 1) * slab, :] = out[:, h * head : (h + 1) * head]

    loads[1].wait()
    project(pc.a)
    wq_line.hop(1)
    keys.round(1)
    wq_line.hop(2)
    wq_line.spread(1)
    keys.round(2)
    wq_line.here(pc.near(1))
    project(pc.near(1))
    wq_line.hop(3)
    wout_line.start()
    wq_line.spread(2)
    keys.round(3)
    wq_line.here(pc.near(2))
    project(pc.near(2))
    wq_line.spread(3)
    tick(0)
    wq_line.here(pc.near(3))
    project(pc.near(3))

    def fold(scores, values, a0, fresh):
        new_top = jnp.max(scores, axis=-1, keepdims=True)
        if not fresh:
            new_top = jnp.maximum(top_ref[a0], new_top)
        probs = jnp.exp(scores - new_top)
        total = jnp.sum(probs, axis=-1, keepdims=True)
        weighted = jnp.dot(probs.astype(jnp.bfloat16), values, preferred_element_type=jnp.float32)
        if not fresh:
            factor = jnp.exp(top_ref[a0] - new_top)
            total = total + total_ref[a0] * factor
            weighted = weighted + weighted_ref[a0] * factor
        return new_top, total, weighted

    def raw_scores(a0, keys_here):
        return lax.dot_general(queries[a0], keys_here, (((1,), (1,)), ((), ())),
                               preferred_element_type=jnp.float32)

    def over_prefix(e, fresh=False):
        keys.pair_arrived(e)

        def body(a0, carry):
            pair = cached[pl.ds(e * B, B), :span, :].reshape(B * span, 2 * head)
            state = fold(raw_scores(a0, pair[:, :head]), pair[:, head:], a0, fresh)
            top_ref[a0], total_ref[a0], weighted_ref[a0] = state
            return carry

        lax.fori_loop(0, A, body, 0)

    def over_suffix():
        spot = pc.a * slab + lax.broadcasted_iota(jnp.int32, (slab, row_len), 0)
        other = lax.broadcasted_iota(jnp.int32, (slab, row_len), 1)
        ids = seg[...].astype(jnp.float32)
        mine = jnp.sum(jnp.where(other == spot, ids, 0.0), axis=1, keepdims=True)
        allowed = (other <= spot) & (mine == ids)

        def body(a0, carry):
            fresh = cached[:, span:, :].reshape(row_len, 2 * head)
            scores = raw_scores(a0, fresh[:, :head]).reshape(heads, slab, row_len)
            scores = jnp.where(allowed[None], scores, -jnp.inf).reshape(heads * slab, row_len)
            _, total, weighted = fold(scores, fresh[:, head:], a0, False)
            out = (weighted / total).astype(jnp.bfloat16)
            for h in range(heads):
                attn[a0, :, h * head : (h + 1) * head] = out[h * slab : (h + 1) * slab]
            return carry

        lax.fori_loop(0, A, body, 0)

    over_prefix(pc.near(0), True)
    tick(1)
    over_prefix(pc.near(1))
    wout_line.hop(1)
    over_prefix(pc.near(2))
    wout_line.hop(2)
    wout_line.spread(1)
    over_prefix(pc.near(3))
    tick(2)
    wout_line.hop(3)
    wout_line.spread(2)
    over_suffix()
    wout_line.spread(3)

    out_wide = min(512, width)

    def out_part(a0, first_one):
        def column(c, carry):
            cols = span_of(c, out_wide)
            out = jnp.dot(attn[a0], wout[a0, :, cols], preferred_element_type=jnp.float32)
            if not first_one:
                out = out + out_sum[:, cols]
            out_sum[:, cols] = out
            return carry

        lax.fori_loop(0, width // out_wide, column, 0)

    loads[2].wait()
    out_part(pc.a, True)
    for k in range(1, A):
        wout_line.here(pc.near(k))
        out_part(pc.near(k), False)

    def out_copy(o, s):
        here = pl.ds(s * half, half)
        return remote(out_send.at[o - 1, here, :], out_in.at[o - 1, here, :], out_sem.at[o - 1, s],
                      out_recv.at[o - 1, s], pc.side(o))

    for s in range(HALVES):
        for o in range(1, B):
            base = pc.across(o) * rows

            def give(part):
                spot = pl.ds(pl.multiple_of(base + part.start, ROWS), ROWS)
                out_send[o - 1, part, :] = out_sum[spot, :].astype(jnp.bfloat16)

            row_loop(s * half, half, give)
            out_copy(o, s).start()

    gains2 = gain2[...].astype(jnp.float32).reshape(1, width)

    def second(part):
        total = out_sum[pl.ds(pl.multiple_of(pc.b * rows + part.start, ROWS), ROWS), :]
        for o in range(1, B):
            total = total + out_in[o - 1, part, :].astype(jnp.float32)
        out = total.astype(jnp.bfloat16)
        attended[part, :] = out
        mid = (hidden[part, :].astype(jnp.float32) + out.astype(jnp.float32)).astype(jnp.bfloat16)
        middle[part, :] = mid
        normed2[pc.a, part, :] = norm_rows(mid.astype(jnp.float32), gains2)

    for s in range(HALVES):
        for o in range(1, B):
            out_copy(o, s).wait_recv()
        row_loop(s * half, half, second)
        gather.start(s)

    tick(3)
    tick(4)
    loads[3].wait()
    loads[4].wait()

    def expand(e):
        for s in range(B):
            def column(c, carry):
                cols = span_of(c, fc_cols)
                out = jnp.dot(normed2[e], wfc[s, :, cols], preferred_element_type=jnp.float32)
                spot = pl.ds(pl.multiple_of(s * units + c * fc_cols, fc_cols), fc_cols)
                act[span_of(e, rows), spot] = jax.nn.gelu(out, approximate=True).astype(jnp.bfloat16)
                return carry

            lax.fori_loop(0, PIECES, column, 0)

    for i in range(PIECES):
        fc_side.here(i)
    expand(pc.a)
    for r in range(1, A):
        gather.hop(r)
        tick(4 + r)
        expand(pc.near(r))
    mlp("spread", 2 * PIECES - 1)

    end = (pc.a == 0) | (pc.a == A - 1)

    def pass_all(i):
        def go(k, carry):
            reduce.pass_on(pc.far(k), i)
            return carry

        lax.fori_loop(0, A - 1, go, 0)

    def contract(i, carry):
        pr_side.here(i)
        cols = span_of(i, pr_cols)
        out = jnp.dot(act[...], wproj[:, cols], preferred_element_type=jnp.float32)
        term[:, :, cols] = out.astype(jnp.bfloat16).reshape(A, rows, pr_cols)

        @pl.when(end)
        def _():
            pass_all(i)

        @pl.when(jnp.logical_not(end) & (i > 0))
        def _():
            pass_all(i - 1)

        return carry

    lax.fori_loop(0, PIECES, contract, 0)

    @pl.when(jnp.logical_not(end))
    def _():
        pass_all(PIECES - 1)

    def last(part, cols, total):
        layer_out[part, cols] = (middle[part, cols].astype(jnp.float32) + total).astype(jnp.bfloat16)

    def result(i, carry):
        reduce.result(i, last)
        return carry

    lax.fori_loop(0, PIECES, result, 0)
    for o in range(1, pc.pairs):
        dp_copy(o).wait_send()
    for o in range(pc.pairs):
        dp_to_core(o).wait_send()
    for o in range(1, B):
        tok_copy(o).wait_send()
        for s in range(HALVES):
            out_copy(o, s).wait_send()
    keys.finish()
    wq_line.finish()
    wout_line.finish()
    fc_side.finish()
    pr_side.finish()
    gather.finish()
    reduce.finish()


def hand_on(attended, layer_out, attended_to, layer_to):
    attended_to[...] = attended[...]
    layer_to[...] = layer_out[...]


VM = pl.BlockSpec(memory_space=pltpu.VMEM)


def local(n, ndp, hidden_in, norm1_gain, norm2_gain, w_query, w_keyval, w_out, w_fc, w_proj,
          prefix_kv, owner_ids, segment_ids):
    A, B = plane(n)
    rows, width = hidden_in.shape
    head = w_keyval.shape[1] // 2
    query_cols = w_query.shape[1]
    heads = query_cols // head
    span = prefix_kv.shape[1]
    units = w_fc.shape[1]
    q_scale = 1.0 / math.sqrt(head)
    bf, f32 = jnp.bfloat16, jnp.float32
    any_space = pl.BlockSpec(memory_space=pl.ANY)
    own = jax.ShapeDtypeStruct((rows, width), bf)
    V = pltpu.VMEM
    stack = heads * B * rows
    line = V((A, rows, width), bf)
    sides = max(B - 1, 1)
    scratch = [
        V(w_keyval.shape, bf), V((A,) + w_query.shape, bf), V((A,) + w_out.shape, bf),
        V((B,) + w_fc.shape, bf), V((B * units, width), bf),
        V((B, rows, width), bf), line, V((A * rows, B * units), bf), line, line, line,
        V((n, span + rows, 2 * head), bf), V((ndp, span, 2 * head), bf), V((A, stack, head), bf),
        V((A, stack, 1), f32), V((A, stack, 1), f32), V((A, stack, head), f32),
        V((A, B * rows, query_cols), bf), V((B * rows, width), f32),
        V((sides, rows, width), bf), V((sides, rows, width), bf), V((rows, width), bf),
        DMA((5,)),
        DMA((B,)), DMA((sides,)), DMA((sides, HALVES)), DMA((sides, HALVES)),
        DMA((ndp,)), DMA((max(ndp // 2 - 1, 1),)), DMA((ndp // 2,)),
    ]
    scratch += gather_sems(n) + line_weight_sems(n) * 2 + side_weight_sems(n) * 2
    scratch += [DMA((A, HALVES))] * 3 + [DMA((A, PIECES))] * 4
    attended, layer_out = pl.pallas_call(
        functools.partial(layer_kernel, n, ndp, heads, q_scale),
        out_shape=(own, own),
        in_specs=[VM] * 4 + [pl.BlockSpec(memory_space=pltpu.SMEM), VM] + [any_space] * 5,
        out_specs=(VM, VM),
        scratch_shapes=scratch,
        compiler_params=pltpu.CompilerParams(collective_id=1, has_side_effects=True, vmem_limit_bytes=62 << 20),
        name="layer",
    )(hidden_in, norm1_gain, norm2_gain, prefix_kv, owner_ids, segment_ids, w_keyval, w_query, w_out,
      w_fc, w_proj)
    attended, layer_out = pl.pallas_call(
        hand_on, out_shape=(own, own), in_specs=[VM] * 2, out_specs=(VM, VM), name="hand_on",
    )(attended, layer_out)
    return (layer_out, attended)


def solution(mesh):
    return jax.shard_map(
        functools.partial(local, mesh.shape["tensor"], mesh.shape["dp"]),
        mesh=mesh,
        in_specs=(
            P(("dp", "tensor"), None),
            P(),
            P(),
            P(None, "tensor"),
            P(),
            P("tensor", None),
            P(None, "tensor"),
            P("tensor", None),
            P("dp", "tensor", None),
            P(),
            P("dp", None),
        ),
        out_specs=(P(("dp", "tensor"), None), P(("dp", "tensor"), None)),
        check_vma=False,
    )
```

```python
import functools
import math

import jax
import jax.numpy as jnp
from jax import lax
from jax.experimental import pallas as pl
from jax.experimental.pallas import tpu as pltpu
from jax.sharding import PartitionSpec as P

MESH = pl.DeviceIdType.MESH
ROWS = 16
PIECES = 4
HALVES = 2
TEAM = 4


def plane(n):
    lines = 4 if n % 4 == 0 else n
    return lines, n // lines


def norm_rows(widened, gains):
    centre = jnp.mean(widened, axis=-1, keepdims=True)
    centred = widened - centre
    variance = jnp.mean(centred * centred, axis=-1, keepdims=True)
    return (centred * lax.rsqrt(variance + 1e-05) * gains).astype(jnp.bfloat16)


def row_loop(start, rows, body):
    def step(i, carry):
        body(pl.ds(pl.multiple_of(start + i * ROWS, ROWS), ROWS))
        return carry

    lax.fori_loop(0, rows // ROWS, step, 0)


def span_of(i, size):
    return pl.ds(pl.multiple_of(i * size, size), size)


class Place:
    def __init__(self, n, ndp):
        self.n, self.ndp = n, ndp
        self.A, self.B = plane(n)
        self.me = lax.axis_index("tensor")
        self.a = self.me // self.B
        self.b = self.me % self.B
        self.dp = lax.axis_index("dp")
        self.pairs = ndp // 2
        self.q = self.dp % TEAM
        base = self.dp - self.q
        self.q_core = self.q + 1 - 2 * (self.q % 2)
        self.q_far = (self.q + 2) % TEAM
        self.q_diag = (self.q_core + 2) % TEAM
        self.core = {"dp": base + self.q_core}
        self.across_dp = {"dp": base + self.q_far}

    def across(self, o):
        return (self.b + o) % self.B

    def peer(self, a, b):
        return {"tensor": a * self.B + b}

    def side(self, o):
        return self.peer(self.a, self.across(o))

    def up(self):
        return self.peer(jnp.minimum(self.a + 1, self.A - 1), self.b)

    def down(self):
        return self.peer(jnp.maximum(self.a - 1, 0), self.b)

    def same_core(self, o):
        return ((self.dp // 2 + o) % self.pairs) * 2 + self.dp % 2

    def choose(self, k, key):
        found = 0
        for a in range(self.A):
            order = sorted(range(self.A), key=lambda d: key(a, d))
            for i, d in enumerate(order):
                found = found + jnp.where((self.a == a) & (k == i), d, 0)
        return found

    def near(self, k):
        return self.choose(k, lambda a, d: (abs(d - a), d))

    def far(self, k):
        return self.choose(k, lambda a, d: (-abs(d - a), d))


def greet_signal(pc):
    barrier = pltpu.get_barrier_semaphore()

    def signal(device):
        pl.semaphore_signal(barrier, inc=1, device_id=device, device_id_type=MESH)

    @pl.when(pc.a > 0)
    def _():
        signal(pc.peer(pc.a - 1, pc.b))

    @pl.when(pc.a < pc.A - 1)
    def _():
        signal(pc.peer(pc.a + 1, pc.b))

    for o in range(1, pc.B):
        signal(pc.side(o))
    for o in range(1, pc.pairs):
        signal({"dp": pc.same_core(o)})
    signal(pc.core)


def greet_wait(pc):
    ends = jnp.where((pc.a == 0) | (pc.a == pc.A - 1), 1, 2)
    pl.semaphore_wait(pltpu.get_barrier_semaphore(), pc.B - 1 + pc.pairs + ends)


def remote(src, dst, send, recv, device):
    return pltpu.make_async_remote_copy(
        src_ref=src, dst_ref=dst, send_sem=send, recv_sem=recv, device_id=device, device_id_type=MESH
    )


class Gather:
    def __init__(self, place, buf, recv, up, down, side):
        self.pc, self.buf, self.recv, self.up, self.down, self.side = place, buf, recv, up, down, side

    def copy_up(self, a0):
        blk = a0 * self.pc.B + self.pc.b
        return remote(self.buf.at[blk], self.buf.at[blk], self.up.at[a0], self.recv.at[blk], self.pc.up())

    def copy_down(self, a0):
        blk = a0 * self.pc.B + self.pc.b
        return remote(self.buf.at[blk], self.buf.at[blk], self.down.at[a0], self.recv.at[blk], self.pc.down())

    def copy_side(self, a0, o):
        blk = a0 * self.pc.B + self.pc.b
        return remote(self.buf.at[blk], self.buf.at[blk], self.side.at[a0, o - 1], self.recv.at[blk],
                      self.pc.side(o))

    def arrived(self, blk):
        remote(self.buf.at[blk], self.buf.at[blk], self.up.at[0], self.recv.at[blk],
               self.pc.side(1)).wait_recv()

    def start(self):
        pc = self.pc

        @pl.when(pc.a < pc.A - 1)
        def _():
            self.copy_up(pc.a).start()

        @pl.when(pc.a > 0)
        def _():
            self.copy_down(pc.a).start()

        for o in range(1, pc.B):
            self.copy_side(pc.a, o).start()

    def round(self, r):
        pc = self.pc

        @pl.when(pc.a - r >= 0)
        def _():
            a0 = pc.a - r
            self.arrived(a0 * pc.B + pc.b)

            @pl.when(pc.a < pc.A - 1)
            def _():
                self.copy_up(a0).start()

            for o in range(1, pc.B):
                self.copy_side(a0, o).start()

        @pl.when(pc.a + r < pc.A)
        def _():
            a0 = pc.a + r
            self.arrived(a0 * pc.B + pc.b)

            @pl.when(pc.a > 0)
            def _():
                self.copy_down(a0).start()

            for o in range(1, pc.B):
                self.copy_side(a0, o).start()

    def pair_arrived(self, a0):
        for o in range(1, self.pc.B):
            self.arrived(a0 * self.pc.B + self.pc.across(o))

    def finish(self):
        pc = self.pc
        for a0 in range(pc.A):
            for o in range(1, pc.B):
                self.copy_side(a0, o).wait_send()

            @pl.when((pc.a >= a0) & (pc.a < pc.A - 1))
            def _():
                self.copy_up(a0).wait_send()

            @pl.when((pc.a <= a0) & (pc.a > 0))
            def _():
                self.copy_down(a0).wait_send()


DMA = pltpu.SemaphoreType.DMA


def gather_sems(n):
    A, B = plane(n)
    return [DMA((n,)), DMA((A,)), DMA((A,)), DMA((A, max(B - 1, 1)))]


class Team:
    def __init__(self, place, part, recv, far_send, core_send):
        self.pc, self.part, self.recv, self.far_send, self.core_send = place, part, recv, far_send, core_send

    def far_copy(self, s):
        pc = self.pc
        ref = self.part(s, pc.q)
        return remote(ref, ref, self.far_send.at[s], self.recv.at[s, pc.q], pc.across_dp)

    def core_copy(self, s, which):
        pc = self.pc
        q = pc.q_far if which else pc.q
        ref = self.part(s, q)
        return remote(ref, ref, self.core_send.at[s, which], self.recv.at[s, q], pc.core)

    def wait(self, s, q):
        ref = self.part(s, q)
        remote(ref, ref, self.far_send.at[s], self.recv.at[s, q], self.pc.core).wait_recv()

    def landed(self, s):
        self.wait(s, self.pc.q)
        self.far_copy(s).start()
        self.core_copy(s, 0).start()

    def spread(self, s):
        self.wait(s, self.pc.q_far)
        self.core_copy(s, 1).start()

    def here(self, s):
        self.wait(s, self.pc.q_core)
        self.wait(s, self.pc.q_diag)

    def finish(self, s):
        self.far_copy(s).wait_send()
        self.core_copy(s, 0).wait_send()
        self.core_copy(s, 1).wait_send()


def team_sems(slots):
    return [DMA((slots, TEAM)), DMA((slots,)), DMA((slots, 2))]


class LineWeights:
    def __init__(self, place, hbm, buf, recv, far_send, core_send, up, down):
        self.pc, self.hbm, self.up, self.down, self.recv = place, hbm, up, down, recv
        quarter = buf.shape[1] // TEAM
        self.part = lambda s, q: buf.at[s, span_of(q, quarter), :]
        self.own = lambda: hbm.at[span_of(place.q, quarter), :]
        self.team = Team(place, self.part, recv, far_send, core_send)

    def copy_up(self, a0, src=None):
        pc = self.pc
        ref = self.part(a0, pc.q)
        return remote(ref if src is None else src, ref, self.up.at[a0], self.recv.at[a0, pc.q], pc.up())

    def copy_down(self, a0, src=None):
        pc = self.pc
        ref = self.part(a0, pc.q)
        return remote(ref if src is None else src, ref, self.down.at[a0], self.recv.at[a0, pc.q], pc.down())

    def start(self):
        pc = self.pc

        @pl.when(pc.a < pc.A - 1)
        def _():
            self.copy_up(pc.a, self.own()).start()

        @pl.when(pc.a > 0)
        def _():
            self.copy_down(pc.a, self.own()).start()

    def hop(self, r):
        pc = self.pc

        @pl.when(pc.a - r >= 0)
        def _():
            self.team.landed(pc.a - r)

            @pl.when(pc.a < pc.A - 1)
            def _():
                self.copy_up(pc.a - r).start()

        @pl.when(pc.a + r < pc.A)
        def _():
            self.team.landed(pc.a + r)

            @pl.when(pc.a > 0)
            def _():
                self.copy_down(pc.a + r).start()

    def spread(self, r):
        pc = self.pc

        @pl.when(pc.a - r >= 0)
        def _():
            self.team.spread(pc.a - r)

        @pl.when(pc.a + r < pc.A)
        def _():
            self.team.spread(pc.a + r)

    def here(self, a0):
        self.team.here(a0)

    def finish(self):
        pc = self.pc
        for a0 in range(pc.A):

            @pl.when((pc.a >= a0) & (pc.a < pc.A - 1))
            def _():
                self.copy_up(a0).wait_send()

            @pl.when((pc.a <= a0) & (pc.a > 0))
            def _():
                self.copy_down(a0).wait_send()

            @pl.when(pc.a != a0)
            def _():
                self.team.finish(a0)


def line_weight_sems(n):
    A, _ = plane(n)
    return team_sems(A) + [DMA((A,)), DMA((A,))]


class SideWeights:
    def __init__(self, place, part, own, recv, far_send, core_send, side_send):
        self.pc, self.part3, self.own, self.recv, self.side_send = place, part, own, recv, side_send
        self.team = Team(place, lambda s, q: part(s // PIECES, s % PIECES, q), recv, far_send, core_send)

    def slots(self, i):
        return [self.pc.across(o) * PIECES + i for o in range(1, self.pc.B)]

    def copy(self, i, o):
        pc = self.pc
        return remote(self.own(i, pc.q), self.part3(pc.b, i, pc.q), self.side_send.at[o - 1, i],
                      self.recv.at[pc.b * PIECES + i, pc.q], pc.side(o))

    def start(self, i):
        for o in range(1, self.pc.B):
            self.copy(i, o).start()

    def hop(self, i):
        for s in self.slots(i):
            self.team.landed(s)

    def spread(self, i):
        for s in self.slots(i):
            self.team.spread(s)

    def here(self, i):
        for s in self.slots(i):
            self.team.here(s)

    def finish(self):
        for i in range(PIECES):
            for o in range(1, self.pc.B):
                self.copy(i, o).wait_send()
            for s in self.slots(i):
                self.team.finish(s)


def side_weight_sems(n):
    _, B = plane(n)
    return team_sems(B * PIECES) + [DMA((max(B - 1, 1), PIECES))]


class LineGather:
    def __init__(self, place, buf, recv, up, down):
        self.pc, self.buf, self.recv, self.up, self.down = place, buf, recv, up, down
        self.half = buf.shape[1] // HALVES

    def ref(self, a0, s):
        return self.buf.at[a0, pl.ds(s * self.half, self.half), :]

    def copy_up(self, a0, s):
        return remote(self.ref(a0, s), self.ref(a0, s), self.up.at[a0, s], self.recv.at[a0, s], self.pc.up())

    def copy_down(self, a0, s):
        return remote(self.ref(a0, s), self.ref(a0, s), self.down.at[a0, s], self.recv.at[a0, s], self.pc.down())

    def start(self, s):
        pc = self.pc

        @pl.when(pc.a < pc.A - 1)
        def _():
            self.copy_up(pc.a, s).start()

        @pl.when(pc.a > 0)
        def _():
            self.copy_down(pc.a, s).start()

    def hop(self, r):
        pc = self.pc
        for s in range(HALVES):

            @pl.when(pc.a - r >= 0)
            def _():
                self.copy_up(pc.a - r, s).wait_recv()

                @pl.when(pc.a < pc.A - 1)
                def _():
                    self.copy_up(pc.a - r, s).start()

            @pl.when(pc.a + r < pc.A)
            def _():
                self.copy_down(pc.a + r, s).wait_recv()

                @pl.when(pc.a > 0)
                def _():
                    self.copy_down(pc.a + r, s).start()

    def finish(self):
        pc = self.pc
        for a0 in range(pc.A):
            for s in range(HALVES):

                @pl.when((pc.a >= a0) & (pc.a < pc.A - 1))
                def _():
                    self.copy_up(a0, s).wait_send()

                @pl.when((pc.a <= a0) & (pc.a > 0))
                def _():
                    self.copy_down(a0, s).wait_send()


class LineReduce:
    def __init__(self, place, term, up_in, down_in, up_send, up_recv, down_send, down_recv):
        self.pc, self.term, self.up_in, self.down_in = place, term, up_in, down_in
        self.up_send, self.up_recv, self.down_send, self.down_recv = up_send, up_recv, down_send, down_recv
        self.rows = term.shape[1]
        self.wide = term.shape[2] // PIECES

    def copy_up(self, d, i):
        cols = span_of(i, self.wide)
        return remote(self.term.at[d, :, cols], self.up_in.at[d, :, cols], self.up_send.at[d, i],
                      self.up_recv.at[d, i], self.pc.up())

    def copy_down(self, d, i):
        cols = span_of(i, self.wide)
        return remote(self.term.at[d, :, cols], self.down_in.at[d, :, cols], self.down_send.at[d, i],
                      self.down_recv.at[d, i], self.pc.down())

    def add(self, d, i, arrived):
        cols = span_of(i, self.wide)

        def body(rows):
            total = self.term[d, rows, cols].astype(jnp.float32) + arrived[d, rows, cols].astype(jnp.float32)
            self.term[d, rows, cols] = total.astype(jnp.bfloat16)

        row_loop(0, self.rows, body)

    def pass_on(self, d, i):
        pc = self.pc

        @pl.when(d > pc.a)
        def _():
            @pl.when(pc.a > 0)
            def _():
                self.copy_up(d, i).wait_recv()
                self.add(d, i, self.up_in)

            self.copy_up(d, i).start()

        @pl.when(d < pc.a)
        def _():
            @pl.when(pc.a < pc.A - 1)
            def _():
                self.copy_down(d, i).wait_recv()
                self.add(d, i, self.down_in)

            self.copy_down(d, i).start()

    def result(self, i, use):
        pc = self.pc
        cols = span_of(i, self.wide)

        def go(terms):
            def body(rows):
                total = self.term[pc.a, rows, cols].astype(jnp.float32)
                for arrived in terms:
                    total = total + arrived[pc.a, rows, cols].astype(jnp.float32)
                use(rows, cols, total)

            row_loop(0, self.rows, body)

        @pl.when(pc.a == 0)
        def _():
            self.copy_down(pc.a, i).wait_recv()
            go([self.down_in])

        @pl.when(pc.a == pc.A - 1)
        def _():
            self.copy_up(pc.a, i).wait_recv()
            go([self.up_in])

        @pl.when((pc.a > 0) & (pc.a < pc.A - 1))
        def _():
            self.copy_up(pc.a, i).wait_recv()
            self.copy_down(pc.a, i).wait_recv()
            go([self.up_in, self.down_in])

    def finish(self):
        pc = self.pc
        for d in range(pc.A):
            for i in range(PIECES):

                @pl.when(pc.a < d)
                def _():
                    self.copy_up(d, i).wait_send()

                @pl.when(pc.a > d)
                def _():
                    self.copy_down(d, i).wait_send()


def layer_kernel(n, ndp, heads, q_scale, hidden, gain1, gain2, prefix, owners, seg, w_keyval_hbm, w_query_hbm,
                 w_out_hbm, w_fc_hbm, w_proj_hbm, attended, layer_out, *scratch):
    pc = Place(n, ndp)
    A, B = pc.A, pc.B
    greet_signal(pc)
    scratch = list(scratch)

    def take(count):
        got = scratch[:count]
        del scratch[:count]
        return got

    wkv, wq, wout, wfc, wproj = take(5)
    normed, normed2, act, term, up_in, down_in = take(6)
    cached, from_dp, queries, top_ref, total_ref, weighted_ref, attn, out_sum, out_send, out_in, middle = take(11)
    (load,) = take(1)
    tok_recv, tok_send, out_sem, out_recv = take(4)
    dp_recv, dp_send, dp_core = take(3)
    rows, width = hidden.shape
    slab = B * rows
    span = prefix.shape[1]
    row_len = n * rows
    head = wkv.shape[1] // 2
    units = w_fc_hbm.shape[1]
    half = rows // HALVES
    dp = pc.dp

    keys = Gather(pc, cached, *take(4))
    wq_line = LineWeights(pc, w_query_hbm, wq, *take(5))
    wout_line = LineWeights(pc, w_out_hbm, wout, *take(5))
    fc_rows, fc_cols = width // TEAM, units // PIECES
    pr_rows, pr_cols = units // TEAM, width // PIECES
    fc_side = SideWeights(
        pc,
        lambda s, i, q: wfc.at[s, span_of(q, fc_rows), span_of(i, fc_cols)],
        lambda i, q: w_fc_hbm.at[span_of(q, fc_rows), span_of(i, fc_cols)],
        *take(4))
    pr_side = SideWeights(
        pc,
        lambda s, i, q: wproj.at[pl.ds(pl.multiple_of(s * units + q * pr_rows, pr_rows), pr_rows), span_of(i, pr_cols)],
        lambda i, q: w_proj_hbm.at[span_of(q, pr_rows), span_of(i, pr_cols)],
        *take(4))
    gather = LineGather(pc, normed2, *take(3))
    reduce = LineReduce(pc, term, up_in, down_in, *take(4))

    def mlp(kind, j):
        if 0 <= j < 2 * PIECES:
            getattr(fc_side if j < PIECES else pr_side, kind)(j % PIECES)

    def tick(j, start=True):
        mlp("hop", j)
        if start:
            mlp("start", j + 2)
        mlp("spread", j - 1)

    loads = [
        pltpu.make_async_copy(w_keyval_hbm, wkv, load.at[0]),
        pltpu.make_async_copy(w_query_hbm, wq.at[pc.a], load.at[1]),
        pltpu.make_async_copy(w_out_hbm, wout.at[pc.a], load.at[2]),
        pltpu.make_async_copy(w_fc_hbm, wfc.at[pc.b], load.at[3]),
        pltpu.make_async_copy(w_proj_hbm, wproj.at[span_of(pc.b, units), :], load.at[4]),
    ]
    for copy in loads:
        copy.start()

    gains = gain1[...].astype(jnp.float32).reshape(1, width)

    def first(part):
        normed[pc.b, part, :] = norm_rows(hidden[part, :].astype(jnp.float32), gains)

    greet_wait(pc)

    def dp_copy(o):
        return remote(prefix.at[0], from_dp.at[dp], dp_send.at[o - 1], dp_recv.at[dp], {"dp": pc.same_core(o)})

    def dp_to_core(o):
        src = pc.same_core(o)
        ref = prefix.at[0] if o == 0 else from_dp.at[src]
        return remote(ref, from_dp.at[src], dp_core.at[o], dp_recv.at[src], pc.core)

    def dp_arrived(src):
        remote(prefix.at[0], from_dp.at[src], dp_send.at[0], dp_recv.at[src], pc.core).wait_recv()

    for o in range(1, pc.pairs):
        dp_copy(o).start()
    dp_to_core(0).start()
    wq_line.start()
    row_loop(0, rows, first)

    def tok_copy(o):
        return remote(normed.at[pc.b], normed.at[pc.b], tok_send.at[o - 1], tok_recv.at[pc.b], pc.side(o))

    for o in range(1, B):
        tok_copy(o).start()
    from_dp[dp] = prefix[0]
    loads[0].wait()
    cached[pc.me, span:, :] = jnp.dot(
        normed[pc.b], wkv[...], preferred_element_type=jnp.float32
    ).astype(jnp.bfloat16)
    for o in range(1, pc.pairs):
        dp_arrived(pc.same_core(o))
        dp_to_core(o).start()
    wq_line.hop(1)
    for o in range(pc.pairs):
        src = pc.same_core(o)
        dp_arrived(src + 1 - 2 * (src % 2))
    cached[pc.me, :span, :] = from_dp[owners[dp]]
    keys.start()
    for o in range(1, B):
        s = pc.across(o)
        remote(normed.at[s], normed.at[s], tok_send.at[0], tok_recv.at[s], pc.side(1)).wait_recv()
    mlp("start", 0)

    def project(a0):
        left = normed[...].reshape(slab, width)
        out = (jnp.dot(left, wq[a0], preferred_element_type=jnp.float32) * q_scale).astype(jnp.bfloat16)
        for h in range(heads):
            queries[a0, h * slab : (h + 1) * slab, :] = out[:, h * head : (h + 1) * head]

    loads[1].wait()
    project(pc.a)
    wq_line.hop(2)
    wq_line.spread(1)
    wq_line.here(pc.near(1))
    project(pc.near(1))
    keys.round(1)
    wq_line.hop(3)
    wq_line.spread(2)
    wout_line.start()
    mlp("start", 1)
    wq_line.here(pc.near(2))
    project(pc.near(2))
    wq_line.spread(3)
    wq_line.here(pc.near(3))
    project(pc.near(3))

    def fold(scores, values, a0, fresh):
        new_top = jnp.max(scores, axis=-1, keepdims=True)
        if not fresh:
            new_top = jnp.maximum(top_ref[a0], new_top)
        probs = jnp.exp(scores - new_top)
        total = jnp.sum(probs, axis=-1, keepdims=True)
        weighted = jnp.dot(probs.astype(jnp.bfloat16), values, preferred_element_type=jnp.float32)
        if not fresh:
            factor = jnp.exp(top_ref[a0] - new_top)
            total = total + total_ref[a0] * factor
            weighted = weighted + weighted_ref[a0] * factor
        return new_top, total, weighted

    def raw_scores(a0, keys_here):
        return lax.dot_general(queries[a0], keys_here, (((1,), (1,)), ((), ())),
                               preferred_element_type=jnp.float32)

    def over_prefix(e, part, fresh=False):
        if part == 0:
            keys.pair_arrived(e)

        def body(a0, carry):
            pair = cached[pl.ds(e * B, B), :span, :].reshape(B * span, 2 * head)
            state = fold(raw_scores(a0, pair[:, :head]), pair[:, head:], a0, fresh)
            top_ref[a0], total_ref[a0], weighted_ref[a0] = state
            return carry

        lax.fori_loop(part * A // 2, (part + 1) * A // 2, body, 0)

    def over_suffix():
        spot = pc.a * slab + lax.broadcasted_iota(jnp.int32, (slab, row_len), 0)
        other = lax.broadcasted_iota(jnp.int32, (slab, row_len), 1)
        ids = seg[...].astype(jnp.float32)
        mine = jnp.sum(jnp.where(other == spot, ids, 0.0), axis=1, keepdims=True)
        allowed = (other <= spot) & (mine == ids)

        def body(a0, carry):
            fresh = cached[:, span:, :].reshape(row_len, 2 * head)
            scores = raw_scores(a0, fresh[:, :head]).reshape(heads, slab, row_len)
            scores = jnp.where(allowed[None], scores, -jnp.inf).reshape(heads * slab, row_len)
            _, total, weighted = fold(scores, fresh[:, head:], a0, False)
            out = (weighted / total).astype(jnp.bfloat16)
            for h in range(heads):
                attn[a0, :, h * head : (h + 1) * head] = out[h * slab : (h + 1) * slab]
            return carry

        lax.fori_loop(0, A, body, 0)

    over_prefix(pc.near(0), 0, True)
    keys.round(2)
    over_prefix(pc.near(0), 1, True)
    over_prefix(pc.near(1), 0)
    keys.round(3)
    tick(0)
    over_prefix(pc.near(1), 1)
    wout_line.hop(1)
    over_prefix(pc.near(2), 0)
    tick(1)
    over_prefix(pc.near(2), 1)
    wout_line.hop(2)
    wout_line.spread(1)
    over_prefix(pc.near(3), 0)
    tick(2)
    over_prefix(pc.near(3), 1)
    wout_line.hop(3)
    wout_line.spread(2)
    over_suffix()
    wout_line.spread(3)
    tick(3)

    out_wide = min(512, width)

    def out_part(a0, first_one):
        def column(c, carry):
            cols = span_of(c, out_wide)
            out = jnp.dot(attn[a0], wout[a0, :, cols], preferred_element_type=jnp.float32)
            if not first_one:
                out = out + out_sum[:, cols]
            out_sum[:, cols] = out
            return carry

        lax.fori_loop(0, width // out_wide, column, 0)

    loads[2].wait()
    out_part(pc.a, True)
    for k in range(1, A):
        wout_line.here(pc.near(k))
        out_part(pc.near(k), False)
    tick(4, False)

    def out_copy(o, s):
        here = pl.ds(s * half, half)
        return remote(out_send.at[o - 1, here, :], out_in.at[o - 1, here, :], out_sem.at[o - 1, s],
                      out_recv.at[o - 1, s], pc.side(o))

    for s in range(HALVES):
        for o in range(1, B):
            base = pc.across(o) * rows

            def give(part):
                spot = pl.ds(pl.multiple_of(base + part.start, ROWS), ROWS)
                out_send[o - 1, part, :] = out_sum[spot, :].astype(jnp.bfloat16)

            row_loop(s * half, half, give)
            out_copy(o, s).start()

    gains2 = gain2[...].astype(jnp.float32).reshape(1, width)

    def second(part):
        total = out_sum[pl.ds(pl.multiple_of(pc.b * rows + part.start, ROWS), ROWS), :]
        for o in range(1, B):
            total = total + out_in[o - 1, part, :].astype(jnp.float32)
        out = total.astype(jnp.bfloat16)
        attended[part, :] = out
        mid = (hidden[part, :].astype(jnp.float32) + out.astype(jnp.float32)).astype(jnp.bfloat16)
        middle[part, :] = mid
        normed2[pc.a, part, :] = norm_rows(mid.astype(jnp.float32), gains2)

    for s in range(HALVES):
        for o in range(1, B):
            out_copy(o, s).wait_recv()
        row_loop(s * half, half, second)
        gather.start(s)

    mlp("start", 6)
    loads[3].wait()
    loads[4].wait()

    def expand(e):
        for s in range(B):
            def column(c, carry):
                cols = span_of(c, fc_cols)
                out = jnp.dot(normed2[e], wfc[s, :, cols], preferred_element_type=jnp.float32)
                spot = pl.ds(pl.multiple_of(s * units + c * fc_cols, fc_cols), fc_cols)
                act[span_of(e, rows), spot] = jax.nn.gelu(out, approximate=True).astype(jnp.bfloat16)
                return carry

            lax.fori_loop(0, PIECES, column, 0)

    end = (pc.a == 0) | (pc.a == A - 1)

    def contract(k, pieces):
        e = pc.near(k)

        def piece(i, carry):
            cols = span_of(i, pr_cols)
            out = jnp.dot(act[span_of(e, rows), :], wproj[:, cols], preferred_element_type=jnp.float32)
            term[e, :, cols] = out.astype(jnp.bfloat16)
            if k > 0:

                @pl.when(end)
                def _():
                    reduce.pass_on(e, i)

            return carry

        lax.fori_loop(pieces[0], pieces[1], piece, 0)

    for i in range(PIECES):
        fc_side.here(i)
    expand(pc.a)
    tick(5)
    gather.hop(1)
    expand(pc.near(1))
    tick(6)
    pr_side.here(0)
    pr_side.here(1)
    contract(1, (0, 2))
    contract(0, (0, 2))
    gather.hop(2)
    expand(pc.near(2))
    tick(7)
    pr_side.here(2)
    contract(1, (2, 3))
    contract(2, (0, 3))
    mlp("spread", 7)
    pr_side.here(3)
    contract(1, (3, 4))
    contract(2, (3, 4))
    gather.hop(3)
    expand(pc.near(3))
    contract(3, (0, 4))
    contract(0, (2, 4))

    def last(part, cols, total):
        layer_out[part, cols] = (middle[part, cols].astype(jnp.float32) + total).astype(jnp.bfloat16)

    def result(i, carry):
        reduce.result(i, last)
        return carry

    @pl.when(jnp.logical_not(end))
    def _():
        low = pc.a < A // 2
        middle_block = jnp.where(low, pc.a + 1, pc.a - 1)
        far_block = jnp.where(low, A - 1, 0)
        near_block = A - 1 - far_block

        def to_middle(i, carry):
            reduce.pass_on(middle_block, i)
            return carry

        lax.fori_loop(0, PIECES, to_middle, 0)
        reduce.pass_on(far_block, 0)
        lax.fori_loop(0, PIECES, result, 0)

        def both(i, carry):
            reduce.pass_on(far_block, i + 1)
            reduce.pass_on(near_block, i)
            return carry

        lax.fori_loop(0, PIECES - 1, both, 0)
        reduce.pass_on(near_block, PIECES - 1)

    @pl.when(end)
    def _():
        lax.fori_loop(0, PIECES, result, 0)

    for o in range(1, pc.pairs):
        dp_copy(o).wait_send()
    for o in range(pc.pairs):
        dp_to_core(o).wait_send()
    for o in range(1, B):
        tok_copy(o).wait_send()
        for s in range(HALVES):
            out_copy(o, s).wait_send()
    keys.finish()
    wq_line.finish()
    wout_line.finish()
    fc_side.finish()
    pr_side.finish()
    gather.finish()
    reduce.finish()


def hand_on(attended, layer_out, attended_to, layer_to):
    attended_to[...] = attended[...]
    layer_to[...] = layer_out[...]


VM = pl.BlockSpec(memory_space=pltpu.VMEM)


def local(n, ndp, hidden_in, norm1_gain, norm2_gain, w_query, w_keyval, w_out, w_fc, w_proj,
          prefix_kv, owner_ids, segment_ids):
    A, B = plane(n)
    rows, width = hidden_in.shape
    head = w_keyval.shape[1] // 2
    query_cols = w_query.shape[1]
    heads = query_cols // head
    span = prefix_kv.shape[1]
    units = w_fc.shape[1]
    q_scale = 1.0 / math.sqrt(head)
    bf, f32 = jnp.bfloat16, jnp.float32
    any_space = pl.BlockSpec(memory_space=pl.ANY)
    own = jax.ShapeDtypeStruct((rows, width), bf)
    V = pltpu.VMEM
    stack = heads * B * rows
    line = V((A, rows, width), bf)
    sides = max(B - 1, 1)
    scratch = [
        V(w_keyval.shape, bf), V((A,) + w_query.shape, bf), V((A,) + w_out.shape, bf),
        V((B,) + w_fc.shape, bf), V((B * units, width), bf),
        V((B, rows, width), bf), line, V((A * rows, B * units), bf), line, line, line,
        V((n, span + rows, 2 * head), bf), V((ndp, span, 2 * head), bf), V((A, stack, head), bf),
        V((A, stack, 1), f32), V((A, stack, 1), f32), V((A, stack, head), f32),
        V((A, B * rows, query_cols), bf), V((B * rows, width), f32),
        V((sides, rows, width), bf), V((sides, rows, width), bf), V((rows, width), bf),
        DMA((5,)),
        DMA((B,)), DMA((sides,)), DMA((sides, HALVES)), DMA((sides, HALVES)),
        DMA((ndp,)), DMA((max(ndp // 2 - 1, 1),)), DMA((ndp // 2,)),
    ]
    scratch += gather_sems(n) + line_weight_sems(n) * 2 + side_weight_sems(n) * 2
    scratch += [DMA((A, HALVES))] * 3 + [DMA((A, PIECES))] * 4
    attended, layer_out = pl.pallas_call(
        functools.partial(layer_kernel, n, ndp, heads, q_scale),
        out_shape=(own, own),
        in_specs=[VM] * 4 + [pl.BlockSpec(memory_space=pltpu.SMEM), VM] + [any_space] * 5,
        out_specs=(VM, VM),
        scratch_shapes=scratch,
        compiler_params=pltpu.CompilerParams(collective_id=1, has_side_effects=True, vmem_limit_bytes=62 << 20),
        name="layer",
    )(hidden_in, norm1_gain, norm2_gain, prefix_kv, owner_ids, segment_ids, w_keyval, w_query, w_out,
      w_fc, w_proj)
    attended, layer_out = pl.pallas_call(
        hand_on, out_shape=(own, own), in_specs=[VM] * 2, out_specs=(VM, VM), name="hand_on",
    )(attended, layer_out)
    return (layer_out, attended)


def solution(mesh):
    return jax.shard_map(
        functools.partial(local, mesh.shape["tensor"], mesh.shape["dp"]),
        mesh=mesh,
        in_specs=(
            P(("dp", "tensor"), None),
            P(),
            P(),
            P(None, "tensor"),
            P(),
            P("tensor", None),
            P(None, "tensor"),
            P("tensor", None),
            P("dp", "tensor", None),
            P(),
            P("dp", None),
        ),
        out_specs=(P(("dp", "tensor"), None), P(("dp", "tensor"), None)),
        check_vma=False,
    )
```

```python
import functools
import math

import jax
import jax.numpy as jnp
from jax import lax
from jax.experimental import pallas as pl
from jax.experimental.pallas import tpu as pltpu
from jax.sharding import PartitionSpec as P

MESH = pl.DeviceIdType.MESH
ROWS = 16
PIECES = 4
SIDE = 8
PARTS = 2
HALVES = 2
TEAM = 4


def plane(n):
    lines = 4 if n % 4 == 0 else n
    return lines, n // lines


def norm_rows(widened, gains):
    centre = jnp.mean(widened, axis=-1, keepdims=True)
    centred = widened - centre
    variance = jnp.mean(centred * centred, axis=-1, keepdims=True)
    return (centred * lax.rsqrt(variance + 1e-05) * gains).astype(jnp.bfloat16)


def row_loop(start, rows, body):
    def step(i, carry):
        body(pl.ds(pl.multiple_of(start + i * ROWS, ROWS), ROWS))
        return carry

    lax.fori_loop(0, rows // ROWS, step, 0)


def span_of(i, size):
    return pl.ds(pl.multiple_of(i * size, size), size)


class Place:
    def __init__(self, n, ndp):
        self.n, self.ndp = n, ndp
        self.A, self.B = plane(n)
        self.me = lax.axis_index("tensor")
        self.a = self.me // self.B
        self.b = self.me % self.B
        self.dp = lax.axis_index("dp")
        self.pairs = ndp // 2
        self.q = self.dp % TEAM
        base = self.dp - self.q
        self.q_core = self.q + 1 - 2 * (self.q % 2)
        self.q_far = (self.q + 2) % TEAM
        self.q_diag = (self.q_core + 2) % TEAM
        self.core = {"dp": base + self.q_core}
        self.across_dp = {"dp": base + self.q_far}

    def across(self, o):
        return (self.b + o) % self.B

    def peer(self, a, b):
        return {"tensor": a * self.B + b}

    def side(self, o):
        return self.peer(self.a, self.across(o))

    def up(self):
        return self.peer(jnp.minimum(self.a + 1, self.A - 1), self.b)

    def down(self):
        return self.peer(jnp.maximum(self.a - 1, 0), self.b)

    def same_core(self, o):
        return ((self.dp // 2 + o) % self.pairs) * 2 + self.dp % 2

    def choose(self, k, key):
        found = 0
        for a in range(self.A):
            order = sorted(range(self.A), key=lambda d: key(a, d))
            for i, d in enumerate(order):
                found = found + jnp.where((self.a == a) & (k == i), d, 0)
        return found

    def near(self, k):
        return self.choose(k, lambda a, d: (abs(d - a), d))

    def far(self, k):
        return self.choose(k, lambda a, d: (-abs(d - a), d))


def greet_signal(pc):
    barrier = pltpu.get_barrier_semaphore()

    def signal(device):
        pl.semaphore_signal(barrier, inc=1, device_id=device, device_id_type=MESH)

    @pl.when(pc.a > 0)
    def _():
        signal(pc.peer(pc.a - 1, pc.b))

    @pl.when(pc.a < pc.A - 1)
    def _():
        signal(pc.peer(pc.a + 1, pc.b))

    for o in range(1, pc.B):
        signal(pc.side(o))
    for o in range(1, pc.pairs):
        signal({"dp": pc.same_core(o)})
    signal(pc.core)


def greet_wait(pc):
    ends = jnp.where((pc.a == 0) | (pc.a == pc.A - 1), 1, 2)
    pl.semaphore_wait(pltpu.get_barrier_semaphore(), pc.B - 1 + pc.pairs + ends)


def remote(src, dst, send, recv, device):
    return pltpu.make_async_remote_copy(
        src_ref=src, dst_ref=dst, send_sem=send, recv_sem=recv, device_id=device, device_id_type=MESH
    )


class Gather:
    def __init__(self, place, buf, recv, up, down, side):
        self.pc, self.buf, self.recv, self.up, self.down, self.side = place, buf, recv, up, down, side

    def copy_up(self, a0):
        blk = a0 * self.pc.B + self.pc.b
        return remote(self.buf.at[blk], self.buf.at[blk], self.up.at[a0], self.recv.at[blk], self.pc.up())

    def copy_down(self, a0):
        blk = a0 * self.pc.B + self.pc.b
        return remote(self.buf.at[blk], self.buf.at[blk], self.down.at[a0], self.recv.at[blk], self.pc.down())

    def copy_side(self, a0, o):
        blk = a0 * self.pc.B + self.pc.b
        return remote(self.buf.at[blk], self.buf.at[blk], self.side.at[a0, o - 1], self.recv.at[blk],
                      self.pc.side(o))

    def arrived(self, blk):
        remote(self.buf.at[blk], self.buf.at[blk], self.up.at[0], self.recv.at[blk],
               self.pc.side(1)).wait_recv()

    def start(self):
        pc = self.pc

        @pl.when(pc.a < pc.A - 1)
        def _():
            self.copy_up(pc.a).start()

        @pl.when(pc.a > 0)
        def _():
            self.copy_down(pc.a).start()

        for o in range(1, pc.B):
            self.copy_side(pc.a, o).start()

    def round(self, r):
        pc = self.pc

        @pl.when(pc.a - r >= 0)
        def _():
            a0 = pc.a - r
            self.arrived(a0 * pc.B + pc.b)

            @pl.when(pc.a < pc.A - 1)
            def _():
                self.copy_up(a0).start()

            for o in range(1, pc.B):
                self.copy_side(a0, o).start()

        @pl.when(pc.a + r < pc.A)
        def _():
            a0 = pc.a + r
            self.arrived(a0 * pc.B + pc.b)

            @pl.when(pc.a > 0)
            def _():
                self.copy_down(a0).start()

            for o in range(1, pc.B):
                self.copy_side(a0, o).start()

    def pair_arrived(self, a0):
        for o in range(1, self.pc.B):
            self.arrived(a0 * self.pc.B + self.pc.across(o))

    def finish(self):
        pc = self.pc
        for a0 in range(pc.A):
            for o in range(1, pc.B):
                self.copy_side(a0, o).wait_send()

            @pl.when((pc.a >= a0) & (pc.a < pc.A - 1))
            def _():
                self.copy_up(a0).wait_send()

            @pl.when((pc.a <= a0) & (pc.a > 0))
            def _():
                self.copy_down(a0).wait_send()


DMA = pltpu.SemaphoreType.DMA


def gather_sems(n):
    A, B = plane(n)
    return [DMA((n,)), DMA((A,)), DMA((A,)), DMA((A, max(B - 1, 1)))]


class Team:
    def __init__(self, place, part, recv, far_send, core_send):
        self.pc, self.part, self.recv, self.far_send, self.core_send = place, part, recv, far_send, core_send

    def far_copy(self, s):
        pc = self.pc
        ref = self.part(s, pc.q)
        return remote(ref, ref, self.far_send.at[s], self.recv.at[s, pc.q], pc.across_dp)

    def core_copy(self, s, which):
        pc = self.pc
        q = pc.q_far if which else pc.q
        ref = self.part(s, q)
        return remote(ref, ref, self.core_send.at[s, which], self.recv.at[s, q], pc.core)

    def wait(self, s, q):
        ref = self.part(s, q)
        remote(ref, ref, self.far_send.at[s], self.recv.at[s, q], self.pc.core).wait_recv()

    def landed(self, s):
        self.far_copy(s).start()
        self.core_copy(s, 0).start()

    def spread(self, s):
        self.wait(s, self.pc.q_far)
        self.core_copy(s, 1).start()

    def here(self, s):
        self.wait(s, self.pc.q_core)
        self.wait(s, self.pc.q_diag)

    def finish(self, s):
        self.far_copy(s).wait_send()
        self.core_copy(s, 0).wait_send()
        self.core_copy(s, 1).wait_send()


def team_sems(slots):
    return [DMA((slots, TEAM)), DMA((slots,)), DMA((slots, 2))]


class LineWeights:
    def __init__(self, place, hbm, buf, parts, recv, far_send, core_send, up, down):
        self.pc, self.hbm, self.up, self.down, self.recv, self.parts = place, hbm, up, down, recv, parts
        quarter = buf.shape[1] // TEAM
        cols = buf.shape[2] // parts
        self.part = lambda s, q: buf.at[s // parts, span_of(q, quarter), span_of(s % parts, cols)]
        self.own = lambda j: hbm.at[span_of(place.q, quarter), pl.ds(j * cols, cols)]
        self.team = Team(place, self.part, recv, far_send, core_send)

    def copy_up(self, s, src=None):
        pc = self.pc
        ref = self.part(s, pc.q)
        return remote(ref if src is None else src, ref, self.up.at[s], self.recv.at[s, pc.q], pc.up())

    def copy_down(self, s, src=None):
        pc = self.pc
        ref = self.part(s, pc.q)
        return remote(ref if src is None else src, ref, self.down.at[s], self.recv.at[s, pc.q], pc.down())

    def start(self, j=0):
        pc = self.pc
        s = pc.a * self.parts + j

        @pl.when(pc.a < pc.A - 1)
        def _():
            self.copy_up(s, self.own(j)).start()

        @pl.when(pc.a > 0)
        def _():
            self.copy_down(s, self.own(j)).start()

    def hop(self, r, j=0):
        pc = self.pc

        @pl.when(pc.a - r >= 0)
        def _():
            s = (pc.a - r) * self.parts + j
            self.team.wait(s, pc.q)

            @pl.when(pc.a < pc.A - 1)
            def _():
                self.copy_up(s).start()

            self.team.landed(s)

        @pl.when(pc.a + r < pc.A)
        def _():
            s = (pc.a + r) * self.parts + j
            self.team.wait(s, pc.q)

            @pl.when(pc.a > 0)
            def _():
                self.copy_down(s).start()

            self.team.landed(s)

    def spread(self, r, j=0):
        pc = self.pc

        @pl.when(pc.a - r >= 0)
        def _():
            self.team.spread((pc.a - r) * self.parts + j)

        @pl.when(pc.a + r < pc.A)
        def _():
            self.team.spread((pc.a + r) * self.parts + j)

    def here(self, a0, j=0):
        self.team.here(a0 * self.parts + j)

    def finish(self):
        pc = self.pc
        for s in range(pc.A * self.parts):
            a0 = s // self.parts

            @pl.when((pc.a >= a0) & (pc.a < pc.A - 1))
            def _():
                self.copy_up(s).wait_send()

            @pl.when((pc.a <= a0) & (pc.a > 0))
            def _():
                self.copy_down(s).wait_send()

            @pl.when(pc.a != a0)
            def _():
                self.team.finish(s)


def line_weight_sems(n, parts):
    A, _ = plane(n)
    return team_sems(A * parts) + [DMA((A * parts,)), DMA((A * parts,))]


class SideWeights:
    def __init__(self, place, part, own, recv, far_send, core_send, side_send):
        self.pc, self.part3, self.own, self.recv, self.side_send = place, part, own, recv, side_send
        self.team = Team(place, lambda s, q: part(s // SIDE, s % SIDE, q), recv, far_send, core_send)

    def slots(self, i):
        return [self.pc.across(o) * SIDE + i for o in range(1, self.pc.B)]

    def copy(self, i, o):
        pc = self.pc
        return remote(self.own(i, pc.q), self.part3(pc.b, i, pc.q), self.side_send.at[o - 1, i],
                      self.recv.at[pc.b * SIDE + i, pc.q], pc.side(o))

    def start(self, i):
        for o in range(1, self.pc.B):
            self.copy(i, o).start()

    def hop(self, i):
        for s in self.slots(i):
            self.team.wait(s, self.pc.q)
            self.team.landed(s)

    def spread(self, i):
        for s in self.slots(i):
            self.team.spread(s)

    def here(self, i):
        for s in self.slots(i):
            self.team.here(s)

    def finish(self):
        for i in range(SIDE):
            for o in range(1, self.pc.B):
                self.copy(i, o).wait_send()
            for s in self.slots(i):
                self.team.finish(s)


def side_weight_sems(n):
    _, B = plane(n)
    return team_sems(B * SIDE) + [DMA((max(B - 1, 1), SIDE))]


class LineGather:
    def __init__(self, place, buf, recv, up, down):
        self.pc, self.buf, self.recv, self.up, self.down = place, buf, recv, up, down
        self.half = buf.shape[1] // HALVES

    def ref(self, a0, s):
        return self.buf.at[a0, pl.ds(s * self.half, self.half), :]

    def copy_up(self, a0, s):
        return remote(self.ref(a0, s), self.ref(a0, s), self.up.at[a0, s], self.recv.at[a0, s], self.pc.up())

    def copy_down(self, a0, s):
        return remote(self.ref(a0, s), self.ref(a0, s), self.down.at[a0, s], self.recv.at[a0, s], self.pc.down())

    def start(self, s):
        pc = self.pc

        @pl.when(pc.a < pc.A - 1)
        def _():
            self.copy_up(pc.a, s).start()

        @pl.when(pc.a > 0)
        def _():
            self.copy_down(pc.a, s).start()

    def hop(self, r):
        pc = self.pc
        for s in range(HALVES):

            @pl.when(pc.a - r >= 0)
            def _():
                self.copy_up(pc.a - r, s).wait_recv()

                @pl.when(pc.a < pc.A - 1)
                def _():
                    self.copy_up(pc.a - r, s).start()

            @pl.when(pc.a + r < pc.A)
            def _():
                self.copy_down(pc.a + r, s).wait_recv()

                @pl.when(pc.a > 0)
                def _():
                    self.copy_down(pc.a + r, s).start()

    def finish(self):
        pc = self.pc
        for a0 in range(pc.A):
            for s in range(HALVES):

                @pl.when((pc.a >= a0) & (pc.a < pc.A - 1))
                def _():
                    self.copy_up(a0, s).wait_send()

                @pl.when((pc.a <= a0) & (pc.a > 0))
                def _():
                    self.copy_down(a0, s).wait_send()


class LineReduce:
    def __init__(self, place, term, up_in, down_in, up_send, up_recv, down_send, down_recv):
        self.pc, self.term, self.up_in, self.down_in = place, term, up_in, down_in
        self.up_send, self.up_recv, self.down_send, self.down_recv = up_send, up_recv, down_send, down_recv
        self.rows = term.shape[1]
        self.wide = term.shape[2] // PIECES

    def copy_up(self, d, i):
        cols = span_of(i, self.wide)
        return remote(self.term.at[d, :, cols], self.up_in.at[d, :, cols], self.up_send.at[d, i],
                      self.up_recv.at[d, i], self.pc.up())

    def copy_down(self, d, i):
        cols = span_of(i, self.wide)
        return remote(self.term.at[d, :, cols], self.down_in.at[d, :, cols], self.down_send.at[d, i],
                      self.down_recv.at[d, i], self.pc.down())

    def add(self, d, i, arrived):
        cols = span_of(i, self.wide)

        def body(rows):
            total = self.term[d, rows, cols].astype(jnp.float32) + arrived[d, rows, cols].astype(jnp.float32)
            self.term[d, rows, cols] = total.astype(jnp.bfloat16)

        row_loop(0, self.rows, body)

    def pass_on(self, d, i):
        pc = self.pc

        @pl.when(d > pc.a)
        def _():
            @pl.when(pc.a > 0)
            def _():
                self.copy_up(d, i).wait_recv()
                self.add(d, i, self.up_in)

            self.copy_up(d, i).start()

        @pl.when(d < pc.a)
        def _():
            @pl.when(pc.a < pc.A - 1)
            def _():
                self.copy_down(d, i).wait_recv()
                self.add(d, i, self.down_in)

            self.copy_down(d, i).start()

    def result(self, i, use):
        pc = self.pc
        cols = span_of(i, self.wide)

        def go(terms):
            def body(rows):
                total = self.term[pc.a, rows, cols].astype(jnp.float32)
                for arrived in terms:
                    total = total + arrived[pc.a, rows, cols].astype(jnp.float32)
                use(rows, cols, total)

            row_loop(0, self.rows, body)

        @pl.when(pc.a == 0)
        def _():
            self.copy_down(pc.a, i).wait_recv()
            go([self.down_in])

        @pl.when(pc.a == pc.A - 1)
        def _():
            self.copy_up(pc.a, i).wait_recv()
            go([self.up_in])

        @pl.when((pc.a > 0) & (pc.a < pc.A - 1))
        def _():
            self.copy_up(pc.a, i).wait_recv()
            self.copy_down(pc.a, i).wait_recv()
            go([self.up_in, self.down_in])

    def finish(self):
        pc = self.pc
        for d in range(pc.A):
            for i in range(PIECES):

                @pl.when(pc.a < d)
                def _():
                    self.copy_up(d, i).wait_send()

                @pl.when(pc.a > d)
                def _():
                    self.copy_down(d, i).wait_send()


PLAN = (
    ("wq.start",), ("side.start", 0), ("ln1",), ("tok.start",), ("dp.start",), ("side.start", 1),
    ("side.start", 2), ("wo.start", 0), ("skv",), ("wq.hop", 1), ("dp.relay",), ("select",), ("keys.start",),
    ("wq.hop", 2), ("keys.round", 1), ("tok.wait",), ("proj", 0), ("wq.spread", 1), ("proj", 1), ("att", 0, 1),
    ("side.start", 3), ("wq.spread", 2), ("wq.hop", 3), ("side.hop", 0), ("side.hop", 1), ("att", 0, 0),
    ("side.hop", 2), ("proj", 2), ("att", 0, 2), ("att", 1, 2), ("keys.round", 2), ("wq.spread", 3),
    ("att", 1, 0), ("wo.hop", 0, 1), ("proj", 3), ("att", 0, 3), ("att", 1, 1), ("att", 1, 3),
    ("keys.round", 3), ("wo.start", 1), ("side.start", 4), ("side.hop", 3), ("att", 2, 0), ("att", 2, 3),
    ("att", 2, 1), ("side.spread", 1), ("wo.hop", 0, 2), ("wo.hop", 1, 1), ("att", 2, 2), ("side.start", 5),
    ("side.start", 6), ("side.start", 7), ("side.start", 8), ("side.spread", 3), ("att", 3, 1), ("att", 3, 3),
    ("suf", 3), ("wo.spread", 0, 2), ("wo.hop", 0, 3), ("wo.hop", 1, 2), ("wo.spread", 0, 1), ("att", 3, 0),
    ("suf", 1), ("wo.hop", 1, 3), ("suf", 0), ("att", 3, 2), ("out", 0, 0), ("out", 0, 1), ("wo.spread", 0, 3),
    ("suf", 2), ("out", 0, 2), ("out", 0, 3), ("rs.send", 0), ("side.hop", 4), ("fc.here", 3),
    ("wo.spread", 1, 1), ("out", 1, 0), ("side.hop", 5), ("out", 1, 1), ("side.hop", 6), ("wo.spread", 1, 3),
    ("wo.spread", 1, 2), ("out", 1, 2), ("out", 1, 3), ("side.spread", 0), ("rs.send", 1), ("rs.recv", 0),
    ("fc.here", 0), ("side.hop", 7), ("side.start", 9), ("side.spread", 2), ("rs.recv", 1), ("ln2", 0),
    ("fc.here", 2), ("ln2", 1), ("side.hop", 8), ("side.start", 10), ("side.start", 11), ("side.spread", 4),
    ("side.start", 12), ("side.hop", 9), ("side.hop", 10), ("side.hop", 11), ("side.start", 13),
    ("side.spread", 5), ("g.hop", 1), ("side.spread", 6), ("side.spread", 7), ("fc.here", 5),
    ("side.spread", 10), ("side.spread", 9), ("side.spread", 8), ("pr.here", 2), ("fc.here", 1), ("pr.here", 1),
    ("fc.here", 4), ("fc.here", 6), ("fc.here", 7), ("expand", 1), ("side.spread", 11), ("side.hop", 12),
    ("pr.here", 0), ("side.start", 14), ("side.start", 15), ("contract", 1, 0), ("pr.here", 3),
    ("side.hop", 13), ("contract", 1, 1), ("g.hop", 2), ("expand", 2), ("contract", 2, 0), ("side.spread", 12),
    ("side.hop", 14), ("contract", 2, 1), ("pr.here", 4), ("side.spread", 13), ("expand", 0), ("pr.here", 5),
    ("contract", 2, 2), ("contract", 0, 1), ("po", "m", 0), ("po", "m", 1), ("side.hop", 15),
    ("contract", 1, 2), ("po", "m", 2), ("g.hop", 3), ("expand", 3), ("contract", 3, 0), ("contract", 3, 1),
    ("po", "f", 0), ("side.spread", 15), ("side.spread", 14), ("contract", 3, 2), ("contract", 0, 0),
    ("pr.here", 6), ("pr.here", 7), ("po", "f", 1), ("contract", 3, 3), ("po", "n", 0), ("po", "f", 2),
    ("contract", 2, 3), ("po", "n", 1), ("po", "f", 3), ("contract", 1, 3), ("po", "n", 2), ("po", "m", 3),
    ("res", 0), ("contract", 0, 3), ("po", "n", 3), ("res", 1), ("contract", 0, 2), ("res", 2), ("res", 3),
)


def layer_kernel(n, ndp, heads, q_scale, hidden, gain1, gain2, prefix, owners, seg, w_keyval_hbm, w_query_hbm,
                 w_out_hbm, w_fc_hbm, w_proj_hbm, attended, layer_out, *scratch):
    pc = Place(n, ndp)
    A, B = pc.A, pc.B
    greet_signal(pc)
    scratch = list(scratch)

    def take(count):
        got = scratch[:count]
        del scratch[:count]
        return got

    wkv, wq, wout, wfc, wproj = take(5)
    normed, normed2, act, term, up_in, down_in = take(6)
    cached, from_dp, queries, top_ref, total_ref, weighted_ref, attn, out_sum, out_send, out_in, middle, bias = take(12)
    (load,) = take(1)
    tok_recv, tok_send, out_sem, out_recv = take(4)
    dp_recv, dp_send, dp_core = take(3)
    rows, width = hidden.shape
    slab = B * rows
    span = prefix.shape[1]
    row_len = n * rows
    head = wkv.shape[1] // 2
    units = w_fc_hbm.shape[1]
    half = rows // HALVES
    dp = pc.dp

    keys = Gather(pc, cached, *take(4))
    wq_line = LineWeights(pc, w_query_hbm, wq, 1, *take(5))
    wout_line = LineWeights(pc, w_out_hbm, wout, PARTS, *take(5))
    fc_rows, fc_part = width // TEAM, width // TEAM // SIDE
    pr_rows, pr_cols = units // TEAM, width // SIDE
    red_cols = width // PIECES
    part_cols = width // PARTS
    fc_side = SideWeights(
        pc,
        lambda s, i, q: wfc.at[s, pl.ds(pl.multiple_of(q * fc_rows + i * fc_part, fc_part), fc_part), :],
        lambda i, q: w_fc_hbm.at[pl.ds(pl.multiple_of(q * fc_rows + i * fc_part, fc_part), fc_part), :],
        *take(4))
    pr_side = SideWeights(
        pc,
        lambda s, i, q: wproj.at[pl.ds(pl.multiple_of(s * units + q * pr_rows, pr_rows), pr_rows), span_of(i, pr_cols)],
        lambda i, q: w_proj_hbm.at[span_of(q, pr_rows), span_of(i, pr_cols)],
        *take(4))
    gather = LineGather(pc, normed2, *take(3))
    reduce = LineReduce(pc, term, up_in, down_in, *take(4))

    def side(kind, j):
        getattr(fc_side if j < SIDE else pr_side, kind)(j % SIDE)

    loads = [
        pltpu.make_async_copy(w_keyval_hbm, wkv, load.at[0]),
        pltpu.make_async_copy(w_query_hbm, wq.at[pc.a], load.at[1]),
        pltpu.make_async_copy(w_out_hbm, wout.at[pc.a], load.at[2]),
        pltpu.make_async_copy(w_fc_hbm, wfc.at[pc.b], load.at[3]),
        pltpu.make_async_copy(w_proj_hbm, wproj.at[span_of(pc.b, units), :], load.at[4]),
    ]
    for copy in loads:
        copy.start()
    end = (pc.a == 0) | (pc.a == A - 1)
    low = pc.a < A // 2
    far_block = jnp.where(low, A - 1, 0)
    reduce_blocks = {"m": jnp.where(low, pc.a + 1, pc.a - 1), "f": far_block, "n": A - 1 - far_block}
    seen = set()

    def once(*key):
        if key in seen:
            return False
        seen.add(key)
        return True

    def dp_copy(o):
        return remote(prefix.at[0], from_dp.at[dp], dp_send.at[o - 1], dp_recv.at[dp], {"dp": pc.same_core(o)})

    def dp_to_core(o):
        src = pc.same_core(o)
        ref = prefix.at[0] if o == 0 else from_dp.at[src]
        return remote(ref, from_dp.at[src], dp_core.at[o], dp_recv.at[src], pc.core)

    def dp_arrived(src):
        remote(prefix.at[0], from_dp.at[src], dp_send.at[0], dp_recv.at[src], pc.core).wait_recv()

    def dp_start():
        for o in range(1, pc.pairs):
            dp_copy(o).start()
        dp_to_core(0).start()
        from_dp[dp] = prefix[0]

    def dp_relay():
        for o in range(1, pc.pairs):
            dp_arrived(pc.same_core(o))
            dp_to_core(o).start()

    def select():
        for o in range(pc.pairs):
            src = pc.same_core(o)
            dp_arrived(src + 1 - 2 * (src % 2))
        cached[pc.me, :span, :] = from_dp[owners[dp]]

    def norm_tokens():
        gains = gain1[...].astype(jnp.float32).reshape(1, width)

        def first(part):
            normed[pc.b, part, :] = norm_rows(hidden[part, :].astype(jnp.float32), gains)

        row_loop(0, rows, first)

    def tok_copy(o):
        return remote(normed.at[pc.b], normed.at[pc.b], tok_send.at[o - 1], tok_recv.at[pc.b], pc.side(o))

    def tok_start():
        for o in range(1, B):
            tok_copy(o).start()

    def tok_wait():
        for o in range(1, B):
            s = pc.across(o)
            remote(normed.at[s], normed.at[s], tok_send.at[0], tok_recv.at[s], pc.side(1)).wait_recv()

    def suffix_keys():
        loads[0].wait()
        cached[pc.me, span:, :] = jnp.dot(
            normed[pc.b], wkv[...], preferred_element_type=jnp.float32
        ).astype(jnp.bfloat16)
        spot = pc.a * slab + lax.broadcasted_iota(jnp.int32, (slab, row_len), 0)
        other = lax.broadcasted_iota(jnp.int32, (slab, row_len), 1)
        ids = seg[...].astype(jnp.float32)
        mine = jnp.sum(jnp.where(other == spot, ids, 0.0), axis=1, keepdims=True)
        bias[...] = jnp.where((other <= spot) & (mine == ids), 0.0, -jnp.inf)

    def project(k):
        if once("wq"):
            loads[1].wait()
        a0 = pc.near(k)
        if k > 0:
            wq_line.here(a0)
        left = normed[...].reshape(slab, width)
        out = (jnp.dot(left, wq[a0], preferred_element_type=jnp.float32) * q_scale).astype(jnp.bfloat16)
        for h in range(heads):
            queries[a0, h * slab : (h + 1) * slab, :] = out[:, h * head : (h + 1) * head]

    def fold(scores, values, a0, fresh):
        new_top = jnp.max(scores, axis=-1, keepdims=True)
        if not fresh:
            new_top = jnp.maximum(top_ref[a0], new_top)
        probs = jnp.exp(scores - new_top)
        total = jnp.sum(probs, axis=-1, keepdims=True)
        weighted = jnp.dot(probs.astype(jnp.bfloat16), values, preferred_element_type=jnp.float32)
        if not fresh:
            factor = jnp.exp(top_ref[a0] - new_top)
            total = total + total_ref[a0] * factor
            weighted = weighted + weighted_ref[a0] * factor
        return new_top, total, weighted

    def raw_scores(a0, keys_here):
        return lax.dot_general(queries[a0], keys_here, (((1,), (1,)), ((), ())),
                               preferred_element_type=jnp.float32)

    def over_prefix(k, h):
        e, a0 = pc.near(k), pc.near(h)
        if once("kv", k):
            keys.pair_arrived(e)
        pair = cached[pl.ds(e * B, B), :span, :].reshape(B * span, 2 * head)
        state = fold(raw_scores(a0, pair[:, :head]), pair[:, head:], a0, k == 0)
        top_ref[a0], total_ref[a0], weighted_ref[a0] = state

    def over_suffix(h):
        a0 = pc.near(h)
        fresh = cached[:, span:, :].reshape(row_len, 2 * head)
        scores = raw_scores(a0, fresh[:, :head]).reshape(heads, slab, row_len) + bias[...][None]
        _, total, weighted = fold(scores.reshape(heads * slab, row_len), fresh[:, head:], a0, False)
        out = (weighted / total).astype(jnp.bfloat16)
        for g in range(heads):
            attn[a0, :, g * head : (g + 1) * head] = out[g * slab : (g + 1) * slab]

    out_wide = min(512, part_cols)

    def out_part(j, k):
        if once("wout"):
            loads[2].wait()
        a0 = pc.near(k)
        if k > 0:
            wout_line.here(a0, j)

        def column(c, carry):
            cols = pl.ds(pl.multiple_of(j * part_cols + c * out_wide, out_wide), out_wide)
            out = jnp.dot(attn[a0], wout[a0, :, cols], preferred_element_type=jnp.float32)
            if k > 0:
                out = out + out_sum[:, cols]
            out_sum[:, cols] = out
            return carry

        lax.fori_loop(0, part_cols // out_wide, column, 0)

    def out_copy(o, j):
        cols = pl.ds(j * part_cols, part_cols)
        return remote(out_send.at[o - 1, :, cols], out_in.at[o - 1, :, cols], out_sem.at[o - 1, j],
                      out_recv.at[o - 1, j], pc.side(o))

    def out_give(j):
        cols = pl.ds(j * part_cols, part_cols)
        for o in range(1, B):
            base = pc.across(o) * rows

            def give(part):
                spot = pl.ds(pl.multiple_of(base + part.start, ROWS), ROWS)
                out_send[o - 1, part, cols] = out_sum[spot, cols].astype(jnp.bfloat16)

            row_loop(0, rows, give)
            out_copy(o, j).start()

    def out_take(j):
        cols = pl.ds(j * part_cols, part_cols)
        for o in range(1, B):
            out_copy(o, j).wait_recv()

        def body(part):
            total = out_sum[pl.ds(pl.multiple_of(pc.b * rows + part.start, ROWS), ROWS), cols]
            for o in range(1, B):
                total = total + out_in[o - 1, part, cols].astype(jnp.float32)
            out = total.astype(jnp.bfloat16)
            attended[part, cols] = out
            middle[part, cols] = (hidden[part, cols].astype(jnp.float32) + out.astype(jnp.float32)).astype(jnp.bfloat16)

        row_loop(0, rows, body)

    def norm_middle(s):
        gains = gain2[...].astype(jnp.float32).reshape(1, width)

        def second(part):
            normed2[pc.a, part, :] = norm_rows(middle[part, :].astype(jnp.float32), gains)

        row_loop(s * half, half, second)
        gather.start(s)

    act_wide = min(256, units)

    def expand(k):
        e = pc.near(k)
        if once("wfc"):
            loads[3].wait()
        for s in range(B):

            def column(c, carry):
                cols = span_of(c, act_wide)
                out = jnp.dot(normed2[e], wfc[s, :, cols], preferred_element_type=jnp.float32)
                spot = pl.ds(pl.multiple_of(s * units + c * act_wide, act_wide), act_wide)
                act[span_of(e, rows), spot] = jax.nn.gelu(out, approximate=True).astype(jnp.bfloat16)
                return carry

            lax.fori_loop(0, units // act_wide, column, 0)

    def contract(k, i):
        e = pc.near(k)
        if once("wproj"):
            loads[4].wait()
        cols = pl.ds(i * red_cols, red_cols)
        out = jnp.dot(act[span_of(e, rows), :], wproj[:, cols], preferred_element_type=jnp.float32)
        term[e, :, cols] = out.astype(jnp.bfloat16)
        if k > 0:

            @pl.when(end)
            def _():
                reduce.pass_on(e, i)

    def pass_on(which, i):
        @pl.when(jnp.logical_not(end))
        def _():
            reduce.pass_on(reduce_blocks[which], i)

    def last(part, cols, total):
        layer_out[part, cols] = (middle[part, cols].astype(jnp.float32) + total).astype(jnp.bfloat16)

    steps = {
        "wq.start": wq_line.start,
        "wq.hop": wq_line.hop,
        "wq.spread": wq_line.spread,
        "wo.start": wout_line.start,
        "wo.hop": lambda j, r: wout_line.hop(r, j),
        "wo.spread": lambda j, r: wout_line.spread(r, j),
        "dp.start": dp_start,
        "dp.relay": dp_relay,
        "select": select,
        "keys.start": keys.start,
        "keys.round": keys.round,
        "ln1": norm_tokens,
        "tok.start": tok_start,
        "tok.wait": tok_wait,
        "skv": suffix_keys,
        "proj": project,
        "att": over_prefix,
        "suf": over_suffix,
        "out": out_part,
        "rs.send": out_give,
        "rs.recv": out_take,
        "ln2": norm_middle,
        "side.start": lambda j: side("start", j),
        "side.hop": lambda j: side("hop", j),
        "side.spread": lambda j: side("spread", j),
        "fc.here": fc_side.here,
        "pr.here": pr_side.here,
        "g.hop": gather.hop,
        "expand": expand,
        "contract": contract,
        "po": pass_on,
        "res": lambda i: reduce.result(i, last),
    }
    greet_wait(pc)
    for name, *numbers in PLAN:
        steps[name](*numbers)
    for o in range(1, pc.pairs):
        dp_copy(o).wait_send()
    for o in range(pc.pairs):
        dp_to_core(o).wait_send()
    for o in range(1, B):
        tok_copy(o).wait_send()
        for j in range(PARTS):
            out_copy(o, j).wait_send()
    keys.finish()
    wq_line.finish()
    wout_line.finish()
    fc_side.finish()
    pr_side.finish()
    gather.finish()
    reduce.finish()


def hand_on(attended, layer_out, attended_to, layer_to):
    attended_to[...] = attended[...]
    layer_to[...] = layer_out[...]


VM = pl.BlockSpec(memory_space=pltpu.VMEM)


def local(n, ndp, hidden_in, norm1_gain, norm2_gain, w_query, w_keyval, w_out, w_fc, w_proj,
          prefix_kv, owner_ids, segment_ids):
    A, B = plane(n)
    rows, width = hidden_in.shape
    head = w_keyval.shape[1] // 2
    query_cols = w_query.shape[1]
    heads = query_cols // head
    span = prefix_kv.shape[1]
    units = w_fc.shape[1]
    q_scale = 1.0 / math.sqrt(head)
    bf, f32 = jnp.bfloat16, jnp.float32
    any_space = pl.BlockSpec(memory_space=pl.ANY)
    own = jax.ShapeDtypeStruct((rows, width), bf)
    V = pltpu.VMEM
    stack = heads * B * rows
    line = V((A, rows, width), bf)
    sides = max(B - 1, 1)
    scratch = [
        V(w_keyval.shape, bf), V((A,) + w_query.shape, bf), V((A,) + w_out.shape, bf),
        V((B,) + w_fc.shape, bf), V((B * units, width), bf),
        V((B, rows, width), bf), line, V((A * rows, B * units), bf), line, line, line,
        V((n, span + rows, 2 * head), bf), V((ndp, span, 2 * head), bf), V((A, stack, head), bf),
        V((A, stack, 1), f32), V((A, stack, 1), f32), V((A, stack, head), f32),
        V((A, B * rows, query_cols), bf), V((B * rows, width), f32),
        V((sides, rows, width), bf), V((sides, rows, width), bf), V((rows, width), bf),
        V((B * rows, n * rows), f32), DMA((5,)),
        DMA((B,)), DMA((sides,)), DMA((sides, PARTS)), DMA((sides, PARTS)),
        DMA((ndp,)), DMA((max(ndp // 2 - 1, 1),)), DMA((ndp // 2,)),
    ]
    scratch += gather_sems(n) + line_weight_sems(n, 1) + line_weight_sems(n, PARTS) + side_weight_sems(n) * 2
    scratch += [DMA((A, HALVES))] * 3 + [DMA((A, PIECES))] * 4
    attended, layer_out = pl.pallas_call(
        functools.partial(layer_kernel, n, ndp, heads, q_scale),
        out_shape=(own, own),
        in_specs=[VM] * 4 + [pl.BlockSpec(memory_space=pltpu.SMEM), VM] + [any_space] * 5,
        out_specs=(VM, VM),
        scratch_shapes=scratch,
        compiler_params=pltpu.CompilerParams(collective_id=1, has_side_effects=True, vmem_limit_bytes=62 << 20),
        name="layer",
    )(hidden_in, norm1_gain, norm2_gain, prefix_kv, owner_ids, segment_ids, w_keyval, w_query, w_out,
      w_fc, w_proj)
    attended, layer_out = pl.pallas_call(
        hand_on, out_shape=(own, own), in_specs=[VM] * 2, out_specs=(VM, VM), name="hand_on",
    )(attended, layer_out)
    return (layer_out, attended)


def solution(mesh):
    return jax.shard_map(
        functools.partial(local, mesh.shape["tensor"], mesh.shape["dp"]),
        mesh=mesh,
        in_specs=(
            P(("dp", "tensor"), None),
            P(),
            P(),
            P(None, "tensor"),
            P(),
            P("tensor", None),
            P(None, "tensor"),
            P("tensor", None),
            P("dp", "tensor", None),
            P(),
            P("dp", None),
        ),
        out_specs=(P(("dp", "tensor"), None), P(("dp", "tensor"), None)),
        check_vma=False,
    )
```

```python
import functools
import math

import jax
import jax.numpy as jnp
from jax import lax
from jax.experimental import pallas as pl
from jax.experimental.pallas import tpu as pltpu
from jax.sharding import PartitionSpec as P

MESH = pl.DeviceIdType.MESH
ROWS = 16
PIECES = 4
SIDE = 8
PARTS = 2
HALVES = 2
TEAM = 4


def plane(n):
    lines = 4 if n % 4 == 0 else n
    return lines, n // lines


def norm_rows(widened, gains):
    centre = jnp.mean(widened, axis=-1, keepdims=True)
    centred = widened - centre
    variance = jnp.mean(centred * centred, axis=-1, keepdims=True)
    return (centred * lax.rsqrt(variance + 1e-05) * gains).astype(jnp.bfloat16)


def row_loop(start, rows, body):
    def step(i, carry):
        body(pl.ds(pl.multiple_of(start + i * ROWS, ROWS), ROWS))
        return carry

    lax.fori_loop(0, rows // ROWS, step, 0)


def span_of(i, size):
    return pl.ds(pl.multiple_of(i * size, size), size)


class Place:
    def __init__(self, n, ndp):
        self.n, self.ndp = n, ndp
        self.A, self.B = plane(n)
        self.me = lax.axis_index("tensor")
        self.a = self.me // self.B
        self.b = self.me % self.B
        self.dp = lax.axis_index("dp")
        self.pairs = ndp // 2
        self.q = self.dp % TEAM
        base = self.dp - self.q
        self.q_core = self.q + 1 - 2 * (self.q % 2)
        self.q_far = (self.q + 2) % TEAM
        self.q_diag = (self.q_core + 2) % TEAM
        self.core = {"dp": base + self.q_core}
        self.across_dp = {"dp": base + self.q_far}

    def across(self, o):
        return (self.b + o) % self.B

    def peer(self, a, b):
        return {"tensor": a * self.B + b}

    def side(self, o):
        return self.peer(self.a, self.across(o))

    def up(self):
        return self.peer(jnp.minimum(self.a + 1, self.A - 1), self.b)

    def down(self):
        return self.peer(jnp.maximum(self.a - 1, 0), self.b)

    def same_core(self, o):
        return ((self.dp // 2 + o) % self.pairs) * 2 + self.dp % 2

    def choose(self, k, key):
        found = 0
        for a in range(self.A):
            order = sorted(range(self.A), key=lambda d: key(a, d))
            for i, d in enumerate(order):
                found = found + jnp.where((self.a == a) & (k == i), d, 0)
        return found

    def near(self, k):
        return self.choose(k, lambda a, d: (abs(d - a), d))

    def far(self, k):
        return self.choose(k, lambda a, d: (-abs(d - a), d))


def greet_signal(pc):
    barrier = pltpu.get_barrier_semaphore()

    def signal(device):
        pl.semaphore_signal(barrier, inc=1, device_id=device, device_id_type=MESH)

    @pl.when(pc.a > 0)
    def _():
        signal(pc.peer(pc.a - 1, pc.b))

    @pl.when(pc.a < pc.A - 1)
    def _():
        signal(pc.peer(pc.a + 1, pc.b))

    for o in range(1, pc.B):
        signal(pc.side(o))
    for o in range(1, pc.pairs):
        signal({"dp": pc.same_core(o)})
    signal(pc.core)


def greet_wait(pc):
    ends = jnp.where((pc.a == 0) | (pc.a == pc.A - 1), 1, 2)
    pl.semaphore_wait(pltpu.get_barrier_semaphore(), pc.B - 1 + pc.pairs + ends)


def remote(src, dst, send, recv, device):
    return pltpu.make_async_remote_copy(
        src_ref=src, dst_ref=dst, send_sem=send, recv_sem=recv, device_id=device, device_id_type=MESH
    )


class Gather:
    def __init__(self, place, buf, recv, up, down, side):
        self.pc, self.buf, self.recv, self.up, self.down, self.side = place, buf, recv, up, down, side

    def copy_up(self, a0):
        blk = a0 * self.pc.B + self.pc.b
        return remote(self.buf.at[blk], self.buf.at[blk], self.up.at[a0], self.recv.at[blk], self.pc.up())

    def copy_down(self, a0):
        blk = a0 * self.pc.B + self.pc.b
        return remote(self.buf.at[blk], self.buf.at[blk], self.down.at[a0], self.recv.at[blk], self.pc.down())

    def copy_side(self, a0, o):
        blk = a0 * self.pc.B + self.pc.b
        return remote(self.buf.at[blk], self.buf.at[blk], self.side.at[a0, o - 1], self.recv.at[blk],
                      self.pc.side(o))

    def arrived(self, blk):
        remote(self.buf.at[blk], self.buf.at[blk], self.up.at[0], self.recv.at[blk],
               self.pc.side(1)).wait_recv()

    def start(self):
        pc = self.pc

        @pl.when(pc.a < pc.A - 1)
        def _():
            self.copy_up(pc.a).start()

        @pl.when(pc.a > 0)
        def _():
            self.copy_down(pc.a).start()

        for o in range(1, pc.B):
            self.copy_side(pc.a, o).start()

    def round(self, r):
        pc = self.pc

        @pl.when(pc.a - r >= 0)
        def _():
            a0 = pc.a - r
            self.arrived(a0 * pc.B + pc.b)

            @pl.when(pc.a < pc.A - 1)
            def _():
                self.copy_up(a0).start()

            for o in range(1, pc.B):
                self.copy_side(a0, o).start()

        @pl.when(pc.a + r < pc.A)
        def _():
            a0 = pc.a + r
            self.arrived(a0 * pc.B + pc.b)

            @pl.when(pc.a > 0)
            def _():
                self.copy_down(a0).start()

            for o in range(1, pc.B):
                self.copy_side(a0, o).start()

    def pair_arrived(self, a0):
        for o in range(1, self.pc.B):
            self.arrived(a0 * self.pc.B + self.pc.across(o))

    def finish(self):
        pc = self.pc
        for a0 in range(pc.A):
            for o in range(1, pc.B):
                self.copy_side(a0, o).wait_send()

            @pl.when((pc.a >= a0) & (pc.a < pc.A - 1))
            def _():
                self.copy_up(a0).wait_send()

            @pl.when((pc.a <= a0) & (pc.a > 0))
            def _():
                self.copy_down(a0).wait_send()


DMA = pltpu.SemaphoreType.DMA


def gather_sems(n):
    A, B = plane(n)
    return [DMA((n,)), DMA((A,)), DMA((A,)), DMA((A, max(B - 1, 1)))]


class Team:
    def __init__(self, place, part, recv, far_send, core_send):
        self.pc, self.part, self.recv, self.far_send, self.core_send = place, part, recv, far_send, core_send

    def far_copy(self, s):
        pc = self.pc
        ref = self.part(s, pc.q)
        return remote(ref, ref, self.far_send.at[s], self.recv.at[s, pc.q], pc.across_dp)

    def core_copy(self, s, which):
        pc = self.pc
        q = pc.q_far if which else pc.q
        ref = self.part(s, q)
        return remote(ref, ref, self.core_send.at[s, which], self.recv.at[s, q], pc.core)

    def wait(self, s, q):
        ref = self.part(s, q)
        remote(ref, ref, self.far_send.at[s], self.recv.at[s, q], self.pc.core).wait_recv()

    def landed(self, s):
        self.far_copy(s).start()
        self.core_copy(s, 0).start()

    def spread(self, s):
        self.wait(s, self.pc.q_far)
        self.core_copy(s, 1).start()

    def here(self, s):
        self.wait(s, self.pc.q_core)
        self.wait(s, self.pc.q_diag)

    def finish(self, s):
        self.far_copy(s).wait_send()
        self.core_copy(s, 0).wait_send()
        self.core_copy(s, 1).wait_send()


def team_sems(slots):
    return [DMA((slots, TEAM)), DMA((slots,)), DMA((slots, 2))]


class LineWeights:
    def __init__(self, place, hbm, buf, parts, recv, far_send, core_send, up, down):
        self.pc, self.hbm, self.up, self.down, self.recv, self.parts = place, hbm, up, down, recv, parts
        quarter = buf.shape[1] // TEAM
        cols = buf.shape[2] // parts
        self.part = lambda s, q: buf.at[s // parts, span_of(q, quarter), span_of(s % parts, cols)]
        self.own = lambda j: hbm.at[span_of(place.q, quarter), pl.ds(j * cols, cols)]
        self.team = Team(place, self.part, recv, far_send, core_send)

    def copy_up(self, s, src=None):
        pc = self.pc
        ref = self.part(s, pc.q)
        return remote(ref if src is None else src, ref, self.up.at[s], self.recv.at[s, pc.q], pc.up())

    def copy_down(self, s, src=None):
        pc = self.pc
        ref = self.part(s, pc.q)
        return remote(ref if src is None else src, ref, self.down.at[s], self.recv.at[s, pc.q], pc.down())

    def start(self, j=0):
        pc = self.pc
        s = pc.a * self.parts + j

        @pl.when(pc.a < pc.A - 1)
        def _():
            self.copy_up(s, self.own(j)).start()

        @pl.when(pc.a > 0)
        def _():
            self.copy_down(s, self.own(j)).start()

    def hop(self, r, j=0):
        pc = self.pc

        @pl.when(pc.a - r >= 0)
        def _():
            s = (pc.a - r) * self.parts + j
            self.team.wait(s, pc.q)

            @pl.when(pc.a < pc.A - 1)
            def _():
                self.copy_up(s).start()

            self.team.landed(s)

        @pl.when(pc.a + r < pc.A)
        def _():
            s = (pc.a + r) * self.parts + j
            self.team.wait(s, pc.q)

            @pl.when(pc.a > 0)
            def _():
                self.copy_down(s).start()

            self.team.landed(s)

    def spread(self, r, j=0):
        pc = self.pc

        @pl.when(pc.a - r >= 0)
        def _():
            self.team.spread((pc.a - r) * self.parts + j)

        @pl.when(pc.a + r < pc.A)
        def _():
            self.team.spread((pc.a + r) * self.parts + j)

    def here(self, a0, j=0):
        self.team.here(a0 * self.parts + j)

    def finish(self):
        pc = self.pc
        for s in range(pc.A * self.parts):
            a0 = s // self.parts

            @pl.when((pc.a >= a0) & (pc.a < pc.A - 1))
            def _():
                self.copy_up(s).wait_send()

            @pl.when((pc.a <= a0) & (pc.a > 0))
            def _():
                self.copy_down(s).wait_send()

            @pl.when(pc.a != a0)
            def _():
                self.team.finish(s)


def line_weight_sems(n, parts):
    A, _ = plane(n)
    return team_sems(A * parts) + [DMA((A * parts,)), DMA((A * parts,))]


class SideWeights:
    def __init__(self, place, part, own, recv, far_send, core_send, side_send):
        self.pc, self.part3, self.own, self.recv, self.side_send = place, part, own, recv, side_send
        self.team = Team(place, lambda s, q: part(s // SIDE, s % SIDE, q), recv, far_send, core_send)

    def slots(self, i):
        return [self.pc.across(o) * SIDE + i for o in range(1, self.pc.B)]

    def copy(self, i, o):
        pc = self.pc
        return remote(self.own(i, pc.q), self.part3(pc.b, i, pc.q), self.side_send.at[o - 1, i],
                      self.recv.at[pc.b * SIDE + i, pc.q], pc.side(o))

    def start(self, i):
        for o in range(1, self.pc.B):
            self.copy(i, o).start()

    def hop(self, i):
        for s in self.slots(i):
            self.team.wait(s, self.pc.q)
            self.team.landed(s)

    def spread(self, i):
        for s in self.slots(i):
            self.team.spread(s)

    def here(self, i):
        for s in self.slots(i):
            self.team.here(s)

    def finish(self):
        for i in range(SIDE):
            for o in range(1, self.pc.B):
                self.copy(i, o).wait_send()
            for s in self.slots(i):
                self.team.finish(s)


def side_weight_sems(n):
    _, B = plane(n)
    return team_sems(B * SIDE) + [DMA((max(B - 1, 1), SIDE))]


class LineGather:
    def __init__(self, place, buf, recv, up, down):
        self.pc, self.buf, self.recv, self.up, self.down = place, buf, recv, up, down
        self.half = buf.shape[1] // HALVES

    def ref(self, a0, s):
        return self.buf.at[a0, pl.ds(s * self.half, self.half), :]

    def copy_up(self, a0, s):
        return remote(self.ref(a0, s), self.ref(a0, s), self.up.at[a0, s], self.recv.at[a0, s], self.pc.up())

    def copy_down(self, a0, s):
        return remote(self.ref(a0, s), self.ref(a0, s), self.down.at[a0, s], self.recv.at[a0, s], self.pc.down())

    def start(self, s):
        pc = self.pc

        @pl.when(pc.a < pc.A - 1)
        def _():
            self.copy_up(pc.a, s).start()

        @pl.when(pc.a > 0)
        def _():
            self.copy_down(pc.a, s).start()

    def hop(self, r):
        pc = self.pc
        for s in range(HALVES):

            @pl.when(pc.a - r >= 0)
            def _():
                self.copy_up(pc.a - r, s).wait_recv()

                @pl.when(pc.a < pc.A - 1)
                def _():
                    self.copy_up(pc.a - r, s).start()

            @pl.when(pc.a + r < pc.A)
            def _():
                self.copy_down(pc.a + r, s).wait_recv()

                @pl.when(pc.a > 0)
                def _():
                    self.copy_down(pc.a + r, s).start()

    def finish(self):
        pc = self.pc
        for a0 in range(pc.A):
            for s in range(HALVES):

                @pl.when((pc.a >= a0) & (pc.a < pc.A - 1))
                def _():
                    self.copy_up(a0, s).wait_send()

                @pl.when((pc.a <= a0) & (pc.a > 0))
                def _():
                    self.copy_down(a0, s).wait_send()


class LineReduce:
    def __init__(self, place, term, up_in, down_in, up_send, up_recv, down_send, down_recv):
        self.pc, self.term, self.up_in, self.down_in = place, term, up_in, down_in
        self.up_send, self.up_recv, self.down_send, self.down_recv = up_send, up_recv, down_send, down_recv
        self.rows = term.shape[1]
        self.wide = term.shape[2] // PIECES

    def copy_up(self, d, i):
        cols = span_of(i, self.wide)
        return remote(self.term.at[d, :, cols], self.up_in.at[d, :, cols], self.up_send.at[d, i],
                      self.up_recv.at[d, i], self.pc.up())

    def copy_down(self, d, i):
        cols = span_of(i, self.wide)
        return remote(self.term.at[d, :, cols], self.down_in.at[d, :, cols], self.down_send.at[d, i],
                      self.down_recv.at[d, i], self.pc.down())

    def add(self, d, i, arrived):
        cols = span_of(i, self.wide)

        def body(rows):
            total = self.term[d, rows, cols].astype(jnp.float32) + arrived[d, rows, cols].astype(jnp.float32)
            self.term[d, rows, cols] = total.astype(jnp.bfloat16)

        row_loop(0, self.rows, body)

    def pass_on(self, d, i):
        pc = self.pc

        @pl.when(d > pc.a)
        def _():
            @pl.when(pc.a > 0)
            def _():
                self.copy_up(d, i).wait_recv()
                self.add(d, i, self.up_in)

            self.copy_up(d, i).start()

        @pl.when(d < pc.a)
        def _():
            @pl.when(pc.a < pc.A - 1)
            def _():
                self.copy_down(d, i).wait_recv()
                self.add(d, i, self.down_in)

            self.copy_down(d, i).start()

    def result(self, i, use):
        pc = self.pc
        cols = span_of(i, self.wide)

        def go(terms):
            def body(rows):
                total = self.term[pc.a, rows, cols].astype(jnp.float32)
                for arrived in terms:
                    total = total + arrived[pc.a, rows, cols].astype(jnp.float32)
                use(rows, cols, total)

            row_loop(0, self.rows, body)

        @pl.when(pc.a == 0)
        def _():
            self.copy_down(pc.a, i).wait_recv()
            go([self.down_in])

        @pl.when(pc.a == pc.A - 1)
        def _():
            self.copy_up(pc.a, i).wait_recv()
            go([self.up_in])

        @pl.when((pc.a > 0) & (pc.a < pc.A - 1))
        def _():
            self.copy_up(pc.a, i).wait_recv()
            self.copy_down(pc.a, i).wait_recv()
            go([self.up_in, self.down_in])

    def finish(self):
        pc = self.pc
        for d in range(pc.A):
            for i in range(PIECES):

                @pl.when(pc.a < d)
                def _():
                    self.copy_up(d, i).wait_send()

                @pl.when(pc.a > d)
                def _():
                    self.copy_down(d, i).wait_send()


PLAN = (
    ("wq.start",), ("side.start", 0), ("side.start", 1), ("side.start", 2), ("dp.start",), ("side.start", 3),
    ("ln1",), ("wo.start", 0), ("wq.hop", 1), ("dp.relay",), ("skv",), ("side.hop", 0), ("select",),
    ("keys.start",), ("tok.start",), ("wq.hop", 2), ("keys.round", 1), ("wq.hop", 3), ("tok.wait",),
    ("wq.spread", 1), ("side.hop", 1), ("proj", 0), ("att", 0, 0), ("wq.spread", 2), ("proj", 2), ("att", 0, 2),
    ("proj", 1), ("keys.round", 2), ("wo.start", 1), ("side.hop", 2), ("wq.spread", 3), ("side.hop", 3),
    ("proj", 3), ("att", 0, 1), ("att", 1, 0), ("att", 0, 3), ("att", 1, 3), ("keys.round", 3), ("att", 1, 1),
    ("side.start", 4), ("att", 1, 2), ("side.start", 5), ("wo.hop", 1, 1), ("att", 2, 3), ("wo.hop", 0, 1),
    ("side.spread", 2), ("side.start", 6), ("att", 2, 1), ("side.spread", 1), ("att", 2, 0),
    ("wo.spread", 1, 1), ("wo.hop", 1, 2), ("att", 2, 2), ("att", 3, 2), ("att", 3, 0), ("suf", 0),
    ("wo.hop", 1, 3), ("out", 1, 0), ("wo.hop", 0, 2), ("att", 3, 1), ("suf", 1), ("side.start", 7),
    ("att", 3, 3), ("suf", 3), ("side.spread", 0), ("out", 1, 1), ("wo.hop", 0, 3), ("wo.spread", 1, 3),
    ("wo.spread", 1, 2), ("suf", 2), ("out", 1, 2), ("out", 1, 3), ("rs.send", 1), ("out", 0, 0),
    ("wo.spread", 0, 1), ("side.hop", 4), ("side.hop", 5), ("fc.here", 0), ("wo.spread", 0, 2), ("out", 0, 1),
    ("out", 0, 2), ("wo.spread", 0, 3), ("out", 0, 3), ("rs.send", 0), ("side.hop", 6), ("fc.here", 2),
    ("fin.wo",), ("side.hop", 7), ("side.spread", 5), ("side.start", 8), ("side.spread", 3), ("side.start", 9),
    ("rs.recv", 1), ("rs.recv", 0), ("ln2", 0), ("ln2", 1), ("side.spread", 4), ("side.start", 10),
    ("fin.keys",), ("fin.misc",), ("side.hop", 8), ("side.start", 11), ("fc.here", 4), ("side.hop", 9),
    ("side.hop", 10), ("side.start", 12), ("side.start", 13), ("side.spread", 6), ("fin.wq",), ("fc.here", 3),
    ("side.spread", 8), ("fc.here", 1), ("side.spread", 7), ("g.hop", 1), ("fc.here", 5), ("fc.here", 7),
    ("side.spread", 9), ("side.spread", 10), ("side.start", 14), ("side.hop", 11), ("pr.here", 0),
    ("fc.here", 6), ("expand", 1), ("side.start", 15), ("side.hop", 12), ("pr.here", 1), ("contract", 1, 0),
    ("g.hop", 2), ("side.spread", 11), ("pr.here", 2), ("pr.here", 3), ("contract", 1, 1), ("side.hop", 13),
    ("expand", 2), ("contract", 2, 1), ("side.spread", 12), ("side.hop", 14), ("side.hop", 15),
    ("side.spread", 13), ("contract", 2, 0), ("pr.here", 4), ("pr.here", 5), ("contract", 2, 2), ("g.hop", 3),
    ("expand", 3), ("contract", 3, 1), ("po", "m", 1), ("po", "m", 0), ("contract", 3, 0), ("side.spread", 14),
    ("expand", 0), ("pr.here", 6), ("side.spread", 15), ("contract", 3, 2), ("po", "f", 1), ("po", "f", 0),
    ("contract", 0, 0), ("contract", 0, 2), ("po", "n", 1), ("po", "f", 2), ("pr.here", 7), ("contract", 3, 3),
    ("contract", 0, 1), ("contract", 2, 3), ("po", "n", 0), ("po", "f", 3), ("res", 1), ("contract", 1, 2),
    ("po", "m", 2), ("po", "n", 2), ("contract", 1, 3), ("po", "m", 3), ("po", "n", 3), ("res", 0),
    ("fin.side",), ("contract", 0, 3), ("fin.r",), ("res", 2), ("fin.g",), ("res", 3),
)


def layer_kernel(n, ndp, heads, q_scale, hidden, gain1, gain2, prefix, owners, seg, w_keyval_hbm, w_query_hbm,
                 w_out_hbm, w_fc_hbm, w_proj_hbm, attended, layer_out, *scratch):
    pc = Place(n, ndp)
    A, B = pc.A, pc.B
    greet_signal(pc)
    scratch = list(scratch)

    def take(count):
        got = scratch[:count]
        del scratch[:count]
        return got

    wkv, wq, wout, wfc, wproj = take(5)
    normed, normed2, act, term, up_in, down_in = take(6)
    cached, from_dp, queries, top_ref, total_ref, weighted_ref, attn, out_sum, out_send, out_in, middle, bias = take(12)
    (load,) = take(1)
    tok_recv, tok_send, out_sem, out_recv = take(4)
    dp_recv, dp_send, dp_core = take(3)
    rows, width = hidden.shape
    slab = B * rows
    span = prefix.shape[1]
    row_len = n * rows
    head = wkv.shape[1] // 2
    units = w_fc_hbm.shape[1]
    half = rows // HALVES
    dp = pc.dp

    keys = Gather(pc, cached, *take(4))
    wq_line = LineWeights(pc, w_query_hbm, wq, 1, *take(5))
    wout_line = LineWeights(pc, w_out_hbm, wout, PARTS, *take(5))
    fc_rows, fc_part = width // TEAM, width // TEAM // SIDE
    pr_rows, pr_cols = units // TEAM, width // SIDE
    red_cols = width // PIECES
    part_cols = width // PARTS
    fc_side = SideWeights(
        pc,
        lambda s, i, q: wfc.at[s, pl.ds(pl.multiple_of(q * fc_rows + i * fc_part, fc_part), fc_part), :],
        lambda i, q: w_fc_hbm.at[pl.ds(pl.multiple_of(q * fc_rows + i * fc_part, fc_part), fc_part), :],
        *take(4))
    pr_side = SideWeights(
        pc,
        lambda s, i, q: wproj.at[pl.ds(pl.multiple_of(s * units + q * pr_rows, pr_rows), pr_rows), span_of(i, pr_cols)],
        lambda i, q: w_proj_hbm.at[span_of(q, pr_rows), span_of(i, pr_cols)],
        *take(4))
    gather = LineGather(pc, normed2, *take(3))
    reduce = LineReduce(pc, term, up_in, down_in, *take(4))

    def side(kind, j):
        getattr(fc_side if j < SIDE else pr_side, kind)(j % SIDE)

    loads = [
        pltpu.make_async_copy(w_keyval_hbm, wkv, load.at[0]),
        pltpu.make_async_copy(w_query_hbm, wq.at[pc.a], load.at[1]),
        pltpu.make_async_copy(w_out_hbm, wout.at[pc.a], load.at[2]),
        pltpu.make_async_copy(w_fc_hbm, wfc.at[pc.b], load.at[3]),
        pltpu.make_async_copy(w_proj_hbm, wproj.at[span_of(pc.b, units), :], load.at[4]),
    ]
    for copy in loads[:2]:
        copy.start()
    end = (pc.a == 0) | (pc.a == A - 1)
    low = pc.a < A // 2
    far_block = jnp.where(low, A - 1, 0)
    reduce_blocks = {"m": jnp.where(low, pc.a + 1, pc.a - 1), "f": far_block, "n": A - 1 - far_block}
    seen = set()

    def once(*key):
        if key in seen:
            return False
        seen.add(key)
        return True

    def dp_copy(o):
        return remote(prefix.at[0], from_dp.at[dp], dp_send.at[o - 1], dp_recv.at[dp], {"dp": pc.same_core(o)})

    def dp_to_core(o):
        src = pc.same_core(o)
        ref = prefix.at[0] if o == 0 else from_dp.at[src]
        return remote(ref, from_dp.at[src], dp_core.at[o], dp_recv.at[src], pc.core)

    def dp_arrived(src):
        remote(prefix.at[0], from_dp.at[src], dp_send.at[0], dp_recv.at[src], pc.core).wait_recv()

    def dp_start():
        for o in range(1, pc.pairs):
            dp_copy(o).start()
        dp_to_core(0).start()
        from_dp[dp] = prefix[0]

    def dp_relay():
        for o in range(1, pc.pairs):
            dp_arrived(pc.same_core(o))
            dp_to_core(o).start()

    def select():
        for o in range(pc.pairs):
            src = pc.same_core(o)
            dp_arrived(src + 1 - 2 * (src % 2))
        cached[pc.me, :span, :] = from_dp[owners[dp]]

    def norm_tokens():
        gains = gain1[...].astype(jnp.float32).reshape(1, width)

        def first(part):
            normed[pc.b, part, :] = norm_rows(hidden[part, :].astype(jnp.float32), gains)

        row_loop(0, rows, first)

    def tok_copy(o):
        return remote(normed.at[pc.b], normed.at[pc.b], tok_send.at[o - 1], tok_recv.at[pc.b], pc.side(o))

    def tok_start():
        for copy in loads[2:]:
            copy.start()
        for o in range(1, B):
            tok_copy(o).start()

    def tok_wait():
        for o in range(1, B):
            s = pc.across(o)
            remote(normed.at[s], normed.at[s], tok_send.at[0], tok_recv.at[s], pc.side(1)).wait_recv()

    def suffix_keys():
        loads[0].wait()
        cached[pc.me, span:, :] = jnp.dot(
            normed[pc.b], wkv[...], preferred_element_type=jnp.float32
        ).astype(jnp.bfloat16)
        spot = pc.a * slab + lax.broadcasted_iota(jnp.int32, (slab, row_len), 0)
        other = lax.broadcasted_iota(jnp.int32, (slab, row_len), 1)
        ids = seg[...].astype(jnp.float32)
        mine = jnp.sum(jnp.where(other == spot, ids, 0.0), axis=1, keepdims=True)
        bias[...] = jnp.where((other <= spot) & (mine == ids), 0.0, -jnp.inf)

    def project(k):
        if once("wq"):
            loads[1].wait()
        a0 = pc.near(k)
        if k > 0:
            wq_line.here(a0)
        left = normed[...].reshape(slab, width)
        out = (jnp.dot(left, wq[a0], preferred_element_type=jnp.float32) * q_scale).astype(jnp.bfloat16)
        for h in range(heads):
            queries[a0, h * slab : (h + 1) * slab, :] = out[:, h * head : (h + 1) * head]

    def fold(scores, values, a0, fresh):
        new_top = jnp.max(scores, axis=-1, keepdims=True)
        if not fresh:
            new_top = jnp.maximum(top_ref[a0], new_top)
        probs = jnp.exp(scores - new_top)
        total = jnp.sum(probs, axis=-1, keepdims=True)
        weighted = jnp.dot(probs.astype(jnp.bfloat16), values, preferred_element_type=jnp.float32)
        if not fresh:
            factor = jnp.exp(top_ref[a0] - new_top)
            total = total + total_ref[a0] * factor
            weighted = weighted + weighted_ref[a0] * factor
        return new_top, total, weighted

    def raw_scores(a0, keys_here):
        return lax.dot_general(queries[a0], keys_here, (((1,), (1,)), ((), ())),
                               preferred_element_type=jnp.float32)

    def over_prefix(k, h):
        e, a0 = pc.near(k), pc.near(h)
        if once("kv", k):
            keys.pair_arrived(e)
        pair = cached[pl.ds(e * B, B), :span, :].reshape(B * span, 2 * head)
        state = fold(raw_scores(a0, pair[:, :head]), pair[:, head:], a0, k == 0)
        top_ref[a0], total_ref[a0], weighted_ref[a0] = state

    def over_suffix(h):
        a0 = pc.near(h)
        fresh = cached[:, span:, :].reshape(row_len, 2 * head)
        scores = raw_scores(a0, fresh[:, :head]).reshape(heads, slab, row_len) + bias[...][None]
        _, total, weighted = fold(scores.reshape(heads * slab, row_len), fresh[:, head:], a0, False)
        out = (weighted / total).astype(jnp.bfloat16)
        for g in range(heads):
            attn[a0, :, g * head : (g + 1) * head] = out[g * slab : (g + 1) * slab]

    out_wide = min(512, part_cols)

    def out_part(j, k):
        if once("wout"):
            loads[2].wait()
        a0 = pc.near(k)
        if k > 0:
            wout_line.here(a0, j)

        def column(c, carry):
            cols = pl.ds(pl.multiple_of(j * part_cols + c * out_wide, out_wide), out_wide)
            out = jnp.dot(attn[a0], wout[a0, :, cols], preferred_element_type=jnp.float32)
            if k > 0:
                out = out + out_sum[:, cols]
            out_sum[:, cols] = out
            return carry

        lax.fori_loop(0, part_cols // out_wide, column, 0)

    def out_copy(o, j):
        cols = pl.ds(j * part_cols, part_cols)
        return remote(out_send.at[o - 1, :, cols], out_in.at[o - 1, :, cols], out_sem.at[o - 1, j],
                      out_recv.at[o - 1, j], pc.side(o))

    def out_give(j):
        cols = pl.ds(j * part_cols, part_cols)
        for o in range(1, B):
            base = pc.across(o) * rows

            def give(part):
                spot = pl.ds(pl.multiple_of(base + part.start, ROWS), ROWS)
                out_send[o - 1, part, cols] = out_sum[spot, cols].astype(jnp.bfloat16)

            row_loop(0, rows, give)
            out_copy(o, j).start()

    def out_take(j):
        cols = pl.ds(j * part_cols, part_cols)
        for o in range(1, B):
            out_copy(o, j).wait_recv()

        def body(part):
            total = out_sum[pl.ds(pl.multiple_of(pc.b * rows + part.start, ROWS), ROWS), cols]
            for o in range(1, B):
                total = total + out_in[o - 1, part, cols].astype(jnp.float32)
            out = total.astype(jnp.bfloat16)
            attended[part, cols] = out
            middle[part, cols] = (hidden[part, cols].astype(jnp.float32) + out.astype(jnp.float32)).astype(jnp.bfloat16)

        row_loop(0, rows, body)

    def norm_middle(s):
        gains = gain2[...].astype(jnp.float32).reshape(1, width)

        def second(part):
            normed2[pc.a, part, :] = norm_rows(middle[part, :].astype(jnp.float32), gains)

        row_loop(s * half, half, second)
        gather.start(s)

    act_wide = min(256, units)

    def expand(k):
        e = pc.near(k)
        if once("wfc"):
            loads[3].wait()
        for s in range(B):

            def column(c, carry):
                cols = span_of(c, act_wide)
                out = jnp.dot(normed2[e], wfc[s, :, cols], preferred_element_type=jnp.float32)
                spot = pl.ds(pl.multiple_of(s * units + c * act_wide, act_wide), act_wide)
                act[span_of(e, rows), spot] = jax.nn.gelu(out, approximate=True).astype(jnp.bfloat16)
                return carry

            lax.fori_loop(0, units // act_wide, column, 0)

    def contract(k, i):
        e = pc.near(k)
        if once("wproj"):
            loads[4].wait()
        cols = pl.ds(i * red_cols, red_cols)
        out = jnp.dot(act[span_of(e, rows), :], wproj[:, cols], preferred_element_type=jnp.float32)
        term[e, :, cols] = out.astype(jnp.bfloat16)
        if k > 0:

            @pl.when(end)
            def _():
                reduce.pass_on(e, i)

    def pass_on(which, i):
        @pl.when(jnp.logical_not(end))
        def _():
            reduce.pass_on(reduce_blocks[which], i)

    def last(part, cols, total):
        layer_out[part, cols] = (middle[part, cols].astype(jnp.float32) + total).astype(jnp.bfloat16)

    def finish_misc():
        for o in range(1, pc.pairs):
            dp_copy(o).wait_send()
        for o in range(pc.pairs):
            dp_to_core(o).wait_send()
        for o in range(1, B):
            tok_copy(o).wait_send()
            for j in range(PARTS):
                out_copy(o, j).wait_send()

    def finish_side():
        fc_side.finish()
        pr_side.finish()

    steps = {
        "fin.wq": wq_line.finish,
        "fin.wo": wout_line.finish,
        "fin.keys": keys.finish,
        "fin.misc": finish_misc,
        "fin.side": finish_side,
        "fin.g": gather.finish,
        "fin.r": reduce.finish,
        "wq.start": wq_line.start,
        "wq.hop": wq_line.hop,
        "wq.spread": wq_line.spread,
        "wo.start": wout_line.start,
        "wo.hop": lambda j, r: wout_line.hop(r, j),
        "wo.spread": lambda j, r: wout_line.spread(r, j),
        "dp.start": dp_start,
        "dp.relay": dp_relay,
        "select": select,
        "keys.start": keys.start,
        "keys.round": keys.round,
        "ln1": norm_tokens,
        "tok.start": tok_start,
        "tok.wait": tok_wait,
        "skv": suffix_keys,
        "proj": project,
        "att": over_prefix,
        "suf": over_suffix,
        "out": out_part,
        "rs.send": out_give,
        "rs.recv": out_take,
        "ln2": norm_middle,
        "side.start": lambda j: side("start", j),
        "side.hop": lambda j: side("hop", j),
        "side.spread": lambda j: side("spread", j),
        "fc.here": fc_side.here,
        "pr.here": pr_side.here,
        "g.hop": gather.hop,
        "expand": expand,
        "contract": contract,
        "po": pass_on,
        "res": lambda i: reduce.result(i, last),
    }
    greet_wait(pc)
    for name, *numbers in PLAN:
        steps[name](*numbers)


def hand_on(attended, layer_out, attended_to, layer_to):
    attended_to[...] = attended[...]
    layer_to[...] = layer_out[...]


VM = pl.BlockSpec(memory_space=pltpu.VMEM)


def local(n, ndp, hidden_in, norm1_gain, norm2_gain, w_query, w_keyval, w_out, w_fc, w_proj,
          prefix_kv, owner_ids, segment_ids):
    A, B = plane(n)
    rows, width = hidden_in.shape
    head = w_keyval.shape[1] // 2
    query_cols = w_query.shape[1]
    heads = query_cols // head
    span = prefix_kv.shape[1]
    units = w_fc.shape[1]
    q_scale = 1.0 / math.sqrt(head)
    bf, f32 = jnp.bfloat16, jnp.float32
    any_space = pl.BlockSpec(memory_space=pl.ANY)
    own = jax.ShapeDtypeStruct((rows, width), bf)
    V = pltpu.VMEM
    stack = heads * B * rows
    line = V((A, rows, width), bf)
    sides = max(B - 1, 1)
    scratch = [
        V(w_keyval.shape, bf), V((A,) + w_query.shape, bf), V((A,) + w_out.shape, bf),
        V((B,) + w_fc.shape, bf), V((B * units, width), bf),
        V((B, rows, width), bf), line, V((A * rows, B * units), bf), line, line, line,
        V((n, span + rows, 2 * head), bf), V((ndp, span, 2 * head), bf), V((A, stack, head), bf),
        V((A, stack, 1), f32), V((A, stack, 1), f32), V((A, stack, head), f32),
        V((A, B * rows, query_cols), bf), V((B * rows, width), f32),
        V((sides, rows, width), bf), V((sides, rows, width), bf), V((rows, width), bf),
        V((B * rows, n * rows), f32), DMA((5,)),
        DMA((B,)), DMA((sides,)), DMA((sides, PARTS)), DMA((sides, PARTS)),
        DMA((ndp,)), DMA((max(ndp // 2 - 1, 1),)), DMA((ndp // 2,)),
    ]
    scratch += gather_sems(n) + line_weight_sems(n, 1) + line_weight_sems(n, PARTS) + side_weight_sems(n) * 2
    scratch += [DMA((A, HALVES))] * 3 + [DMA((A, PIECES))] * 4
    attended, layer_out = pl.pallas_call(
        functools.partial(layer_kernel, n, ndp, heads, q_scale),
        out_shape=(own, own),
        in_specs=[VM] * 4 + [pl.BlockSpec(memory_space=pltpu.SMEM), VM] + [any_space] * 5,
        out_specs=(VM, VM),
        scratch_shapes=scratch,
        compiler_params=pltpu.CompilerParams(collective_id=1, has_side_effects=True, vmem_limit_bytes=62 << 20),
        name="layer",
    )(hidden_in, norm1_gain, norm2_gain, prefix_kv, owner_ids, segment_ids, w_keyval, w_query, w_out,
      w_fc, w_proj)
    attended, layer_out = pl.pallas_call(
        hand_on, out_shape=(own, own), in_specs=[VM] * 2, out_specs=(VM, VM), name="hand_on",
    )(attended, layer_out)
    return (layer_out, attended)


def solution(mesh):
    return jax.shard_map(
        functools.partial(local, mesh.shape["tensor"], mesh.shape["dp"]),
        mesh=mesh,
        in_specs=(
            P(("dp", "tensor"), None),
            P(),
            P(),
            P(None, "tensor"),
            P(),
            P("tensor", None),
            P(None, "tensor"),
            P("tensor", None),
            P("dp", "tensor", None),
            P(),
            P("dp", None),
        ),
        out_specs=(P(("dp", "tensor"), None), P(("dp", "tensor"), None)),
        check_vma=False,
    )
```

```python
import functools
import math

import jax
import jax.numpy as jnp
from jax import lax
from jax.experimental import pallas as pl
from jax.experimental.pallas import tpu as pltpu
from jax.sharding import PartitionSpec as P

MESH = pl.DeviceIdType.MESH
ROWS = 16
PIECES = 4
SIDE = 8
PARTS = 2
HALVES = 2
TEAM = 4


def plane(n):
    lines = 4 if n % 4 == 0 else n
    return lines, n // lines


def norm_rows(widened, gains):
    centre = jnp.mean(widened, axis=-1, keepdims=True)
    centred = widened - centre
    variance = jnp.mean(centred * centred, axis=-1, keepdims=True)
    return (centred * lax.rsqrt(variance + 1e-05) * gains).astype(jnp.bfloat16)


def row_loop(start, rows, body):
    def step(i, carry):
        body(pl.ds(pl.multiple_of(start + i * ROWS, ROWS), ROWS))
        return carry

    lax.fori_loop(0, rows // ROWS, step, 0)


def span_of(i, size):
    return pl.ds(pl.multiple_of(i * size, size), size)


class Place:
    def __init__(self, n, ndp):
        self.n, self.ndp = n, ndp
        self.A, self.B = plane(n)
        self.me = lax.axis_index("tensor")
        self.a = self.me // self.B
        self.b = self.me % self.B
        self.dp = lax.axis_index("dp")
        self.pairs = ndp // 2
        self.q = self.dp % TEAM
        base = self.dp - self.q
        self.q_core = self.q + 1 - 2 * (self.q % 2)
        self.q_far = (self.q + 2) % TEAM
        self.q_diag = (self.q_core + 2) % TEAM
        self.core = {"dp": base + self.q_core}
        self.across_dp = {"dp": base + self.q_far}

    def across(self, o):
        return (self.b + o) % self.B

    def peer(self, a, b):
        return {"tensor": a * self.B + b}

    def side(self, o):
        return self.peer(self.a, self.across(o))

    def up(self):
        return self.peer(jnp.minimum(self.a + 1, self.A - 1), self.b)

    def down(self):
        return self.peer(jnp.maximum(self.a - 1, 0), self.b)

    def same_core(self, o):
        return ((self.dp // 2 + o) % self.pairs) * 2 + self.dp % 2

    def choose(self, k, key):
        found = 0
        for a in range(self.A):
            order = sorted(range(self.A), key=lambda d: key(a, d))
            for i, d in enumerate(order):
                found = found + jnp.where((self.a == a) & (k == i), d, 0)
        return found

    def near(self, k):
        return self.choose(k, lambda a, d: (abs(d - a), d))

    def far(self, k):
        return self.choose(k, lambda a, d: (-abs(d - a), d))


def greet_signal(pc):
    barrier = pltpu.get_barrier_semaphore()

    def signal(device):
        pl.semaphore_signal(barrier, inc=1, device_id=device, device_id_type=MESH)

    @pl.when(pc.a > 0)
    def _():
        signal(pc.peer(pc.a - 1, pc.b))

    @pl.when(pc.a < pc.A - 1)
    def _():
        signal(pc.peer(pc.a + 1, pc.b))

    for o in range(1, pc.B):
        signal(pc.side(o))
    for o in range(1, pc.pairs):
        signal({"dp": pc.same_core(o)})
    signal(pc.core)


def greet_wait(pc):
    ends = jnp.where((pc.a == 0) | (pc.a == pc.A - 1), 1, 2)
    pl.semaphore_wait(pltpu.get_barrier_semaphore(), pc.B - 1 + pc.pairs + ends)


def remote(src, dst, send, recv, device):
    return pltpu.make_async_remote_copy(
        src_ref=src, dst_ref=dst, send_sem=send, recv_sem=recv, device_id=device, device_id_type=MESH
    )


class Gather:
    def __init__(self, place, buf, recv, up, down, side):
        self.pc, self.buf, self.recv, self.up, self.down, self.side = place, buf, recv, up, down, side

    def copy_up(self, a0):
        blk = a0 * self.pc.B + self.pc.b
        return remote(self.buf.at[blk], self.buf.at[blk], self.up.at[a0], self.recv.at[blk], self.pc.up())

    def copy_down(self, a0):
        blk = a0 * self.pc.B + self.pc.b
        return remote(self.buf.at[blk], self.buf.at[blk], self.down.at[a0], self.recv.at[blk], self.pc.down())

    def copy_side(self, a0, o):
        blk = a0 * self.pc.B + self.pc.b
        return remote(self.buf.at[blk], self.buf.at[blk], self.side.at[a0, o - 1], self.recv.at[blk],
                      self.pc.side(o))

    def arrived(self, blk):
        remote(self.buf.at[blk], self.buf.at[blk], self.up.at[0], self.recv.at[blk],
               self.pc.side(1)).wait_recv()

    def start(self):
        pc = self.pc

        @pl.when(pc.a < pc.A - 1)
        def _():
            self.copy_up(pc.a).start()

        @pl.when(pc.a > 0)
        def _():
            self.copy_down(pc.a).start()

        for o in range(1, pc.B):
            self.copy_side(pc.a, o).start()

    def round(self, r):
        pc = self.pc

        @pl.when(pc.a - r >= 0)
        def _():
            a0 = pc.a - r
            self.arrived(a0 * pc.B + pc.b)

            @pl.when(pc.a < pc.A - 1)
            def _():
                self.copy_up(a0).start()

            for o in range(1, pc.B):
                self.copy_side(a0, o).start()

        @pl.when(pc.a + r < pc.A)
        def _():
            a0 = pc.a + r
            self.arrived(a0 * pc.B + pc.b)

            @pl.when(pc.a > 0)
            def _():
                self.copy_down(a0).start()

            for o in range(1, pc.B):
                self.copy_side(a0, o).start()

    def pair_arrived(self, a0):
        for o in range(1, self.pc.B):
            self.arrived(a0 * self.pc.B + self.pc.across(o))

    def finish(self):
        pc = self.pc
        for a0 in range(pc.A):
            for o in range(1, pc.B):
                self.copy_side(a0, o).wait_send()

            @pl.when((pc.a >= a0) & (pc.a < pc.A - 1))
            def _():
                self.copy_up(a0).wait_send()

            @pl.when((pc.a <= a0) & (pc.a > 0))
            def _():
                self.copy_down(a0).wait_send()


DMA = pltpu.SemaphoreType.DMA


def gather_sems(n):
    A, B = plane(n)
    return [DMA((n,)), DMA((A,)), DMA((A,)), DMA((A, max(B - 1, 1)))]


class Team:
    def __init__(self, place, part, recv, far_send, core_send):
        self.pc, self.part, self.recv, self.far_send, self.core_send = place, part, recv, far_send, core_send

    def far_copy(self, s):
        pc = self.pc
        ref = self.part(s, pc.q)
        return remote(ref, ref, self.far_send.at[s], self.recv.at[s, pc.q], pc.across_dp)

    def core_copy(self, s, which):
        pc = self.pc
        q = pc.q_far if which else pc.q
        ref = self.part(s, q)
        return remote(ref, ref, self.core_send.at[s, which], self.recv.at[s, q], pc.core)

    def wait(self, s, q):
        ref = self.part(s, q)
        remote(ref, ref, self.far_send.at[s], self.recv.at[s, q], self.pc.core).wait_recv()

    def landed(self, s):
        self.far_copy(s).start()
        self.core_copy(s, 0).start()

    def spread(self, s):
        self.wait(s, self.pc.q_far)
        self.core_copy(s, 1).start()

    def here(self, s):
        self.wait(s, self.pc.q_core)
        self.wait(s, self.pc.q_diag)

    def finish(self, s):
        self.far_copy(s).wait_send()
        self.core_copy(s, 0).wait_send()
        self.core_copy(s, 1).wait_send()


def team_sems(slots):
    return [DMA((slots, TEAM)), DMA((slots,)), DMA((slots, 2))]


class LineWeights:
    def __init__(self, place, hbm, buf, parts, recv, far_send, core_send, up, down):
        self.pc, self.hbm, self.up, self.down, self.recv, self.parts = place, hbm, up, down, recv, parts
        quarter = buf.shape[1] // TEAM
        cols = buf.shape[2] // parts
        self.part = lambda s, q: buf.at[s // parts, span_of(q, quarter), span_of(s % parts, cols)]
        self.own = lambda j: hbm.at[span_of(place.q, quarter), pl.ds(j * cols, cols)]
        self.team = Team(place, self.part, recv, far_send, core_send)

    def copy_up(self, s, src=None):
        pc = self.pc
        ref = self.part(s, pc.q)
        return remote(ref if src is None else src, ref, self.up.at[s], self.recv.at[s, pc.q], pc.up())

    def copy_down(self, s, src=None):
        pc = self.pc
        ref = self.part(s, pc.q)
        return remote(ref if src is None else src, ref, self.down.at[s], self.recv.at[s, pc.q], pc.down())

    def start(self, j=0):
        pc = self.pc
        s = pc.a * self.parts + j

        @pl.when(pc.a < pc.A - 1)
        def _():
            self.copy_up(s, self.own(j)).start()

        @pl.when(pc.a > 0)
        def _():
            self.copy_down(s, self.own(j)).start()

    def hop(self, r, j=0):
        pc = self.pc

        @pl.when(pc.a - r >= 0)
        def _():
            s = (pc.a - r) * self.parts + j
            self.team.wait(s, pc.q)

            @pl.when(pc.a < pc.A - 1)
            def _():
                self.copy_up(s).start()

            self.team.landed(s)

        @pl.when(pc.a + r < pc.A)
        def _():
            s = (pc.a + r) * self.parts + j
            self.team.wait(s, pc.q)

            @pl.when(pc.a > 0)
            def _():
                self.copy_down(s).start()

            self.team.landed(s)

    def spread(self, r, j=0):
        pc = self.pc

        @pl.when(pc.a - r >= 0)
        def _():
            self.team.spread((pc.a - r) * self.parts + j)

        @pl.when(pc.a + r < pc.A)
        def _():
            self.team.spread((pc.a + r) * self.parts + j)

    def here(self, a0, j=0):
        self.team.here(a0 * self.parts + j)

    def finish(self):
        pc = self.pc
        for s in range(pc.A * self.parts):
            a0 = s // self.parts

            @pl.when((pc.a >= a0) & (pc.a < pc.A - 1))
            def _():
                self.copy_up(s).wait_send()

            @pl.when((pc.a <= a0) & (pc.a > 0))
            def _():
                self.copy_down(s).wait_send()

            @pl.when(pc.a != a0)
            def _():
                self.team.finish(s)


def line_weight_sems(n, parts):
    A, _ = plane(n)
    return team_sems(A * parts) + [DMA((A * parts,)), DMA((A * parts,))]


class SideWeights:
    def __init__(self, place, part, own, recv, far_send, core_send, side_send):
        self.pc, self.part3, self.own, self.recv, self.side_send = place, part, own, recv, side_send
        self.team = Team(place, lambda s, q: part(s // SIDE, s % SIDE, q), recv, far_send, core_send)

    def slots(self, i):
        return [self.pc.across(o) * SIDE + i for o in range(1, self.pc.B)]

    def copy(self, i, o):
        pc = self.pc
        return remote(self.own(i, pc.q), self.part3(pc.b, i, pc.q), self.side_send.at[o - 1, i],
                      self.recv.at[pc.b * SIDE + i, pc.q], pc.side(o))

    def start(self, i):
        for o in range(1, self.pc.B):
            self.copy(i, o).start()

    def hop(self, i):
        for s in self.slots(i):
            self.team.wait(s, self.pc.q)
            self.team.landed(s)

    def spread(self, i):
        for s in self.slots(i):
            self.team.spread(s)

    def here(self, i):
        for s in self.slots(i):
            self.team.here(s)

    def finish(self):
        for i in range(SIDE):
            for o in range(1, self.pc.B):
                self.copy(i, o).wait_send()
            for s in self.slots(i):
                self.team.finish(s)


def side_weight_sems(n):
    _, B = plane(n)
    return team_sems(B * SIDE) + [DMA((max(B - 1, 1), SIDE))]


class LineGather:
    def __init__(self, place, buf, recv, up, down):
        self.pc, self.buf, self.recv, self.up, self.down = place, buf, recv, up, down
        self.half = buf.shape[1] // HALVES

    def ref(self, a0, s):
        return self.buf.at[a0, pl.ds(s * self.half, self.half), :]

    def copy_up(self, a0, s):
        return remote(self.ref(a0, s), self.ref(a0, s), self.up.at[a0, s], self.recv.at[a0, s], self.pc.up())

    def copy_down(self, a0, s):
        return remote(self.ref(a0, s), self.ref(a0, s), self.down.at[a0, s], self.recv.at[a0, s], self.pc.down())

    def start(self, s):
        pc = self.pc

        @pl.when(pc.a < pc.A - 1)
        def _():
            self.copy_up(pc.a, s).start()

        @pl.when(pc.a > 0)
        def _():
            self.copy_down(pc.a, s).start()

    def hop(self, r, only=None):
        pc = self.pc
        for s in range(HALVES) if only is None else (only,):

            @pl.when(pc.a - r >= 0)
            def _():
                self.copy_up(pc.a - r, s).wait_recv()

                @pl.when(pc.a < pc.A - 1)
                def _():
                    self.copy_up(pc.a - r, s).start()

            @pl.when(pc.a + r < pc.A)
            def _():
                self.copy_down(pc.a + r, s).wait_recv()

                @pl.when(pc.a > 0)
                def _():
                    self.copy_down(pc.a + r, s).start()

    def finish(self):
        pc = self.pc
        for a0 in range(pc.A):
            for s in range(HALVES):

                @pl.when((pc.a >= a0) & (pc.a < pc.A - 1))
                def _():
                    self.copy_up(a0, s).wait_send()

                @pl.when((pc.a <= a0) & (pc.a > 0))
                def _():
                    self.copy_down(a0, s).wait_send()


class LineReduce:
    def __init__(self, place, term, up_in, down_in, up_send, up_recv, down_send, down_recv):
        self.pc, self.term, self.up_in, self.down_in = place, term, up_in, down_in
        self.up_send, self.up_recv, self.down_send, self.down_recv = up_send, up_recv, down_send, down_recv
        self.rows = term.shape[1]
        self.wide = term.shape[2] // PIECES

    def spot(self, i, half):
        rows = pl.ds(0, self.rows) if half is None else pl.ds(half * (self.rows // HALVES), self.rows // HALVES)
        return rows, span_of(i, self.wide), 0 if half is None else half

    def copy_up(self, d, i, half=None):
        rows, cols, s = self.spot(i, half)
        return remote(self.term.at[d, rows, cols], self.up_in.at[d, rows, cols], self.up_send.at[d, i, s],
                      self.up_recv.at[d, i, s], self.pc.up())

    def copy_down(self, d, i, half=None):
        rows, cols, s = self.spot(i, half)
        return remote(self.term.at[d, rows, cols], self.down_in.at[d, rows, cols], self.down_send.at[d, i, s],
                      self.down_recv.at[d, i, s], self.pc.down())

    def add(self, d, i, half, arrived):
        area, cols, _ = self.spot(i, half)

        def body(rows):
            total = self.term[d, rows, cols].astype(jnp.float32) + arrived[d, rows, cols].astype(jnp.float32)
            self.term[d, rows, cols] = total.astype(jnp.bfloat16)

        row_loop(area.start, area.size, body)

    def pass_on(self, d, i, half=None):
        pc = self.pc

        @pl.when(d > pc.a)
        def _():
            @pl.when(pc.a > 0)
            def _():
                self.copy_up(d, i, half).wait_recv()
                self.add(d, i, half, self.up_in)

            self.copy_up(d, i, half).start()

        @pl.when(d < pc.a)
        def _():
            @pl.when(pc.a < pc.A - 1)
            def _():
                self.copy_down(d, i, half).wait_recv()
                self.add(d, i, half, self.down_in)

            self.copy_down(d, i, half).start()

    def result(self, i, half, use):
        pc = self.pc

        def go(terms, part):
            area, cols, _ = self.spot(i, part)

            def body(rows):
                total = self.term[pc.a, rows, cols].astype(jnp.float32)
                for arrived in terms:
                    total = total + arrived[pc.a, rows, cols].astype(jnp.float32)
                use(rows, cols, total)

            row_loop(area.start, area.size, body)

        @pl.when(pc.a == 0)
        def _():
            self.copy_down(pc.a, i, half).wait_recv()
            go([self.down_in], half)

        @pl.when(pc.a == pc.A - 1)
        def _():
            self.copy_up(pc.a, i, half).wait_recv()
            go([self.up_in], half)

        if half == 0:

            @pl.when((pc.a > 0) & (pc.a < pc.A - 1))
            def _():
                self.copy_up(pc.a, i).wait_recv()
                self.copy_down(pc.a, i).wait_recv()
                go([self.up_in, self.down_in], None)

    def finish(self):
        pc = self.pc
        for d in range(pc.A):
            for i in range(PIECES):
                for half in range(HALVES) if d in (0, pc.A - 1) else (None,):

                    @pl.when(pc.a < d)
                    def _():
                        self.copy_up(d, i, half).wait_send()

                    @pl.when(pc.a > d)
                    def _():
                        self.copy_down(d, i, half).wait_send()


PLAN = (
    ("dp.start",), ("side.start", 0), ("wq.start",), ("wo.start", 0), ("side.start", 1), ("ln1",),
    ("tok.start",), ("side.start", 2), ("side.hop", 0), ("wq.hop", 1), ("side.start", 3), ("side.start", 4),
    ("dp.relay",), ("select",), ("skv",), ("keys.start",), ("wq.hop", 2), ("side.hop", 1), ("keys.round", 1),
    ("side.hop", 2), ("side.hop", 3), ("wq.hop", 3), ("tok.wait",), ("proj", 0), ("wq.spread", 1), ("proj", 1),
    ("side.spread", 1), ("wq.spread", 2), ("proj", 2), ("att", 0, 0), ("att", 0, 2), ("keys.round", 2),
    ("wo.start", 1), ("wo.hop", 0, 1), ("att", 0, 1), ("side.hop", 4), ("wq.spread", 3), ("proj", 3),
    ("att", 0, 3), ("att", 1, 1), ("att", 1, 2), ("keys.round", 3), ("side.start", 5), ("side.start", 6),
    ("att", 1, 0), ("att", 1, 3), ("wo.hop", 1, 1), ("att", 2, 0), ("side.spread", 0), ("side.spread", 4),
    ("wo.spread", 0, 1), ("side.start", 7), ("side.start", 8), ("wo.hop", 0, 2), ("fc.here", 1), ("att", 2, 1),
    ("att", 2, 3), ("att", 2, 2), ("wo.spread", 1, 1), ("wo.hop", 1, 2), ("att", 3, 3), ("att", 3, 2),
    ("wo.hop", 0, 3), ("suf", 3), ("att", 3, 1), ("att", 3, 0), ("wo.spread", 0, 2), ("wo.hop", 1, 3),
    ("suf", 0), ("out", 0, 0), ("suf", 1), ("wo.spread", 0, 3), ("suf", 2), ("out", 0, 1), ("out", 0, 2),
    ("fc.here", 4), ("out", 0, 3), ("rs.send", 0), ("wo.spread", 1, 3), ("wo.spread", 1, 2), ("out", 1, 0),
    ("out", 1, 1), ("side.spread", 2), ("fin.wq",), ("out", 1, 2), ("fin.keys",), ("side.hop", 5),
    ("fc.here", 0), ("side.hop", 6), ("out", 1, 3), ("side.spread", 3), ("side.hop", 7), ("rs.send", 1),
    ("side.start", 9), ("rs.recv", 0), ("side.hop", 8), ("side.start", 10), ("side.spread", 6),
    ("side.start", 11), ("rs.recv", 1), ("ln2", 0), ("ln2", 1), ("side.hop", 9), ("fin.wo",),
    ("side.spread", 7), ("side.start", 12), ("side.start", 13), ("fc.here", 2), ("side.spread", 5),
    ("fc.here", 5), ("side.hop", 10), ("side.spread", 8), ("fc.here", 6), ("fc.here", 3), ("fc.here", 7),
    ("expand", 0), ("side.hop", 11), ("fin.misc",), ("g.hop", 1), ("side.spread", 9), ("side.start", 14),
    ("pr.here", 0), ("expand", 1), ("side.hop", 12), ("side.start", 15), ("side.spread", 10),
    ("side.spread", 11), ("side.hop", 13), ("side.hop", 14), ("pr.here", 3), ("pr.here", 2), ("pr.here", 1),
    ("contract", 1, 0), ("contract", 1, 1), ("g.hop", 2), ("expand", 2), ("contract", 2, 0), ("side.hop", 15),
    ("contract", 2, 1), ("g.hop", 3, 0), ("side.spread", 13), ("side.spread", 12), ("expand", 3, 0),
    ("contract", 3, 1, 0), ("pr.here", 4), ("po", "m", 0), ("contract", 3, 0, 0), ("pr.here", 5),
    ("contract", 3, 2, 0), ("contract", 0, 0), ("side.spread", 15), ("po", "m", 1), ("g.hop", 3, 1),
    ("expand", 3, 1), ("po", "f", 1, 0), ("po", "f", 0, 0), ("contract", 3, 0, 1), ("po", "f", 0, 1),
    ("side.spread", 14), ("fin.g",), ("contract", 3, 1, 1), ("po", "f", 1, 1), ("pr.here", 6), ("pr.here", 7),
    ("po", "f", 2, 0), ("contract", 3, 3, 1), ("po", "n", 1, 0), ("contract", 3, 3, 0), ("po", "f", 3, 1),
    ("po", "n", 0, 0), ("contract", 3, 2, 1), ("contract", 2, 3), ("po", "n", 0, 1), ("po", "f", 3, 0),
    ("contract", 2, 2), ("po", "f", 2, 1), ("contract", 1, 3), ("po", "n", 1, 1), ("contract", 1, 2),
    ("po", "n", 2, 0), ("contract", 0, 3), ("po", "m", 3), ("po", "n", 3, 1), ("contract", 0, 1), ("res", 1, 0),
    ("contract", 0, 2), ("po", "n", 3, 0), ("po", "m", 2), ("res", 1, 1), ("res", 0, 0), ("po", "n", 2, 1),
    ("fin.side",), ("res", 0, 1), ("fin.r",), ("res", 3, 0), ("res", 3, 1), ("res", 2, 0), ("res", 2, 1),
)


def layer_kernel(n, ndp, heads, q_scale, hidden, gain1, gain2, prefix, owners, seg, w_keyval_hbm, w_query_hbm,
                 w_out_hbm, w_fc_hbm, w_proj_hbm, attended, layer_out, *scratch):
    pc = Place(n, ndp)
    A, B = pc.A, pc.B
    greet_signal(pc)
    scratch = list(scratch)

    def take(count):
        got = scratch[:count]
        del scratch[:count]
        return got

    wkv, wq, wout, wfc, wproj = take(5)
    normed, normed2, act, term, up_in, down_in = take(6)
    cached, from_dp, queries, top_ref, total_ref, weighted_ref, attn, out_sum, out_send, out_in, middle, bias = take(12)
    (load,) = take(1)
    tok_recv, tok_send, out_sem, out_recv = take(4)
    dp_recv, dp_send, dp_core = take(3)
    rows, width = hidden.shape
    slab = B * rows
    span = prefix.shape[1]
    row_len = n * rows
    head = wkv.shape[1] // 2
    units = w_fc_hbm.shape[1]
    half = rows // HALVES
    dp = pc.dp

    keys = Gather(pc, cached, *take(4))
    wq_line = LineWeights(pc, w_query_hbm, wq, 1, *take(5))
    wout_line = LineWeights(pc, w_out_hbm, wout, PARTS, *take(5))
    fc_rows, fc_part = width // TEAM, width // TEAM // SIDE
    pr_rows, pr_cols = units // TEAM, width // SIDE
    red_cols = width // PIECES
    part_cols = width // PARTS
    fc_side = SideWeights(
        pc,
        lambda s, i, q: wfc.at[s, pl.ds(pl.multiple_of(q * fc_rows + i * fc_part, fc_part), fc_part), :],
        lambda i, q: w_fc_hbm.at[pl.ds(pl.multiple_of(q * fc_rows + i * fc_part, fc_part), fc_part), :],
        *take(4))
    pr_side = SideWeights(
        pc,
        lambda s, i, q: wproj.at[pl.ds(pl.multiple_of(s * units + q * pr_rows, pr_rows), pr_rows), span_of(i, pr_cols)],
        lambda i, q: w_proj_hbm.at[span_of(q, pr_rows), span_of(i, pr_cols)],
        *take(4))
    gather = LineGather(pc, normed2, *take(3))
    reduce = LineReduce(pc, term, up_in, down_in, *take(4))

    def side(kind, j):
        getattr(fc_side if j < SIDE else pr_side, kind)(j % SIDE)

    loads = [
        pltpu.make_async_copy(w_keyval_hbm, wkv, load.at[0]),
        pltpu.make_async_copy(w_query_hbm, wq.at[pc.a], load.at[1]),
        pltpu.make_async_copy(w_out_hbm, wout.at[pc.a], load.at[2]),
        pltpu.make_async_copy(w_fc_hbm, wfc.at[pc.b], load.at[3]),
        pltpu.make_async_copy(w_proj_hbm, wproj.at[span_of(pc.b, units), :], load.at[4]),
    ]
    for copy in loads[:2]:
        copy.start()
    end = (pc.a == 0) | (pc.a == A - 1)
    low = pc.a < A // 2
    far_block = jnp.where(low, A - 1, 0)
    reduce_blocks = {"m": jnp.where(low, pc.a + 1, pc.a - 1), "f": far_block, "n": A - 1 - far_block}
    seen = set()

    def once(*key):
        if key in seen:
            return False
        seen.add(key)
        return True

    def dp_copy(o):
        return remote(prefix.at[0], from_dp.at[dp], dp_send.at[o - 1], dp_recv.at[dp], {"dp": pc.same_core(o)})

    def dp_to_core(o):
        src = pc.same_core(o)
        ref = prefix.at[0] if o == 0 else from_dp.at[src]
        return remote(ref, from_dp.at[src], dp_core.at[o], dp_recv.at[src], pc.core)

    def dp_arrived(src):
        remote(prefix.at[0], from_dp.at[src], dp_send.at[0], dp_recv.at[src], pc.core).wait_recv()

    def dp_start():
        for o in range(1, pc.pairs):
            dp_copy(o).start()
        dp_to_core(0).start()
        from_dp[dp] = prefix[0]

    def dp_relay():
        for o in range(1, pc.pairs):
            dp_arrived(pc.same_core(o))
            dp_to_core(o).start()

    def select():
        for o in range(pc.pairs):
            src = pc.same_core(o)
            dp_arrived(src + 1 - 2 * (src % 2))
        cached[pc.me, :span, :] = from_dp[owners[dp]]

    def norm_tokens():
        gains = gain1[...].astype(jnp.float32).reshape(1, width)

        def first(part):
            normed[pc.b, part, :] = norm_rows(hidden[part, :].astype(jnp.float32), gains)

        row_loop(0, rows, first)

    def tok_copy(o):
        return remote(normed.at[pc.b], normed.at[pc.b], tok_send.at[o - 1], tok_recv.at[pc.b], pc.side(o))

    def tok_start():
        for copy in loads[2:]:
            copy.start()
        for o in range(1, B):
            tok_copy(o).start()

    def tok_wait():
        for o in range(1, B):
            s = pc.across(o)
            remote(normed.at[s], normed.at[s], tok_send.at[0], tok_recv.at[s], pc.side(1)).wait_recv()

    def suffix_keys():
        loads[0].wait()
        cached[pc.me, span:, :] = jnp.dot(
            normed[pc.b], wkv[...], preferred_element_type=jnp.float32
        ).astype(jnp.bfloat16)
        spot = pc.a * slab + lax.broadcasted_iota(jnp.int32, (slab, row_len), 0)
        other = lax.broadcasted_iota(jnp.int32, (slab, row_len), 1)
        ids = seg[...].astype(jnp.float32)
        mine = jnp.sum(jnp.where(other == spot, ids, 0.0), axis=1, keepdims=True)
        bias[...] = jnp.where((other <= spot) & (mine == ids), 0.0, -jnp.inf)

    def project(k):
        if once("wq"):
            loads[1].wait()
        a0 = pc.near(k)
        if k > 0:
            wq_line.here(a0)
        left = normed[...].reshape(slab, width)
        out = (jnp.dot(left, wq[a0], preferred_element_type=jnp.float32) * q_scale).astype(jnp.bfloat16)
        for h in range(heads):
            queries[a0, h * slab : (h + 1) * slab, :] = out[:, h * head : (h + 1) * head]

    def fold(scores, values, a0, fresh):
        new_top = jnp.max(scores, axis=-1, keepdims=True)
        if not fresh:
            new_top = jnp.maximum(top_ref[a0], new_top)
        probs = jnp.exp(scores - new_top)
        total = jnp.sum(probs, axis=-1, keepdims=True)
        weighted = jnp.dot(probs.astype(jnp.bfloat16), values, preferred_element_type=jnp.float32)
        if not fresh:
            factor = jnp.exp(top_ref[a0] - new_top)
            total = total + total_ref[a0] * factor
            weighted = weighted + weighted_ref[a0] * factor
        return new_top, total, weighted

    def raw_scores(a0, keys_here):
        return lax.dot_general(queries[a0], keys_here, (((1,), (1,)), ((), ())),
                               preferred_element_type=jnp.float32)

    def over_prefix(k, h):
        e, a0 = pc.near(k), pc.near(h)
        if once("kv", k):
            keys.pair_arrived(e)
        pair = cached[pl.ds(e * B, B), :span, :].reshape(B * span, 2 * head)
        state = fold(raw_scores(a0, pair[:, :head]), pair[:, head:], a0, k == 0)
        top_ref[a0], total_ref[a0], weighted_ref[a0] = state

    def over_suffix(h):
        a0 = pc.near(h)
        fresh = cached[:, span:, :].reshape(row_len, 2 * head)
        scores = raw_scores(a0, fresh[:, :head]).reshape(heads, slab, row_len) + bias[...][None]
        _, total, weighted = fold(scores.reshape(heads * slab, row_len), fresh[:, head:], a0, False)
        out = (weighted / total).astype(jnp.bfloat16)
        for g in range(heads):
            attn[a0, :, g * head : (g + 1) * head] = out[g * slab : (g + 1) * slab]

    out_wide = min(512, part_cols)

    def out_part(j, k):
        if once("wout"):
            loads[2].wait()
        a0 = pc.near(k)
        if k > 0:
            wout_line.here(a0, j)

        def column(c, carry):
            cols = pl.ds(pl.multiple_of(j * part_cols + c * out_wide, out_wide), out_wide)
            out = jnp.dot(attn[a0], wout[a0, :, cols], preferred_element_type=jnp.float32)
            if k > 0:
                out = out + out_sum[:, cols]
            out_sum[:, cols] = out
            return carry

        lax.fori_loop(0, part_cols // out_wide, column, 0)

    def out_copy(o, j):
        cols = pl.ds(j * part_cols, part_cols)
        return remote(out_send.at[o - 1, :, cols], out_in.at[o - 1, :, cols], out_sem.at[o - 1, j],
                      out_recv.at[o - 1, j], pc.side(o))

    def out_give(j):
        cols = pl.ds(j * part_cols, part_cols)
        for o in range(1, B):
            base = pc.across(o) * rows

            def give(part):
                spot = pl.ds(pl.multiple_of(base + part.start, ROWS), ROWS)
                out_send[o - 1, part, cols] = out_sum[spot, cols].astype(jnp.bfloat16)

            row_loop(0, rows, give)
            out_copy(o, j).start()

    def out_take(j):
        cols = pl.ds(j * part_cols, part_cols)
        for o in range(1, B):
            out_copy(o, j).wait_recv()

        def body(part):
            total = out_sum[pl.ds(pl.multiple_of(pc.b * rows + part.start, ROWS), ROWS), cols]
            for o in range(1, B):
                total = total + out_in[o - 1, part, cols].astype(jnp.float32)
            out = total.astype(jnp.bfloat16)
            attended[part, cols] = out
            middle[part, cols] = (hidden[part, cols].astype(jnp.float32) + out.astype(jnp.float32)).astype(jnp.bfloat16)

        row_loop(0, rows, body)

    def norm_middle(s):
        gains = gain2[...].astype(jnp.float32).reshape(1, width)

        def second(part):
            normed2[pc.a, part, :] = norm_rows(middle[part, :].astype(jnp.float32), gains)

        row_loop(s * half, half, second)
        gather.start(s)

    act_wide = min(512, units)

    def expand(k, part=None):
        e = pc.near(k)
        size = rows if part is None else half
        start = 0 if part is None else part * half
        if once("wfc"):
            loads[3].wait()
        for s in range(B):

            def column(c, carry):
                cols = span_of(c, act_wide)
                out = jnp.dot(normed2[e, pl.ds(start, size), :], wfc[s, :, cols], preferred_element_type=jnp.float32)
                spot = pl.ds(pl.multiple_of(s * units + c * act_wide, act_wide), act_wide)
                act[pl.ds(pl.multiple_of(e * rows + start, ROWS), size), spot] = jax.nn.gelu(out, approximate=True).astype(jnp.bfloat16)
                return carry

            lax.fori_loop(0, units // act_wide, column, 0)

    def contract(k, i, part=None):
        e = pc.near(k)
        size = rows if part is None else half
        start = 0 if part is None else part * half
        lines = pl.ds(pl.multiple_of(e * rows + start, ROWS), size)
        if once("wproj"):
            loads[4].wait()
        cols = pl.ds(i * red_cols, red_cols)
        out = jnp.dot(act[lines, :], wproj[:, cols], preferred_element_type=jnp.float32)
        term[e, pl.ds(start, size), cols] = out.astype(jnp.bfloat16)
        if k > 0:

            @pl.when(end)
            def _():
                reduce.pass_on(e, i, part)

    def pass_on(which, i, part=None):
        @pl.when(jnp.logical_not(end))
        def _():
            reduce.pass_on(reduce_blocks[which], i, part)

    def last(part, cols, total):
        layer_out[part, cols] = (middle[part, cols].astype(jnp.float32) + total).astype(jnp.bfloat16)

    def finish_misc():
        for o in range(1, pc.pairs):
            dp_copy(o).wait_send()
        for o in range(pc.pairs):
            dp_to_core(o).wait_send()
        for o in range(1, B):
            tok_copy(o).wait_send()
            for j in range(PARTS):
                out_copy(o, j).wait_send()

    def finish_side():
        fc_side.finish()
        pr_side.finish()

    steps = {
        "fin.wq": wq_line.finish,
        "fin.wo": wout_line.finish,
        "fin.keys": keys.finish,
        "fin.misc": finish_misc,
        "fin.side": finish_side,
        "fin.g": gather.finish,
        "fin.r": reduce.finish,
        "wq.start": wq_line.start,
        "wq.hop": wq_line.hop,
        "wq.spread": wq_line.spread,
        "wo.start": wout_line.start,
        "wo.hop": lambda j, r: wout_line.hop(r, j),
        "wo.spread": lambda j, r: wout_line.spread(r, j),
        "dp.start": dp_start,
        "dp.relay": dp_relay,
        "select": select,
        "keys.start": keys.start,
        "keys.round": keys.round,
        "ln1": norm_tokens,
        "tok.start": tok_start,
        "tok.wait": tok_wait,
        "skv": suffix_keys,
        "proj": project,
        "att": over_prefix,
        "suf": over_suffix,
        "out": out_part,
        "rs.send": out_give,
        "rs.recv": out_take,
        "ln2": norm_middle,
        "side.start": lambda j: side("start", j),
        "side.hop": lambda j: side("hop", j),
        "side.spread": lambda j: side("spread", j),
        "fc.here": fc_side.here,
        "pr.here": pr_side.here,
        "g.hop": gather.hop,
        "expand": expand,
        "contract": contract,
        "po": pass_on,
        "res": lambda i, part: reduce.result(i, part, last),
    }
    greet_wait(pc)
    for name, *numbers in PLAN:
        steps[name](*numbers)


def hand_on(attended, layer_out, attended_to, layer_to):
    attended_to[...] = attended[...]
    layer_to[...] = layer_out[...]


VM = pl.BlockSpec(memory_space=pltpu.VMEM)


def local(n, ndp, hidden_in, norm1_gain, norm2_gain, w_query, w_keyval, w_out, w_fc, w_proj,
          prefix_kv, owner_ids, segment_ids):
    A, B = plane(n)
    rows, width = hidden_in.shape
    head = w_keyval.shape[1] // 2
    query_cols = w_query.shape[1]
    heads = query_cols // head
    span = prefix_kv.shape[1]
    units = w_fc.shape[1]
    q_scale = 1.0 / math.sqrt(head)
    bf, f32 = jnp.bfloat16, jnp.float32
    any_space = pl.BlockSpec(memory_space=pl.ANY)
    own = jax.ShapeDtypeStruct((rows, width), bf)
    V = pltpu.VMEM
    stack = heads * B * rows
    line = V((A, rows, width), bf)
    sides = max(B - 1, 1)
    scratch = [
        V(w_keyval.shape, bf), V((A,) + w_query.shape, bf), V((A,) + w_out.shape, bf),
        V((B,) + w_fc.shape, bf), V((B * units, width), bf),
        V((B, rows, width), bf), line, V((A * rows, B * units), bf), line, line, line,
        V((n, span + rows, 2 * head), bf), V((ndp, span, 2 * head), bf), V((A, stack, head), bf),
        V((A, stack, 1), f32), V((A, stack, 1), f32), V((A, stack, head), f32),
        V((A, B * rows, query_cols), bf), V((B * rows, width), f32),
        V((sides, rows, width), bf), V((sides, rows, width), bf), V((rows, width), bf),
        V((B * rows, n * rows), f32), DMA((5,)),
        DMA((B,)), DMA((sides,)), DMA((sides, PARTS)), DMA((sides, PARTS)),
        DMA((ndp,)), DMA((max(ndp // 2 - 1, 1),)), DMA((ndp // 2,)),
    ]
    scratch += gather_sems(n) + line_weight_sems(n, 1) + line_weight_sems(n, PARTS) + side_weight_sems(n) * 2
    scratch += [DMA((A, HALVES))] * 3 + [DMA((A, PIECES, HALVES))] * 4
    attended, layer_out = pl.pallas_call(
        functools.partial(layer_kernel, n, ndp, heads, q_scale),
        out_shape=(own, own),
        in_specs=[VM] * 4 + [pl.BlockSpec(memory_space=pltpu.SMEM), VM] + [any_space] * 5,
        out_specs=(VM, VM),
        scratch_shapes=scratch,
        compiler_params=pltpu.CompilerParams(collective_id=1, has_side_effects=True, vmem_limit_bytes=62 << 20),
        name="layer",
    )(hidden_in, norm1_gain, norm2_gain, prefix_kv, owner_ids, segment_ids, w_keyval, w_query, w_out,
      w_fc, w_proj)
    attended, layer_out = pl.pallas_call(
        hand_on, out_shape=(own, own), in_specs=[VM] * 2, out_specs=(VM, VM), name="hand_on",
    )(attended, layer_out)
    return (layer_out, attended)


def solution(mesh):
    return jax.shard_map(
        functools.partial(local, mesh.shape["tensor"], mesh.shape["dp"]),
        mesh=mesh,
        in_specs=(
            P(("dp", "tensor"), None),
            P(),
            P(),
            P(None, "tensor"),
            P(),
            P("tensor", None),
            P(None, "tensor"),
            P("tensor", None),
            P("dp", "tensor", None),
            P(),
            P("dp", None),
        ),
        out_specs=(P(("dp", "tensor"), None), P(("dp", "tensor"), None)),
        check_vma=False,
    )
```

```python
import functools
import math

import jax
import jax.numpy as jnp
from jax import lax
from jax.experimental import pallas as pl
from jax.experimental.pallas import tpu as pltpu
from jax.sharding import PartitionSpec as P

MESH = pl.DeviceIdType.MESH
ROWS = 16
PIECES = 4
SIDE = 8
PARTS = 2
HALVES = 2
TEAM = 4


def plane(n):
    lines = 4 if n % 4 == 0 else n
    return lines, n // lines


def norm_rows(widened, gains):
    centre = jnp.mean(widened, axis=-1, keepdims=True)
    centred = widened - centre
    variance = jnp.mean(centred * centred, axis=-1, keepdims=True)
    return (centred * lax.rsqrt(variance + 1e-05) * gains).astype(jnp.bfloat16)


def row_loop(start, rows, body):
    def step(i, carry):
        body(pl.ds(pl.multiple_of(start + i * ROWS, ROWS), ROWS))
        return carry

    lax.fori_loop(0, rows // ROWS, step, 0)


def span_of(i, size):
    return pl.ds(pl.multiple_of(i * size, size), size)


class Place:
    def __init__(self, n, ndp):
        self.n, self.ndp = n, ndp
        self.A, self.B = plane(n)
        self.me = lax.axis_index("tensor")
        self.a = self.me // self.B
        self.b = self.me % self.B
        self.dp = lax.axis_index("dp")
        self.pairs = ndp // 2
        self.q = self.dp % TEAM
        base = self.dp - self.q
        self.q_core = self.q + 1 - 2 * (self.q % 2)
        self.q_far = (self.q + 2) % TEAM
        self.q_diag = (self.q_core + 2) % TEAM
        self.core = {"dp": base + self.q_core}
        self.across_dp = {"dp": base + self.q_far}

    def across(self, o):
        return (self.b + o) % self.B

    def peer(self, a, b):
        return {"tensor": a * self.B + b}

    def side(self, o):
        return self.peer(self.a, self.across(o))

    def up(self):
        return self.peer(jnp.minimum(self.a + 1, self.A - 1), self.b)

    def down(self):
        return self.peer(jnp.maximum(self.a - 1, 0), self.b)

    def same_core(self, o):
        return ((self.dp // 2 + o) % self.pairs) * 2 + self.dp % 2

    def choose(self, k, key):
        found = 0
        for a in range(self.A):
            order = sorted(range(self.A), key=lambda d: key(a, d))
            for i, d in enumerate(order):
                found = found + jnp.where((self.a == a) & (k == i), d, 0)
        return found

    def near(self, k):
        return self.choose(k, lambda a, d: (abs(d - a), d))

    def far(self, k):
        return self.choose(k, lambda a, d: (-abs(d - a), d))


def greet_signal(pc):
    barrier = pltpu.get_barrier_semaphore()

    def signal(device):
        pl.semaphore_signal(barrier, inc=1, device_id=device, device_id_type=MESH)

    @pl.when(pc.a > 0)
    def _():
        signal(pc.peer(pc.a - 1, pc.b))

    @pl.when(pc.a < pc.A - 1)
    def _():
        signal(pc.peer(pc.a + 1, pc.b))

    for o in range(1, pc.B):
        signal(pc.side(o))
    for o in range(1, pc.pairs):
        signal({"dp": pc.same_core(o)})
    signal(pc.core)


def greet_wait(pc):
    ends = jnp.where((pc.a == 0) | (pc.a == pc.A - 1), 1, 2)
    pl.semaphore_wait(pltpu.get_barrier_semaphore(), pc.B - 1 + pc.pairs + ends)


def remote(src, dst, send, recv, device):
    return pltpu.make_async_remote_copy(
        src_ref=src, dst_ref=dst, send_sem=send, recv_sem=recv, device_id=device, device_id_type=MESH
    )


class Gather:
    def __init__(self, place, buf, recv, up, down, side):
        self.pc, self.buf, self.recv, self.up, self.down, self.side = place, buf, recv, up, down, side

    def copy_up(self, a0):
        blk = a0 * self.pc.B + self.pc.b
        return remote(self.buf.at[blk], self.buf.at[blk], self.up.at[a0], self.recv.at[blk], self.pc.up())

    def copy_down(self, a0):
        blk = a0 * self.pc.B + self.pc.b
        return remote(self.buf.at[blk], self.buf.at[blk], self.down.at[a0], self.recv.at[blk], self.pc.down())

    def copy_side(self, a0, o):
        blk = a0 * self.pc.B + self.pc.b
        return remote(self.buf.at[blk], self.buf.at[blk], self.side.at[a0, o - 1], self.recv.at[blk],
                      self.pc.side(o))

    def arrived(self, blk):
        remote(self.buf.at[blk], self.buf.at[blk], self.up.at[0], self.recv.at[blk],
               self.pc.side(1)).wait_recv()

    def start(self):
        pc = self.pc

        @pl.when(pc.a < pc.A - 1)
        def _():
            self.copy_up(pc.a).start()

        @pl.when(pc.a > 0)
        def _():
            self.copy_down(pc.a).start()

        for o in range(1, pc.B):
            self.copy_side(pc.a, o).start()

    def round(self, r):
        pc = self.pc

        @pl.when(pc.a - r >= 0)
        def _():
            a0 = pc.a - r
            self.arrived(a0 * pc.B + pc.b)

            @pl.when(pc.a < pc.A - 1)
            def _():
                self.copy_up(a0).start()

            for o in range(1, pc.B):
                self.copy_side(a0, o).start()

        @pl.when(pc.a + r < pc.A)
        def _():
            a0 = pc.a + r
            self.arrived(a0 * pc.B + pc.b)

            @pl.when(pc.a > 0)
            def _():
                self.copy_down(a0).start()

            for o in range(1, pc.B):
                self.copy_side(a0, o).start()

    def pair_arrived(self, a0):
        for o in range(1, self.pc.B):
            self.arrived(a0 * self.pc.B + self.pc.across(o))

    def finish(self):
        pc = self.pc
        for a0 in range(pc.A):
            for o in range(1, pc.B):
                self.copy_side(a0, o).wait_send()

            @pl.when((pc.a >= a0) & (pc.a < pc.A - 1))
            def _():
                self.copy_up(a0).wait_send()

            @pl.when((pc.a <= a0) & (pc.a > 0))
            def _():
                self.copy_down(a0).wait_send()


DMA = pltpu.SemaphoreType.DMA


def gather_sems(n):
    A, B = plane(n)
    return [DMA((n,)), DMA((A,)), DMA((A,)), DMA((A, max(B - 1, 1)))]


class Team:
    def __init__(self, place, part, recv, far_send, core_send):
        self.pc, self.part, self.recv, self.far_send, self.core_send = place, part, recv, far_send, core_send

    def far_copy(self, s):
        pc = self.pc
        ref = self.part(s, pc.q)
        return remote(ref, ref, self.far_send.at[s], self.recv.at[s, pc.q], pc.across_dp)

    def core_copy(self, s, which):
        pc = self.pc
        q = pc.q_far if which else pc.q
        ref = self.part(s, q)
        return remote(ref, ref, self.core_send.at[s, which], self.recv.at[s, q], pc.core)

    def wait(self, s, q):
        ref = self.part(s, q)
        remote(ref, ref, self.far_send.at[s], self.recv.at[s, q], self.pc.core).wait_recv()

    def landed(self, s):
        self.far_copy(s).start()
        self.core_copy(s, 0).start()

    def spread(self, s):
        self.wait(s, self.pc.q_far)
        self.core_copy(s, 1).start()

    def here(self, s):
        self.wait(s, self.pc.q_core)
        self.wait(s, self.pc.q_diag)

    def finish(self, s):
        self.far_copy(s).wait_send()
        self.core_copy(s, 0).wait_send()
        self.core_copy(s, 1).wait_send()


def team_sems(slots):
    return [DMA((slots, TEAM)), DMA((slots,)), DMA((slots, 2))]


class LineWeights:
    def __init__(self, place, hbm, buf, parts, recv, far_send, core_send, up, down):
        self.pc, self.hbm, self.up, self.down, self.recv, self.parts = place, hbm, up, down, recv, parts
        quarter = buf.shape[1] // TEAM
        cols = buf.shape[2] // parts
        self.part = lambda s, q: buf.at[s // parts, span_of(q, quarter), span_of(s % parts, cols)]
        self.own = lambda j: hbm.at[span_of(place.q, quarter), pl.ds(j * cols, cols)]
        self.team = Team(place, self.part, recv, far_send, core_send)

    def copy_up(self, s, src=None):
        pc = self.pc
        ref = self.part(s, pc.q)
        return remote(ref if src is None else src, ref, self.up.at[s], self.recv.at[s, pc.q], pc.up())

    def copy_down(self, s, src=None):
        pc = self.pc
        ref = self.part(s, pc.q)
        return remote(ref if src is None else src, ref, self.down.at[s], self.recv.at[s, pc.q], pc.down())

    def start(self, j=0):
        pc = self.pc
        s = pc.a * self.parts + j

        @pl.when(pc.a < pc.A - 1)
        def _():
            self.copy_up(s, self.own(j)).start()

        @pl.when(pc.a > 0)
        def _():
            self.copy_down(s, self.own(j)).start()

    def hop(self, r, j=0):
        pc = self.pc

        @pl.when(pc.a - r >= 0)
        def _():
            s = (pc.a - r) * self.parts + j
            self.team.wait(s, pc.q)

            @pl.when(pc.a < pc.A - 1)
            def _():
                self.copy_up(s).start()

            self.team.landed(s)

        @pl.when(pc.a + r < pc.A)
        def _():
            s = (pc.a + r) * self.parts + j
            self.team.wait(s, pc.q)

            @pl.when(pc.a > 0)
            def _():
                self.copy_down(s).start()

            self.team.landed(s)

    def spread(self, r, j=0):
        pc = self.pc

        @pl.when(pc.a - r >= 0)
        def _():
            self.team.spread((pc.a - r) * self.parts + j)

        @pl.when(pc.a + r < pc.A)
        def _():
            self.team.spread((pc.a + r) * self.parts + j)

    def here(self, a0, j=0):
        self.team.here(a0 * self.parts + j)

    def finish(self):
        pc = self.pc
        for s in range(pc.A * self.parts):
            a0 = s // self.parts

            @pl.when((pc.a >= a0) & (pc.a < pc.A - 1))
            def _():
                self.copy_up(s).wait_send()

            @pl.when((pc.a <= a0) & (pc.a > 0))
            def _():
                self.copy_down(s).wait_send()

            @pl.when(pc.a != a0)
            def _():
                self.team.finish(s)


def line_weight_sems(n, parts):
    A, _ = plane(n)
    return team_sems(A * parts) + [DMA((A * parts,)), DMA((A * parts,))]


class SideWeights:
    def __init__(self, place, part, own, recv, far_send, core_send, side_send):
        self.pc, self.part3, self.own, self.recv, self.side_send = place, part, own, recv, side_send
        self.team = Team(place, lambda s, q: part(s // SIDE, s % SIDE, q), recv, far_send, core_send)

    def slots(self, i):
        return [self.pc.across(o) * SIDE + i for o in range(1, self.pc.B)]

    def copy(self, i, o):
        pc = self.pc
        return remote(self.own(i, pc.q), self.part3(pc.b, i, pc.q), self.side_send.at[o - 1, i],
                      self.recv.at[pc.b * SIDE + i, pc.q], pc.side(o))

    def start(self, i):
        for o in range(1, self.pc.B):
            self.copy(i, o).start()

    def hop(self, i):
        for s in self.slots(i):
            self.team.wait(s, self.pc.q)
            self.team.landed(s)

    def spread(self, i):
        for s in self.slots(i):
            self.team.spread(s)

    def here(self, i):
        for s in self.slots(i):
            self.team.here(s)

    def finish(self):
        for i in range(SIDE):
            for o in range(1, self.pc.B):
                self.copy(i, o).wait_send()
            for s in self.slots(i):
                self.team.finish(s)


def side_weight_sems(n):
    _, B = plane(n)
    return team_sems(B * SIDE) + [DMA((max(B - 1, 1), SIDE))]


class LineGather:
    def __init__(self, place, buf, recv, up, down):
        self.pc, self.buf, self.recv, self.up, self.down = place, buf, recv, up, down
        self.half = buf.shape[1] // HALVES

    def ref(self, a0, s):
        return self.buf.at[a0, pl.ds(s * self.half, self.half), :]

    def copy_up(self, a0, s):
        return remote(self.ref(a0, s), self.ref(a0, s), self.up.at[a0, s], self.recv.at[a0, s], self.pc.up())

    def copy_down(self, a0, s):
        return remote(self.ref(a0, s), self.ref(a0, s), self.down.at[a0, s], self.recv.at[a0, s], self.pc.down())

    def start(self, s):
        pc = self.pc

        @pl.when(pc.a < pc.A - 1)
        def _():
            self.copy_up(pc.a, s).start()

        @pl.when(pc.a > 0)
        def _():
            self.copy_down(pc.a, s).start()

    def hop(self, r, only=None):
        pc = self.pc
        for s in range(HALVES) if only is None else (only,):

            @pl.when(pc.a - r >= 0)
            def _():
                self.copy_up(pc.a - r, s).wait_recv()

                @pl.when(pc.a < pc.A - 1)
                def _():
                    self.copy_up(pc.a - r, s).start()

            @pl.when(pc.a + r < pc.A)
            def _():
                self.copy_down(pc.a + r, s).wait_recv()

                @pl.when(pc.a > 0)
                def _():
                    self.copy_down(pc.a + r, s).start()

    def finish(self):
        pc = self.pc
        for a0 in range(pc.A):
            for s in range(HALVES):

                @pl.when((pc.a >= a0) & (pc.a < pc.A - 1))
                def _():
                    self.copy_up(a0, s).wait_send()

                @pl.when((pc.a <= a0) & (pc.a > 0))
                def _():
                    self.copy_down(a0, s).wait_send()


class LineReduce:
    def __init__(self, place, term, up_in, down_in, up_send, up_recv, down_send, down_recv):
        self.pc, self.term, self.up_in, self.down_in = place, term, up_in, down_in
        self.up_send, self.up_recv, self.down_send, self.down_recv = up_send, up_recv, down_send, down_recv
        self.rows = term.shape[1]
        self.wide = term.shape[2] // PIECES

    def spot(self, i, half):
        rows = pl.ds(0, self.rows) if half is None else pl.ds(half * (self.rows // HALVES), self.rows // HALVES)
        return rows, span_of(i, self.wide), 0 if half is None else half

    def copy_up(self, d, i, half=None):
        rows, cols, s = self.spot(i, half)
        return remote(self.term.at[d, rows, cols], self.up_in.at[d, rows, cols], self.up_send.at[d, i, s],
                      self.up_recv.at[d, i, s], self.pc.up())

    def copy_down(self, d, i, half=None):
        rows, cols, s = self.spot(i, half)
        return remote(self.term.at[d, rows, cols], self.down_in.at[d, rows, cols], self.down_send.at[d, i, s],
                      self.down_recv.at[d, i, s], self.pc.down())

    def add(self, d, i, half, arrived):
        area, cols, _ = self.spot(i, half)

        def body(rows):
            total = self.term[d, rows, cols].astype(jnp.float32) + arrived[d, rows, cols].astype(jnp.float32)
            self.term[d, rows, cols] = total.astype(jnp.bfloat16)

        row_loop(area.start, area.size, body)

    def pass_on(self, d, i, half=None):
        pc = self.pc

        @pl.when(d > pc.a)
        def _():
            @pl.when(pc.a > 0)
            def _():
                self.copy_up(d, i, half).wait_recv()
                self.add(d, i, half, self.up_in)

            self.copy_up(d, i, half).start()

        @pl.when(d < pc.a)
        def _():
            @pl.when(pc.a < pc.A - 1)
            def _():
                self.copy_down(d, i, half).wait_recv()
                self.add(d, i, half, self.down_in)

            self.copy_down(d, i, half).start()

    def result(self, i, half, use):
        pc = self.pc

        def go(terms, part):
            area, cols, _ = self.spot(i, part)

            def body(rows):
                total = self.term[pc.a, rows, cols].astype(jnp.float32)
                for arrived in terms:
                    total = total + arrived[pc.a, rows, cols].astype(jnp.float32)
                use(rows, cols, total)

            row_loop(area.start, area.size, body)

        @pl.when(pc.a == 0)
        def _():
            self.copy_down(pc.a, i, half).wait_recv()
            go([self.down_in], half)

        @pl.when(pc.a == pc.A - 1)
        def _():
            self.copy_up(pc.a, i, half).wait_recv()
            go([self.up_in], half)

        if half == 0:

            @pl.when((pc.a > 0) & (pc.a < pc.A - 1))
            def _():
                self.copy_up(pc.a, i).wait_recv()
                self.copy_down(pc.a, i).wait_recv()
                go([self.up_in, self.down_in], None)

    def finish(self):
        pc = self.pc
        for d in range(pc.A):
            for i in range(PIECES):
                for half in range(HALVES) if d in (0, pc.A - 1) else (None,):

                    @pl.when(pc.a < d)
                    def _():
                        self.copy_up(d, i, half).wait_send()

                    @pl.when(pc.a > d)
                    def _():
                        self.copy_down(d, i, half).wait_send()


PLAN = (
    ("dp.start",), ("side.start", 0), ("wq.start",), ("wo.start", 0), ("side.start", 1), ("ln1",),
    ("tok.start",), ("side.start", 2), ("side.hop", 0), ("wq.hop", 1), ("side.start", 3), ("side.start", 4),
    ("dp.relay",), ("select",), ("skv",), ("keys.start",), ("wq.hop", 2), ("side.hop", 1), ("keys.round", 1),
    ("side.hop", 2), ("side.hop", 3), ("wq.hop", 3), ("tok.wait",), ("proj", 0), ("wq.spread", 1), ("proj", 1),
    ("side.spread", 1), ("wq.spread", 2), ("proj", 2), ("att", 0, 0), ("att", 0, 2), ("keys.round", 2),
    ("wo.start", 1), ("wo.hop", 0, 1), ("att", 0, 1), ("side.hop", 4), ("wq.spread", 3), ("proj", 3),
    ("att", 0, 3), ("att", 1, 1), ("att", 1, 2), ("keys.round", 3), ("side.start", 5), ("side.start", 6),
    ("att", 1, 0), ("att", 1, 3), ("wo.hop", 1, 1), ("att", 2, 0), ("side.spread", 0), ("side.spread", 4),
    ("wo.spread", 0, 1), ("side.start", 7), ("side.start", 8), ("wo.hop", 0, 2), ("fc.here", 1), ("att", 2, 1),
    ("att", 2, 3), ("att", 2, 2), ("wo.spread", 1, 1), ("wo.hop", 1, 2), ("att", 3, 3), ("att", 3, 2),
    ("wo.hop", 0, 3), ("suf", 3), ("att", 3, 1), ("att", 3, 0), ("wo.spread", 0, 2), ("wo.hop", 1, 3),
    ("suf", 0), ("out", 0, 0), ("suf", 1), ("wo.spread", 0, 3), ("suf", 2), ("out", 0, 1), ("out", 0, 2),
    ("fc.here", 4), ("out", 0, 3), ("rs.send", 0), ("wo.spread", 1, 3), ("wo.spread", 1, 2), ("out", 1, 0),
    ("out", 1, 1), ("side.spread", 2), ("fin.wq",), ("out", 1, 2), ("fin.keys",), ("side.hop", 5),
    ("fc.here", 0), ("side.hop", 6), ("out", 1, 3), ("side.spread", 3), ("side.hop", 7), ("rs.send", 1),
    ("side.start", 9), ("rs.recv", 0), ("side.hop", 8), ("side.start", 10), ("side.spread", 6),
    ("side.start", 11), ("rs.recv", 1), ("ln2", 0), ("ln2", 1), ("side.hop", 9), ("fin.wo",),
    ("side.spread", 7), ("side.start", 12), ("side.start", 13), ("fc.here", 2), ("side.spread", 5),
    ("fc.here", 5), ("side.hop", 10), ("side.spread", 8), ("fc.here", 6), ("fc.here", 3), ("fc.here", 7),
    ("expand", 0), ("side.hop", 11), ("fin.misc",), ("g.hop", 1), ("side.spread", 9), ("side.start", 14),
    ("pr.here", 0), ("expand", 1), ("side.hop", 12), ("side.start", 15), ("side.spread", 10),
    ("side.spread", 11), ("side.hop", 13), ("side.hop", 14), ("pr.here", 3), ("pr.here", 2), ("pr.here", 1),
    ("contract", 1, 0), ("contract", 1, 1), ("g.hop", 2), ("expand", 2), ("contract", 2, 0), ("side.hop", 15),
    ("contract", 2, 1), ("g.hop", 3, 0), ("side.spread", 13), ("side.spread", 12), ("expand", 3, 0),
    ("contract", 3, 1, 0), ("pr.here", 4), ("po", "m", 0), ("contract", 3, 0, 0), ("pr.here", 5),
    ("contract", 3, 2, 0), ("contract", 0, 0), ("side.spread", 15), ("po", "m", 1), ("g.hop", 3, 1),
    ("expand", 3, 1), ("po", "f", 1, 0), ("po", "f", 0, 0), ("contract", 3, 0, 1), ("po", "f", 0, 1),
    ("side.spread", 14), ("fin.g",), ("contract", 3, 1, 1), ("po", "f", 1, 1), ("pr.here", 6), ("pr.here", 7),
    ("po", "f", 2, 0), ("contract", 3, 3, 1), ("po", "n", 1, 0), ("contract", 3, 3, 0), ("po", "f", 3, 1),
    ("po", "n", 0, 0), ("contract", 3, 2, 1), ("contract", 2, 3), ("po", "n", 0, 1), ("po", "f", 3, 0),
    ("contract", 2, 2), ("po", "f", 2, 1), ("contract", 1, 3), ("po", "n", 1, 1), ("contract", 1, 2),
    ("po", "n", 2, 0), ("contract", 0, 3), ("po", "m", 3), ("po", "n", 3, 1), ("contract", 0, 1), ("res", 1, 0),
    ("contract", 0, 2), ("po", "n", 3, 0), ("po", "m", 2), ("res", 1, 1), ("res", 0, 0), ("po", "n", 2, 1),
    ("fin.side",), ("res", 0, 1), ("fin.r",), ("res", 3, 0), ("res", 3, 1), ("res", 2, 0), ("res", 2, 1),
)


def layer_kernel(n, ndp, heads, q_scale, hidden, gain1, gain2, prefix, owners, seg, w_keyval_hbm, w_query_hbm,
                 w_out_hbm, w_fc_hbm, w_proj_hbm, attended, layer_out, *scratch):
    pc = Place(n, ndp)
    A, B = pc.A, pc.B
    greet_signal(pc)
    scratch = list(scratch)

    def take(count):
        got = scratch[:count]
        del scratch[:count]
        return got

    wkv, wq, wout, wfc, wproj = take(5)
    normed, normed2, act, term, up_in, down_in = take(6)
    cached, from_dp, queries, top_ref, total_ref, weighted_ref, attn, out_sum, out_send, out_in, middle, bias = take(12)
    (load,) = take(1)
    tok_recv, tok_send, out_sem, out_recv = take(4)
    dp_recv, dp_send, dp_core = take(3)
    rows, width = hidden.shape
    slab = B * rows
    span = prefix.shape[1]
    row_len = n * rows
    head = wkv.shape[1] // 2
    units = w_fc_hbm.shape[1]
    half = rows // HALVES
    dp = pc.dp

    keys = Gather(pc, cached, *take(4))
    wq_line = LineWeights(pc, w_query_hbm, wq, 1, *take(5))
    wout_line = LineWeights(pc, w_out_hbm, wout, PARTS, *take(5))
    fc_rows, fc_part = width // TEAM, width // TEAM // SIDE
    pr_rows, pr_cols = units // TEAM, width // SIDE
    red_cols = width // PIECES
    part_cols = width // PARTS
    fc_side = SideWeights(
        pc,
        lambda s, i, q: wfc.at[s, pl.ds(pl.multiple_of(q * fc_rows + i * fc_part, fc_part), fc_part), :],
        lambda i, q: w_fc_hbm.at[pl.ds(pl.multiple_of(q * fc_rows + i * fc_part, fc_part), fc_part), :],
        *take(4))
    pr_side = SideWeights(
        pc,
        lambda s, i, q: wproj.at[pl.ds(pl.multiple_of(s * units + q * pr_rows, pr_rows), pr_rows), span_of(i, pr_cols)],
        lambda i, q: w_proj_hbm.at[span_of(q, pr_rows), span_of(i, pr_cols)],
        *take(4))
    gather = LineGather(pc, normed2, *take(3))
    reduce = LineReduce(pc, term, up_in, down_in, *take(4))

    def side(kind, j):
        getattr(fc_side if j < SIDE else pr_side, kind)(j % SIDE)

    loads = [
        pltpu.make_async_copy(w_keyval_hbm, wkv, load.at[0]),
        pltpu.make_async_copy(w_query_hbm, wq.at[pc.a], load.at[1]),
        pltpu.make_async_copy(w_out_hbm, wout.at[pc.a], load.at[2]),
        pltpu.make_async_copy(w_fc_hbm, wfc.at[pc.b], load.at[3]),
        pltpu.make_async_copy(w_proj_hbm, wproj.at[span_of(pc.b, units), :], load.at[4]),
    ]
    for copy in loads[:2]:
        copy.start()
    end = (pc.a == 0) | (pc.a == A - 1)
    low = pc.a < A // 2
    far_block = jnp.where(low, A - 1, 0)
    reduce_blocks = {"m": jnp.where(low, pc.a + 1, pc.a - 1), "f": far_block, "n": A - 1 - far_block}
    seen = set()

    def once(*key):
        if key in seen:
            return False
        seen.add(key)
        return True

    def dp_copy(o):
        return remote(prefix.at[0], from_dp.at[dp], dp_send.at[o - 1], dp_recv.at[dp], {"dp": pc.same_core(o)})

    def dp_to_core(o):
        src = pc.same_core(o)
        ref = prefix.at[0] if o == 0 else from_dp.at[src]
        return remote(ref, from_dp.at[src], dp_core.at[o], dp_recv.at[src], pc.core)

    def dp_arrived(src):
        remote(prefix.at[0], from_dp.at[src], dp_send.at[0], dp_recv.at[src], pc.core).wait_recv()

    def dp_start():
        for o in range(1, pc.pairs):
            dp_copy(o).start()
        dp_to_core(0).start()
        from_dp[dp] = prefix[0]

    def dp_relay():
        for o in range(1, pc.pairs):
            dp_arrived(pc.same_core(o))
            dp_to_core(o).start()

    def select():
        for o in range(pc.pairs):
            src = pc.same_core(o)
            dp_arrived(src + 1 - 2 * (src % 2))
        cached[pc.me, :span, :] = from_dp[owners[dp]]

    def norm_tokens():
        gains = gain1[...].astype(jnp.float32).reshape(1, width)

        def first(part):
            normed[pc.b, part, :] = norm_rows(hidden[part, :].astype(jnp.float32), gains)

        row_loop(0, rows, first)

    def tok_copy(o):
        return remote(normed.at[pc.b], normed.at[pc.b], tok_send.at[o - 1], tok_recv.at[pc.b], pc.side(o))

    def tok_start():
        for copy in loads[2:]:
            copy.start()
        for o in range(1, B):
            tok_copy(o).start()

    def tok_wait():
        for o in range(1, B):
            s = pc.across(o)
            remote(normed.at[s], normed.at[s], tok_send.at[0], tok_recv.at[s], pc.side(1)).wait_recv()

    def suffix_keys():
        loads[0].wait()
        cached[pc.me, span:, :] = jnp.dot(
            normed[pc.b], wkv[...], preferred_element_type=jnp.float32
        ).astype(jnp.bfloat16)
        spot = pc.a * slab + lax.broadcasted_iota(jnp.int32, (slab, row_len), 0)
        other = lax.broadcasted_iota(jnp.int32, (slab, row_len), 1)
        ids = seg[...].astype(jnp.float32)
        mine = jnp.sum(jnp.where(other == spot, ids, 0.0), axis=1, keepdims=True)
        bias[...] = jnp.where((other <= spot) & (mine == ids), 0.0, -jnp.inf)

    def project(k):
        if once("wq"):
            loads[1].wait()
        a0 = pc.near(k)
        if k > 0:
            wq_line.here(a0)
        left = normed[...].reshape(slab, width)
        out = (jnp.dot(left, wq[a0], preferred_element_type=jnp.float32) * q_scale).astype(jnp.bfloat16)
        for h in range(heads):
            queries[a0, h * slab : (h + 1) * slab, :] = out[:, h * head : (h + 1) * head]

    def fold(scores, values, a0, fresh):
        new_top = jnp.max(scores, axis=-1, keepdims=True)
        if not fresh:
            new_top = jnp.maximum(top_ref[a0], new_top)
        probs = jnp.exp(scores - new_top)
        total = jnp.sum(probs, axis=-1, keepdims=True)
        weighted = jnp.dot(probs.astype(jnp.bfloat16), values, preferred_element_type=jnp.float32)
        if not fresh:
            factor = jnp.exp(top_ref[a0] - new_top)
            total = total + total_ref[a0] * factor
            weighted = weighted + weighted_ref[a0] * factor
        return new_top, total, weighted

    def raw_scores(a0, keys_here):
        return lax.dot_general(queries[a0], keys_here, (((1,), (1,)), ((), ())),
                               preferred_element_type=jnp.float32)

    def over_prefix(k, h):
        e, a0 = pc.near(k), pc.near(h)
        if once("kv", k):
            keys.pair_arrived(e)
        pair = cached[pl.ds(e * B, B), :span, :].reshape(B * span, 2 * head)
        state = fold(raw_scores(a0, pair[:, :head]), pair[:, head:], a0, k == 0)
        top_ref[a0], total_ref[a0], weighted_ref[a0] = state

    def over_suffix(h):
        a0 = pc.near(h)
        fresh = cached[:, span:, :].reshape(row_len, 2 * head)
        scores = raw_scores(a0, fresh[:, :head]).reshape(heads, slab, row_len) + bias[...][None]
        _, total, weighted = fold(scores.reshape(heads * slab, row_len), fresh[:, head:], a0, False)
        out = (weighted / total).astype(jnp.bfloat16)
        for g in range(heads):
            attn[a0, :, g * head : (g + 1) * head] = out[g * slab : (g + 1) * slab]

    out_wide = min(512, part_cols)

    def out_part(j, k):
        if once("wout"):
            loads[2].wait()
        a0 = pc.near(k)
        if k > 0:
            wout_line.here(a0, j)

        def column(c, carry):
            cols = pl.ds(pl.multiple_of(j * part_cols + c * out_wide, out_wide), out_wide)
            out = jnp.dot(attn[a0], wout[a0, :, cols], preferred_element_type=jnp.float32)
            if k > 0:
                out = out + out_sum[:, cols]
            out_sum[:, cols] = out
            return carry

        lax.fori_loop(0, part_cols // out_wide, column, 0)

    def out_copy(o, j):
        cols = pl.ds(j * part_cols, part_cols)
        return remote(out_send.at[o - 1, :, cols], out_in.at[o - 1, :, cols], out_sem.at[o - 1, j],
                      out_recv.at[o - 1, j], pc.side(o))

    def out_give(j):
        cols = pl.ds(j * part_cols, part_cols)
        for o in range(1, B):
            base = pc.across(o) * rows

            def give(part):
                spot = pl.ds(pl.multiple_of(base + part.start, ROWS), ROWS)
                out_send[o - 1, part, cols] = out_sum[spot, cols].astype(jnp.bfloat16)

            row_loop(0, rows, give)
            out_copy(o, j).start()

    def out_take(j):
        cols = pl.ds(j * part_cols, part_cols)
        for o in range(1, B):
            out_copy(o, j).wait_recv()

        def body(part):
            total = out_sum[pl.ds(pl.multiple_of(pc.b * rows + part.start, ROWS), ROWS), cols]
            for o in range(1, B):
                total = total + out_in[o - 1, part, cols].astype(jnp.float32)
            out = total.astype(jnp.bfloat16)
            attended[part, cols] = out
            middle[part, cols] = (hidden[part, cols].astype(jnp.float32) + out.astype(jnp.float32)).astype(jnp.bfloat16)

        row_loop(0, rows, body)

    def norm_middle(s):
        gains = gain2[...].astype(jnp.float32).reshape(1, width)

        def second(part):
            normed2[pc.a, part, :] = norm_rows(middle[part, :].astype(jnp.float32), gains)

        row_loop(s * half, half, second)
        gather.start(s)

    act_wide = min(1024, units)

    def expand(k, part=None):
        e = pc.near(k)
        size = rows if part is None else half
        start = 0 if part is None else part * half
        if once("wfc"):
            loads[3].wait()
        for s in range(B):

            def column(c, carry):
                cols = span_of(c, act_wide)
                out = jnp.dot(normed2[e, pl.ds(start, size), :], wfc[s, :, cols], preferred_element_type=jnp.float32)
                spot = pl.ds(pl.multiple_of(s * units + c * act_wide, act_wide), act_wide)
                act[pl.ds(pl.multiple_of(e * rows + start, ROWS), size), spot] = jax.nn.gelu(out, approximate=True).astype(jnp.bfloat16)
                return carry

            lax.fori_loop(0, units // act_wide, column, 0)

    def contract(k, i, part=None):
        e = pc.near(k)
        size = rows if part is None else half
        start = 0 if part is None else part * half
        lines = pl.ds(pl.multiple_of(e * rows + start, ROWS), size)
        if once("wproj"):
            loads[4].wait()
        cols = pl.ds(i * red_cols, red_cols)
        out = jnp.dot(act[lines, :], wproj[:, cols], preferred_element_type=jnp.float32)
        term[e, pl.ds(start, size), cols] = out.astype(jnp.bfloat16)
        if k > 0:

            @pl.when(end)
            def _():
                reduce.pass_on(e, i, part)

    def pass_on(which, i, part=None):
        @pl.when(jnp.logical_not(end))
        def _():
            reduce.pass_on(reduce_blocks[which], i, part)

    def last(part, cols, total):
        layer_out[part, cols] = (middle[part, cols].astype(jnp.float32) + total).astype(jnp.bfloat16)

    def finish_misc():
        for o in range(1, pc.pairs):
            dp_copy(o).wait_send()
        for o in range(pc.pairs):
            dp_to_core(o).wait_send()
        for o in range(1, B):
            tok_copy(o).wait_send()
            for j in range(PARTS):
                out_copy(o, j).wait_send()

    def finish_side():
        fc_side.finish()
        pr_side.finish()

    steps = {
        "fin.wq": wq_line.finish,
        "fin.wo": wout_line.finish,
        "fin.keys": keys.finish,
        "fin.misc": finish_misc,
        "fin.side": finish_side,
        "fin.g": gather.finish,
        "fin.r": reduce.finish,
        "wq.start": wq_line.start,
        "wq.hop": wq_line.hop,
        "wq.spread": wq_line.spread,
        "wo.start": wout_line.start,
        "wo.hop": lambda j, r: wout_line.hop(r, j),
        "wo.spread": lambda j, r: wout_line.spread(r, j),
        "dp.start": dp_start,
        "dp.relay": dp_relay,
        "select": select,
        "keys.start": keys.start,
        "keys.round": keys.round,
        "ln1": norm_tokens,
        "tok.start": tok_start,
        "tok.wait": tok_wait,
        "skv": suffix_keys,
        "proj": project,
        "att": over_prefix,
        "suf": over_suffix,
        "out": out_part,
        "rs.send": out_give,
        "rs.recv": out_take,
        "ln2": norm_middle,
        "side.start": lambda j: side("start", j),
        "side.hop": lambda j: side("hop", j),
        "side.spread": lambda j: side("spread", j),
        "fc.here": fc_side.here,
        "pr.here": pr_side.here,
        "g.hop": gather.hop,
        "expand": expand,
        "contract": contract,
        "po": pass_on,
        "res": lambda i, part: reduce.result(i, part, last),
    }
    greet_wait(pc)
    for name, *numbers in PLAN:
        steps[name](*numbers)


def hand_on(attended, layer_out, attended_to, layer_to):
    attended_to[...] = attended[...]
    layer_to[...] = layer_out[...]


VM = pl.BlockSpec(memory_space=pltpu.VMEM)


def local(n, ndp, hidden_in, norm1_gain, norm2_gain, w_query, w_keyval, w_out, w_fc, w_proj,
          prefix_kv, owner_ids, segment_ids):
    A, B = plane(n)
    rows, width = hidden_in.shape
    head = w_keyval.shape[1] // 2
    query_cols = w_query.shape[1]
    heads = query_cols // head
    span = prefix_kv.shape[1]
    units = w_fc.shape[1]
    q_scale = 1.0 / math.sqrt(head)
    bf, f32 = jnp.bfloat16, jnp.float32
    any_space = pl.BlockSpec(memory_space=pl.ANY)
    own = jax.ShapeDtypeStruct((rows, width), bf)
    V = pltpu.VMEM
    stack = heads * B * rows
    line = V((A, rows, width), bf)
    sides = max(B - 1, 1)
    scratch = [
        V(w_keyval.shape, bf), V((A,) + w_query.shape, bf), V((A,) + w_out.shape, bf),
        V((B,) + w_fc.shape, bf), V((B * units, width), bf),
        V((B, rows, width), bf), line, V((A * rows, B * units), bf), line, line, line,
        V((n, span + rows, 2 * head), bf), V((ndp, span, 2 * head), bf), V((A, stack, head), bf),
        V((A, stack, 1), f32), V((A, stack, 1), f32), V((A, stack, head), f32),
        V((A, B * rows, query_cols), bf), V((B * rows, width), f32),
        V((sides, rows, width), bf), V((sides, rows, width), bf), V((rows, width), bf),
        V((B * rows, n * rows), f32), DMA((5,)),
        DMA((B,)), DMA((sides,)), DMA((sides, PARTS)), DMA((sides, PARTS)),
        DMA((ndp,)), DMA((max(ndp // 2 - 1, 1),)), DMA((ndp // 2,)),
    ]
    scratch += gather_sems(n) + line_weight_sems(n, 1) + line_weight_sems(n, PARTS) + side_weight_sems(n) * 2
    scratch += [DMA((A, HALVES))] * 3 + [DMA((A, PIECES, HALVES))] * 4
    attended, layer_out = pl.pallas_call(
        functools.partial(layer_kernel, n, ndp, heads, q_scale),
        out_shape=(own, own),
        in_specs=[VM] * 4 + [pl.BlockSpec(memory_space=pltpu.SMEM), VM] + [any_space] * 5,
        out_specs=(VM, VM),
        scratch_shapes=scratch,
        compiler_params=pltpu.CompilerParams(collective_id=1, has_side_effects=True, vmem_limit_bytes=62 << 20),
        name="layer",
    )(hidden_in, norm1_gain, norm2_gain, prefix_kv, owner_ids, segment_ids, w_keyval, w_query, w_out,
      w_fc, w_proj)
    attended, layer_out = pl.pallas_call(
        hand_on, out_shape=(own, own), in_specs=[VM] * 2, out_specs=(VM, VM), name="hand_on",
    )(attended, layer_out)
    return (layer_out, attended)


def solution(mesh):
    return jax.shard_map(
        functools.partial(local, mesh.shape["tensor"], mesh.shape["dp"]),
        mesh=mesh,
        in_specs=(
            P(("dp", "tensor"), None),
            P(),
            P(),
            P(None, "tensor"),
            P(),
            P("tensor", None),
            P(None, "tensor"),
            P("tensor", None),
            P("dp", "tensor", None),
            P(),
            P("dp", None),
        ),
        out_specs=(P(("dp", "tensor"), None), P(("dp", "tensor"), None)),
        check_vma=False,
    )
```
